128 devices in a mesh: rep: 4 (over z_lo, core), shard: 32 (over z_hi, y, x).
Axes of the slice: x: 4, y: 4, z: 4 (z_hi: 2, z_lo: 2; z = z_hi * 2 + z_lo), core: 2. Of those that a mesh axis runs over, the one named last changes fastest.
Arguments:
- inputs: float32 [32, 512, 1024], P('shard', 'rep'), may hold values from -6 to 6
- segment_ids: int32 [32, 512], P('shard', 'rep'), may hold values from 0 to 3, never falling along the last dimension, each value on 1 to 200 neighbouring positions
- cotangent: float32 [32, 512, 1024], P('shard', 'rep'), may hold values from -6 to 6
- w_qkv: bfloat16 [1, 1024, 3072], P(None, 'shard'), may hold values from -0.1875 to 0.1875
- w_out: bfloat16 [1, 1024, 1024], P(None, 'shard'), may hold values from -0.75 to 0.75
- w_up: bfloat16 [1, 1024, 4096], P(None, 'shard'), may hold values from -0.1875 to 0.1875
- w_down: bfloat16 [1, 4096, 1024], P(None, 'shard'), may hold values from -0.09375 to 0.09375
- biases: bfloat16 [1, 6, 1024], P(None, None, 'shard'), may hold values from -3 to 3
- norm_gains: bfloat16 [1, 2, 1024], P(None, None, 'shard'), may hold values from 0.5 to 1.5
- up_bias: bfloat16 [1, 4096], P(None, 'shard'), may hold values from -3 to 3
Outputs:
- outputs: float32 [32, 512, 1024], P('shard', 'rep')
- input_grad: float32 [32, 512, 1024], P('shard', 'rep')
- grad_w_qkv: float32 [1, 1024, 3072], P(None, 'shard')
- grad_w_out: float32 [1, 1024, 1024], P(None, 'shard')
- grad_w_up: float32 [1, 1024, 4096], P(None, 'shard')
- grad_w_down: float32 [1, 4096, 1024], P(None, 'shard')
- grad_biases: float32 [1, 6, 1024], P(None, None, 'shard')
- grad_norm_gains: float32 [1, 2, 1024], P(None, None, 'shard')
- grad_up_bias: float32 [1, 4096], P(None, 'shard')
The draws below stay inside these ranges and needn't reach their ends.
Inputs may be any that keep to these rules, and one draw needn't show every extreme that they name: `segment_ids`: within each sequence the id never falls along the positions; ids of different sequences are unrelated.
All inputs are finite; a program needn't handle non-finite values.
Results may differ from the reference program's by a relative error of at most 0.025.
Values may be sent and summed in bfloat16 or wider, within the bound.
A program may use at most 128 MiB of HBM per device.

```python
import math
import jax
import jax.numpy as jnp
import numpy as np
from jax import lax

D = 1024
HEADS = 16
HEAD_DIM = 64
FF = 4096
SEQ = 512
LAYERS = 1
SEQS = 32


def spiked(drawn, own_key, source, target, blocks, factor):
    owner, partner = [(jnp.arange(drawn.shape[dim]) // (drawn.shape[dim] // blocks)).reshape([-1 if axis == dim else 1 for axis in range(drawn.ndim)]) for dim in (source, target)]
    chosen = jax.random.permutation(own_key, blocks)[partner]
    strong = (owner == chosen) | (owner == (partner + blocks // 2) % blocks)
    return jnp.where(strong, factor * drawn, drawn)


def steps_of(own_key, extent, split, smallest, top_value):
    def one(axis_at, shards_of):
        heights = jax.random.uniform(jax.random.fold_in(jax.random.fold_in(own_key, 6), axis_at), (shards_of,), jnp.float32, smallest / len(split), top_value / len(split))
        return jnp.repeat(jnp.exp(heights), extent[axis_at] // shards_of).reshape((-1,) + (1,) * (len(extent) - axis_at - 1))

    level = one(*split[0])
    for cut in split[1:]:
        level = level * one(*cut)
    return level


def length_profile(number_of, total, limit, skew):
    loads = [(1 << 20) // math.isqrt(standing ** skew) + 1 for standing in range(2, number_of + 1)]
    surplus, counts = total - limit - (number_of - 1), [1] * (number_of - 1)
    while surplus > 0:
        free = [i for i in range(number_of - 1) if counts[i] < limit]
        whole, budget = sum([loads[i] for i in free]), surplus
        for i in free:
            extra = min(limit - counts[i], max(1, budget * loads[i] // whole), surplus)
            counts[i] = counts[i] + extra
            surplus = surplus - extra
    return np.array([limit] + counts)


def uneven(key, amount, total, limit, skew):
    if amount == 2:
        one = jax.random.randint(key, (), max(1, total - limit), min(limit, total - 1) + 1)
        return jnp.stack([one, total - one])
    sizes = jnp.asarray(length_profile(amount, total, limit, skew), jnp.int32)
    pairs = (amount - 1) // 2
    giver, sink = sizes[1:1 + 2 * pairs:2], sizes[2:2 + 2 * pairs:2]
    margin = jnp.minimum(giver - 1, limit - sink)
    passed = jax.random.randint(jax.random.fold_in(key, 1), (pairs,), 0, 1 << 20) % (margin + 1)
    sizes = sizes.at[1:1 + 2 * pairs:2].set(giver - passed).at[2:2 + 2 * pairs:2].set(sink + passed)
    return sizes[jax.random.permutation(jax.random.fold_in(key, 2), amount)]


def gaussian(rng, extent, scale, reach, cuts=(), dtype=jnp.bfloat16):
    array = scale * jax.random.normal(rng, extent, jnp.float32)
    if cuts:
        array = array * steps_of(rng, extent, cuts, -0.22, 0.18)
    return jnp.clip(array, -reach, reach).astype(dtype)


def heavy_noise(key, shape, width, reach, shards, heavy, kind=jnp.bfloat16):
    array = width * jax.random.normal(key, shape, jnp.float32)
    if shards:
        array = array * steps_of(key, shape, shards, -0.22, 0.18)
    return jnp.clip(spiked(array, jax.random.fold_in(key, 3), *heavy), -reach, reach).astype(kind)


def setup_inputs(seed: int = 0) -> dict:
    key_of = jax.random.split(jax.random.key(seed), 11)
    return {
        "inputs": heavy_noise(key_of[0], (SEQS, SEQ, D), 1.0, 6.0, ((0, 32), (1, 4)), (0, 2, 32, 2.75), jnp.float32),
        "segment_ids": jax.vmap(lambda own: jnp.searchsorted(jnp.cumsum(uneven(own, 4, SEQ, SEQ * 25 // 64, 1)), jnp.arange(SEQ), side="right"))(jax.random.split(key_of[1], SEQS)).reshape((SEQS, SEQ)).astype(jnp.int32),
        "cotangent": heavy_noise(key_of[2], (SEQS, SEQ, D), 1.0, 6.0, ((0, 32), (1, 4)), (0, 2, 32, 2.75), jnp.float32),
        "w_qkv": gaussian(key_of[3], (LAYERS, D, 3 * D), D ** -0.5, 0.1875, ((1, 32),)),
        "w_out": gaussian(key_of[4], (LAYERS, D, D), (D // 16) ** -0.5, 0.75, ((1, 32),)),
        "w_up": gaussian(key_of[5], (LAYERS, D, FF), D ** -0.5, 0.1875, ((1, 32),)),
        "w_down": gaussian(key_of[6], (LAYERS, FF, D), FF ** -0.5, 0.09375, ((1, 32),)),
        "biases": gaussian(key_of[7], (LAYERS, 6, D), 0.5, 3.0, ((2, 32),)),
        "norm_gains": jnp.clip(1.0 + 0.1 * jax.random.normal(key_of[8], (LAYERS, 2, D), jnp.float32), 0.5, 1.5).astype(jnp.bfloat16),
        "up_bias": gaussian(key_of[9], (LAYERS, FF), 0.5, 3.0, ((1, 32),)),
    }


epsilon = 1e-06

def round_trip(tensor):
    return lax.optimization_barrier(tensor.astype(jnp.bfloat16)).astype(jnp.float32)

def normalize(residual):
    center = residual - lax.optimization_barrier(jnp.mean(residual, axis=-1, keepdims=True))
    rstd_val = lax.rsqrt(lax.optimization_barrier(jnp.mean(center * center, axis=-1, keepdims=True)) + epsilon)
    return (center * rstd_val, rstd_val)

def norm_back(grad_out, x_hat, rstd_val, gain_row):
    d_hat = grad_out * gain_row
    return rstd_val * (d_hat - lax.optimization_barrier(jnp.mean(d_hat, axis=-1, keepdims=True)) - x_hat * lax.optimization_barrier(jnp.mean(d_hat * x_hat, axis=-1, keepdims=True)))

def gelu_pair(pre_act):
    normal_cdf = 0.5 * (1.0 + lax.erf(pre_act * (1.0 / math.sqrt(2.0))))
    density = jnp.exp(-0.5 * pre_act * pre_act) * (1.0 / math.sqrt(2.0 * math.pi))
    return (pre_act * normal_cdf, normal_cdf + pre_act * density)

def matmul(first_op, second_op):
    return jnp.dot(first_op, second_op, preferred_element_type=jnp.float32)

def matmul_lt(first_op, second_op):
    return jnp.dot(first_op.T, second_op, preferred_element_type=jnp.float32)

def matmul_rt(first_op, second_op):
    return jnp.dot(first_op, second_op.T, preferred_element_type=jnp.float32)

def attention_scores(queries, keys_all, seg_rows, seg_cols):
    scores = jnp.einsum('sqhe,skhe->shqk', queries.astype(jnp.float32), keys_all.astype(jnp.float32)) * (1.0 / math.sqrt(HEAD_DIM))
    allowed = seg_rows[:, None, :, None] == seg_cols[:, None, None, :]
    return (scores, allowed)

def forward_layer(hidden, seg_rows, weights):
    w_qkv, w_out, w_up, w_down, biases, norm_gains, up_bias = weights
    seq_count = hidden.shape[0]
    rows_f32 = hidden.reshape(-1, D)
    rows_bf = rows_f32.astype(jnp.bfloat16)
    qkv_rows = matmul(rows_bf, w_qkv)
    queries = (qkv_rows[:, :D] + biases[0]).astype(jnp.bfloat16).reshape(seq_count, -1, HEADS, HEAD_DIM)
    keys_all = qkv_rows[:, D:2 * D].astype(jnp.bfloat16).reshape(seq_count, -1, HEADS, HEAD_DIM)
    values_all = (qkv_rows[:, 2 * D:] + biases[1]).astype(jnp.bfloat16).reshape(seq_count, -1, HEADS, HEAD_DIM)
    scores, allowed = attention_scores(queries, keys_all, seg_rows, seg_rows)
    expo_all = jnp.where(allowed, jnp.exp(scores), 0.0)
    row_total = lax.optimization_barrier(jnp.sum(expo_all, axis=-1, keepdims=True))
    log_total = jnp.log(row_total)
    attn_probs = expo_all / row_total
    context = jnp.einsum('shqk,skhe->sqhe', round_trip(attn_probs), values_all.astype(jnp.float32)).astype(jnp.bfloat16).reshape(-1, D)
    first_sum = rows_f32 + matmul(context, w_out) + biases[2]
    norm_one, rstd_one = normalize(first_sum)
    mid_norm = norm_one * norm_gains[0] + biases[3]
    mid_b = mid_norm.astype(jnp.bfloat16)
    pre_act = matmul(mid_b, w_up) + up_bias
    act_f32, gelu_slope = gelu_pair(pre_act)
    act_b = act_f32.astype(jnp.bfloat16)
    second_sum = mid_norm + matmul(act_b, w_down) + biases[4]
    norm_two, rstd_two = normalize(second_sum)
    layer_out = norm_two * norm_gains[1] + biases[5]
    saved = (rows_bf, queries, keys_all, values_all, seg_rows, log_total, context, norm_one, rstd_one, mid_b, gelu_slope, act_b, norm_two, rstd_two)
    return (layer_out.reshape(hidden.shape), saved)

def backward_layer(grad_rows, weights, saved):
    w_qkv, w_out, w_up, w_down, biases, norm_gains, up_bias = weights
    rows_bf, queries, keys_all, values_all, seg_rows, log_total, context, norm_one, rstd_one, mid_b, gelu_slope, act_b, norm_two, rstd_two = saved
    seq_count = queries.shape[0]
    d_gain_two = lax.optimization_barrier(jnp.sum(grad_rows * norm_two, axis=0))
    d_bias_two = lax.optimization_barrier(jnp.sum(grad_rows, axis=0))
    d_second = norm_back(grad_rows, norm_two, rstd_two, norm_gains[1])
    d_second_b = d_second.astype(jnp.bfloat16)
    d_bdown = lax.optimization_barrier(jnp.sum(d_second, axis=0))
    d_wdown = matmul_lt(act_b, d_second_b)
    d_pre = matmul_rt(d_second_b, w_down) * gelu_slope
    d_bup = lax.optimization_barrier(jnp.sum(d_pre, axis=0))
    d_pre_b = d_pre.astype(jnp.bfloat16)
    d_wup = matmul_lt(mid_b, d_pre_b)
    d_mid = d_second + matmul_rt(d_pre_b, w_up)
    d_gain_one = lax.optimization_barrier(jnp.sum(d_mid * norm_one, axis=0))
    d_bias_one = lax.optimization_barrier(jnp.sum(d_mid, axis=0))
    d_first = norm_back(d_mid, norm_one, rstd_one, norm_gains[0])
    d_first_b = d_first.astype(jnp.bfloat16)
    d_bout = lax.optimization_barrier(jnp.sum(d_first, axis=0))
    d_wout = matmul_lt(context, d_first_b)
    d_context = matmul_rt(d_first_b, w_out).astype(jnp.bfloat16).reshape(seq_count, -1, HEADS, HEAD_DIM)
    scores, allowed = attention_scores(queries, keys_all, seg_rows, seg_rows)
    probs_again = jnp.where(allowed, jnp.exp(scores - log_total), 0.0)
    d_context_f = d_context.astype(jnp.float32)
    d_probs = jnp.einsum('sqhe,skhe->shqk', d_context_f, values_all.astype(jnp.float32))
    d_scores = round_trip(probs_again * (d_probs - lax.optimization_barrier(jnp.sum(probs_again * d_probs, axis=-1, keepdims=True))) * (1.0 / math.sqrt(HEAD_DIM)))
    d_queries = jnp.einsum('shqk,skhe->sqhe', d_scores, keys_all.astype(jnp.float32)).reshape(-1, D)
    d_keys = jnp.einsum('shqk,sqhe->skhe', d_scores, queries.astype(jnp.float32)).reshape(-1, D)
    d_values = jnp.einsum('shqk,sqhe->skhe', round_trip(probs_again), d_context_f).reshape(-1, D)
    d_qkv = jnp.concatenate([d_queries, d_keys, d_values], axis=-1).astype(jnp.bfloat16)
    d_wqkv = matmul_lt(rows_bf, d_qkv)
    d_hidden = d_first + matmul_rt(d_qkv, w_qkv)
    d_biases = jnp.stack([lax.optimization_barrier(jnp.sum(d_queries, axis=0)), lax.optimization_barrier(jnp.sum(d_values, axis=0)), d_bout, d_bias_one, d_bdown, d_bias_two])
    d_gains = jnp.stack([d_gain_one, d_gain_two])
    return (d_hidden, (d_wqkv, d_wout, d_wup, d_wdown, d_biases, d_gains, d_bup))

def reference(inputs, segment_ids, cotangent, w_qkv, w_out, w_up, w_down, biases, norm_gains, up_bias):
    stacked = (w_qkv, w_out, w_up, w_down, biases, norm_gains, up_bias)
    block_seqs = math.gcd(SEQS, 8)
    block_count = SEQS // block_seqs

    def run_block(carry, pieces):
        block_in, block_seg, block_cot = pieces
        hidden = block_in
        saved_list = []
        for layer_id in range(LAYERS):
            weights = tuple((tensor[layer_id] for tensor in stacked))
            hidden, saved = forward_layer(hidden, block_seg, weights)
            saved_list.append(saved)
        grad_rows = block_cot.reshape(-1, D)
        new_carry = list(carry)
        for layer_id in reversed(range(LAYERS)):
            weights = tuple((tensor[layer_id] for tensor in stacked))
            grad_rows, grads = backward_layer(grad_rows, weights, saved_list[layer_id])
            new_carry[layer_id] = tuple((running + addend for running, addend in zip(carry[layer_id], grads)))
        return (tuple(new_carry), (hidden, grad_rows.reshape(block_in.shape)))
    zero_carry = tuple((tuple((jnp.zeros(tensor.shape[1:], jnp.float32) for tensor in stacked)) for layer_id in range(LAYERS)))
    pieces = (inputs.reshape(block_count, block_seqs, SEQ, D), segment_ids.reshape(block_count, block_seqs, SEQ), cotangent.reshape(block_count, block_seqs, SEQ, D))
    final, (outs_all, grads_all) = lax.scan(run_block, zero_carry, pieces)
    outputs = outs_all.reshape(SEQS, SEQ, D)
    input_grad = grads_all.reshape(SEQS, SEQ, D)
    totals = tuple((jnp.stack([final[layer_id][kind_id] for layer_id in range(LAYERS)]) for kind_id in range(7)))
    return (outputs, input_grad, totals[0], totals[1], totals[2], totals[3], totals[4], totals[5], totals[6])
```

```python
import math

import jax
import jax.numpy as jnp
from jax import lax
from jax.sharding import PartitionSpec as P

D = 1024
HEADS = 16
HEAD_DIM = 64
LAYERS = 1


epsilon = 1e-06


def normalize(residual):
    center = residual - jnp.mean(residual, axis=-1, keepdims=True)
    rstd_val = lax.rsqrt(jnp.mean(center * center, axis=-1, keepdims=True) + epsilon)
    return (center * rstd_val, rstd_val)


def norm_back(grad_out, x_hat, rstd_val, gain_row):
    d_hat = grad_out * gain_row
    return rstd_val * (
        d_hat
        - jnp.mean(d_hat, axis=-1, keepdims=True)
        - x_hat * jnp.mean(d_hat * x_hat, axis=-1, keepdims=True)
    )


def gelu_pair(pre_act):
    normal_cdf = 0.5 * (1.0 + lax.erf(pre_act * (1.0 / math.sqrt(2.0))))
    density = jnp.exp(-0.5 * pre_act * pre_act) * (1.0 / math.sqrt(2.0 * math.pi))
    return (pre_act * normal_cdf, normal_cdf + pre_act * density)


def matmul(first_op, second_op):
    return jnp.dot(first_op, second_op, preferred_element_type=jnp.float32)


def matmul_lt(first_op, second_op):
    return lax.dot_general(
        first_op, second_op, (((0,), (0,)), ((), ())), preferred_element_type=jnp.float32
    )


def matmul_rt(first_op, second_op):
    return lax.dot_general(
        first_op, second_op, (((1,), (1,)), ((), ())), preferred_element_type=jnp.float32
    )


def attention_scores(queries, keys_all, seg_rows, seg_cols):
    scores = jnp.einsum(
        "sqhe,skhe->shqk", queries, keys_all, preferred_element_type=jnp.float32
    ) * (1.0 / math.sqrt(HEAD_DIM))
    allowed = seg_rows[:, None, :, None] == seg_cols[:, None, None, :]
    return (scores, allowed)


def forward_layer(hidden, seg_rows, weights):
    w_qkv, w_out, w_up, w_down, biases, norm_gains, up_bias = weights
    seq_count = hidden.shape[0]
    rows_f32 = hidden.reshape(-1, D)
    rows_bf = rows_f32.astype(jnp.bfloat16)
    qkv_rows = matmul(rows_bf, w_qkv)
    queries = (
        (qkv_rows[:, :D] + biases[0]).astype(jnp.bfloat16).reshape(seq_count, -1, HEADS, HEAD_DIM)
    )
    keys_local = qkv_rows[:, D : 2 * D].astype(jnp.bfloat16)
    values_local = (qkv_rows[:, 2 * D :] + biases[1]).astype(jnp.bfloat16)
    local_pair = jnp.concatenate([keys_local, values_local], axis=-1).reshape(seq_count, -1, 2 * D)
    pair_all, seg_cols = (
        lax.all_gather(local_pair, "rep", axis=1, tiled=True),
        lax.all_gather(seg_rows, "rep", axis=1, tiled=True),
    )
    keys_all = pair_all[:, :, :D].reshape(seq_count, -1, HEADS, HEAD_DIM)
    values_all = pair_all[:, :, D:].reshape(seq_count, -1, HEADS, HEAD_DIM)
    scores, allowed = attention_scores(queries, keys_all, seg_rows, seg_cols)
    expo_all = jnp.where(allowed, jnp.exp(scores), 0.0)
    row_total = jnp.sum(expo_all, axis=-1, keepdims=True)
    log_total = jnp.log(row_total)
    attn_probs = (expo_all / row_total).astype(jnp.bfloat16)
    context = (
        jnp.einsum("shqk,skhe->sqhe", attn_probs, values_all, preferred_element_type=jnp.float32)
        .astype(jnp.bfloat16)
        .reshape(-1, D)
    )
    first_sum = rows_f32 + matmul(context, w_out) + biases[2]
    norm_one, rstd_one = normalize(first_sum)
    mid_norm = norm_one * norm_gains[0] + biases[3]
    mid_b = mid_norm.astype(jnp.bfloat16)
    pre_act = matmul(mid_b, w_up) + up_bias
    act_f32, gelu_slope = gelu_pair(pre_act)
    act_b = act_f32.astype(jnp.bfloat16)
    second_sum = mid_norm + matmul(act_b, w_down) + biases[4]
    norm_two, rstd_two = normalize(second_sum)
    layer_out = norm_two * norm_gains[1] + biases[5]
    saved = (
        rows_bf,
        queries,
        keys_all,
        values_all,
        seg_cols,
        log_total,
        context,
        norm_one,
        rstd_one,
        mid_b,
        gelu_slope,
        act_b,
        norm_two,
        rstd_two,
    )
    return (layer_out.reshape(hidden.shape), saved)


def backward_layer(grad_rows, seg_rows, weights, saved):
    w_qkv, w_out, w_up, w_down, biases, norm_gains, up_bias = weights
    (
        rows_bf,
        queries,
        keys_all,
        values_all,
        seg_cols,
        log_total,
        context,
        norm_one,
        rstd_one,
        mid_b,
        gelu_slope,
        act_b,
        norm_two,
        rstd_two,
    ) = saved
    seq_count = queries.shape[0]
    d_gain_two = jnp.sum(grad_rows * norm_two, axis=0)
    d_bias_two = jnp.sum(grad_rows, axis=0)
    d_second = norm_back(grad_rows, norm_two, rstd_two, norm_gains[1])
    d_second_b = d_second.astype(jnp.bfloat16)
    d_bdown = jnp.sum(d_second, axis=0)
    d_wdown = matmul_lt(act_b, d_second_b)
    d_pre = matmul_rt(d_second_b, w_down) * gelu_slope
    d_bup = jnp.sum(d_pre, axis=0)
    d_pre_b = d_pre.astype(jnp.bfloat16)
    d_wup = matmul_lt(mid_b, d_pre_b)
    d_mid = d_second + matmul_rt(d_pre_b, w_up)
    d_gain_one = jnp.sum(d_mid * norm_one, axis=0)
    d_bias_one = jnp.sum(d_mid, axis=0)
    d_first = norm_back(d_mid, norm_one, rstd_one, norm_gains[0])
    d_first_b = d_first.astype(jnp.bfloat16)
    d_bout = jnp.sum(d_first, axis=0)
    d_wout = matmul_lt(context, d_first_b)
    d_context = (
        matmul_rt(d_first_b, w_out).astype(jnp.bfloat16).reshape(seq_count, -1, HEADS, HEAD_DIM)
    )
    scores, allowed = attention_scores(queries, keys_all, seg_rows, seg_cols)
    probs_again = jnp.where(allowed, jnp.exp(scores - log_total), 0.0)
    d_probs = jnp.einsum(
        "sqhe,skhe->shqk", d_context, values_all, preferred_element_type=jnp.float32
    )
    d_scores = (
        probs_again
        * (d_probs - jnp.sum(probs_again * d_probs, axis=-1, keepdims=True))
        * (1.0 / math.sqrt(HEAD_DIM))
    ).astype(jnp.bfloat16)
    d_queries = jnp.einsum(
        "shqk,skhe->sqhe", d_scores, keys_all, preferred_element_type=jnp.float32
    ).reshape(-1, D)
    d_keys = jnp.einsum(
        "shqk,sqhe->skhe", d_scores, queries, preferred_element_type=jnp.float32
    ).reshape(seq_count, -1, D)
    d_values = jnp.einsum(
        "shqk,sqhe->skhe",
        probs_again.astype(jnp.bfloat16),
        d_context,
        preferred_element_type=jnp.float32,
    ).reshape(seq_count, -1, D)
    d_pair = (
        lax.psum_scatter(
            jnp.concatenate([d_keys, d_values], axis=-1).astype(jnp.bfloat16),
            "rep",
            scatter_dimension=1,
            tiled=True,
        )
        .astype(jnp.float32)
        .reshape(-1, 2 * D)
    )
    d_qkv = jnp.concatenate([d_queries, d_pair], axis=-1).astype(jnp.bfloat16)
    d_wqkv = matmul_lt(rows_bf, d_qkv)
    d_hidden = d_first + matmul_rt(d_qkv, w_qkv)
    d_biases = jnp.stack(
        [
            jnp.sum(d_queries, axis=0),
            jnp.sum(d_pair[:, D:], axis=0),
            d_bout,
            d_bias_one,
            d_bdown,
            d_bias_two,
        ]
    )
    d_gains = jnp.stack([d_gain_one, d_gain_two])
    return (d_hidden, (d_wqkv, d_wout, d_wup, d_wdown, d_biases, d_gains, d_bup))


def pack_rows(tensor, parts):
    return tensor.reshape(parts, -1)


def pack_cols(tensor, parts):
    rows = tensor.shape[0]
    return tensor.reshape(rows, parts, -1).transpose(1, 0, 2).reshape(parts, -1)


def unpack_cols(flat, parts, rows):
    return flat.reshape(parts, rows, -1).transpose(1, 0, 2).reshape(rows, -1)


def local(inputs, segment_ids, cotangent, w_qkv, w_out, w_up, w_down, biases, norm_gains, up_bias):
    hidden = inputs
    layer_id = 0
    parts = lax.axis_size("shard")
    local_params = (
        w_qkv[layer_id],
        w_out[layer_id],
        w_up[layer_id],
        w_down[layer_id],
        biases[layer_id],
        norm_gains[layer_id],
        up_bias[layer_id],
    )
    sizes = [tensor.size for tensor in local_params]
    offsets = [sum(sizes[:i]) for i in range(len(sizes) + 1)]
    packed = jnp.concatenate([tensor.reshape(-1) for tensor in local_params])
    gathered = lax.all_gather(packed, "shard", axis=0, tiled=False)
    pieces = [gathered[:, offsets[i] : offsets[i + 1]] for i in range(len(sizes))]
    weights = (
        pieces[0].reshape(-1, local_params[0].shape[1]),
        pieces[1].reshape(-1, local_params[1].shape[1]),
        pieces[2].reshape(-1, local_params[2].shape[1]),
        pieces[3].reshape(-1, local_params[3].shape[1]),
        unpack_cols(pieces[4], parts, local_params[4].shape[0]),
        unpack_cols(pieces[5], parts, local_params[5].shape[0]),
        pieces[6].reshape(-1),
    )
    hidden, saved = forward_layer(hidden, segment_ids, weights)
    grad_rows = cotangent.reshape(-1, cotangent.shape[-1])
    grad_rows, grads = backward_layer(grad_rows, segment_ids, weights, saved)
    grads_b = [grad.astype(jnp.bfloat16) for grad in grads]
    grad_pack = jnp.concatenate(
        [
            pack_rows(grads_b[0], parts),
            pack_rows(grads_b[1], parts),
            pack_rows(grads_b[2], parts),
            pack_rows(grads_b[3], parts),
            pack_cols(grads_b[4], parts),
            pack_cols(grads_b[5], parts),
            pack_rows(grads_b[6], parts),
        ],
        axis=1,
    )
    width = grad_pack.shape[1]
    padded = -(-width // 1024) * 1024
    grad_pack = jnp.pad(grad_pack, ((0, 0), (0, padded - width))).reshape(parts * 8, -1)
    shares = lax.psum_scatter(grad_pack, "shard", scatter_dimension=0, tiled=True)
    shares = lax.psum(shares, "rep").astype(jnp.float32).reshape(-1)
    totals = [
        shares[offsets[i] : offsets[i + 1]].reshape((1,) + local_params[i].shape)
        for i in range(len(sizes))
    ]
    return (hidden, grad_rows.reshape(inputs.shape), *totals)


def solution(mesh):
    in_specs = (
        P("shard", "rep", None),
        P("shard", "rep"),
        P("shard", "rep", None),
        P(None, "shard", None),
        P(None, "shard", None),
        P(None, "shard", None),
        P(None, "shard", None),
        P(None, None, "shard"),
        P(None, None, "shard"),
        P(None, "shard"),
    )
    out_specs = (
        P("shard", "rep", None),
        P("shard", "rep", None),
        P(None, "shard", None),
        P(None, "shard", None),
        P(None, "shard", None),
        P(None, "shard", None),
        P(None, None, "shard"),
        P(None, None, "shard"),
        P(None, "shard"),
    )
    return jax.shard_map(local, mesh=mesh, in_specs=in_specs, out_specs=out_specs, check_vma=False)
```

```python
import math

import jax
import jax.numpy as jnp
from jax import lax
from jax.sharding import PartitionSpec as P

D = 1024
HEADS = 16
HEAD_DIM = 64
LAYERS = 1


epsilon = 1e-06


def normalize(residual):
    center = residual - jnp.mean(residual, axis=-1, keepdims=True)
    rstd_val = lax.rsqrt(jnp.mean(center * center, axis=-1, keepdims=True) + epsilon)
    return (center * rstd_val, rstd_val)


def norm_back(grad_out, x_hat, rstd_val, gain_row):
    d_hat = grad_out * gain_row
    return rstd_val * (
        d_hat
        - jnp.mean(d_hat, axis=-1, keepdims=True)
        - x_hat * jnp.mean(d_hat * x_hat, axis=-1, keepdims=True)
    )


def gelu_pair(pre_act):
    normal_cdf = 0.5 * (1.0 + lax.erf(pre_act * (1.0 / math.sqrt(2.0))))
    density = jnp.exp(-0.5 * pre_act * pre_act) * (1.0 / math.sqrt(2.0 * math.pi))
    return (pre_act * normal_cdf, normal_cdf + pre_act * density)


def matmul(first_op, second_op):
    return jnp.dot(first_op, second_op, preferred_element_type=jnp.float32)


def matmul_lt(first_op, second_op):
    return lax.dot_general(
        first_op, second_op, (((0,), (0,)), ((), ())), preferred_element_type=jnp.float32
    )


def matmul_rt(first_op, second_op):
    return lax.dot_general(
        first_op, second_op, (((1,), (1,)), ((), ())), preferred_element_type=jnp.float32
    )


def attention_scores(queries, keys_all, seg_rows, seg_cols):
    scores = jnp.einsum(
        "sqhe,skhe->shqk", queries, keys_all, preferred_element_type=jnp.float32
    ) * (1.0 / math.sqrt(HEAD_DIM))
    allowed = seg_rows[:, None, :, None] == seg_cols[:, None, None, :]
    return (scores, allowed)


def pick(tensor, index, axis):
    return lax.dynamic_index_in_dim(tensor, index, axis=axis, keepdims=False)


def pack_cols(tensor, parts):
    rows = tensor.shape[0]
    return tensor.reshape(rows, parts, -1).transpose(1, 0, 2).reshape(parts, -1)


def unpack_cols(flat, parts, rows):
    return flat.reshape(parts, rows, -1).transpose(1, 0, 2).reshape(rows, -1)


def gather_rep(tensor):
    return lax.all_gather(tensor, "rep", axis=0, tiled=True)


def scatter_rep(tensor):
    return lax.psum_scatter(tensor, "rep", scatter_dimension=0, tiled=True)


def local(inputs, segment_ids, cotangent, w_qkv, w_out, w_up, w_down, biases, norm_gains, up_bias):
    parts = lax.axis_size("shard")
    reps = lax.axis_size("rep")
    r = lax.axis_index("rep")
    head_cols = D // reps
    heads_here = HEADS // reps
    ff_all = w_up.shape[2]
    ff_chunk = ff_all // parts
    ff_piece = ff_chunk // reps
    k_rows = D // parts

    qkv_piece = pick(w_qkv[0].reshape(k_rows, 3, reps, head_cols), r, 2).reshape(k_rows, -1)
    out_piece = w_out[0]
    up_piece = pick(w_up[0].reshape(k_rows, parts, reps, ff_piece), r, 2).reshape(k_rows, -1)
    down_piece = pick(w_down[0].reshape(reps, ff_piece, D), r, 0)
    upb_piece = pick(up_bias[0].reshape(reps, ff_piece), r, 0)
    pieces = (qkv_piece, out_piece, up_piece, down_piece, upb_piece, biases[0], norm_gains[0])
    sizes = [piece.size for piece in pieces]
    offsets = [sum(sizes[:i]) for i in range(len(sizes) + 1)]
    packed = jnp.concatenate([piece.reshape(-1) for piece in pieces])
    packed = jnp.pad(packed, (0, -(-packed.size // 1024) * 1024 - packed.size))
    gathered = lax.all_gather(packed, "shard", axis=0, tiled=False)
    got = [gathered[:, offsets[i] : offsets[i + 1]] for i in range(len(sizes))]
    w_qkv_r = got[0].reshape(D, 3 * head_cols)
    w_out_all = got[1].reshape(D, D)
    w_out_r = lax.dynamic_slice_in_dim(w_out_all, r * head_cols, head_cols, axis=0)
    w_up_r = got[2].reshape(D, -1)
    w_down_r = got[3].reshape(-1, D)
    up_bias_r = got[4].reshape(-1)
    bias_all = unpack_cols(got[5], parts, biases.shape[1])
    gain_all = unpack_cols(got[6], parts, norm_gains.shape[1])
    bias_q = lax.dynamic_slice_in_dim(bias_all[0], r * head_cols, head_cols)
    bias_v = lax.dynamic_slice_in_dim(bias_all[1], r * head_cols, head_cols)

    rows_f32 = inputs[0]
    own = rows_f32.shape[0]
    rows_bf = rows_f32.astype(jnp.bfloat16)
    seg_tag = jnp.broadcast_to(segment_ids[0].astype(jnp.bfloat16)[:, None], (own, 128))
    hb_seg = gather_rep(jnp.concatenate([rows_bf, seg_tag], axis=1))
    hb_all = hb_seg[:, :D]
    seg_all = hb_seg[:, D]
    qkv_rows = matmul(hb_all, w_qkv_r)
    queries = (qkv_rows[:, :head_cols] + bias_q).astype(jnp.bfloat16).reshape(1, -1, heads_here, HEAD_DIM)
    keys_all = qkv_rows[:, head_cols : 2 * head_cols].astype(jnp.bfloat16).reshape(1, -1, heads_here, HEAD_DIM)
    values_all = (
        (qkv_rows[:, 2 * head_cols :] + bias_v).astype(jnp.bfloat16).reshape(1, -1, heads_here, HEAD_DIM)
    )
    seg_rows = seg_all[None]
    scores, allowed = attention_scores(queries, keys_all, seg_rows, seg_rows)
    expo_all = jnp.where(allowed, jnp.exp(scores), 0.0)
    row_total = jnp.sum(expo_all, axis=-1, keepdims=True)
    log_total = jnp.log(row_total)
    attn_probs = (expo_all / row_total).astype(jnp.bfloat16)
    context = (
        jnp.einsum("shqk,skhe->sqhe", attn_probs, values_all, preferred_element_type=jnp.float32)
        .astype(jnp.bfloat16)
        .reshape(-1, head_cols)
    )
    first_sum = rows_f32 + scatter_rep(matmul(context, w_out_r)) + bias_all[2]
    norm_one, rstd_one = normalize(first_sum)
    mid_norm = norm_one * gain_all[0] + bias_all[3]
    mid_b = mid_norm.astype(jnp.bfloat16)
    mid_all = gather_rep(mid_b)
    pre_act = matmul(mid_all, w_up_r) + up_bias_r
    act_f32, gelu_slope = gelu_pair(pre_act)
    act_b = act_f32.astype(jnp.bfloat16)
    second_sum = mid_norm + scatter_rep(matmul(act_b, w_down_r)) + bias_all[4]
    norm_two, rstd_two = normalize(second_sum)
    layer_out = norm_two * gain_all[1] + bias_all[5]

    grad_rows = cotangent[0]
    d_gain_two = jnp.sum(grad_rows * norm_two, axis=0)
    d_bias_two = jnp.sum(grad_rows, axis=0)
    d_second = norm_back(grad_rows, norm_two, rstd_two, gain_all[1])
    d_bdown = jnp.sum(d_second, axis=0)
    d_second_all = gather_rep(d_second.astype(jnp.bfloat16))
    d_wdown = matmul_lt(act_b, d_second_all)
    d_pre = matmul_rt(d_second_all, w_down_r) * gelu_slope
    d_bup = jnp.sum(d_pre, axis=0)
    d_pre_b = d_pre.astype(jnp.bfloat16)
    d_wup = matmul_lt(mid_all, d_pre_b)
    d_mid = d_second + scatter_rep(matmul_rt(d_pre_b, w_up_r))
    d_gain_one = jnp.sum(d_mid * norm_one, axis=0)
    d_bias_one = jnp.sum(d_mid, axis=0)
    d_first = norm_back(d_mid, norm_one, rstd_one, gain_all[0])
    d_bout = jnp.sum(d_first, axis=0)
    d_first_all = gather_rep(d_first.astype(jnp.bfloat16))
    d_wout = matmul_lt(context, d_first_all)
    d_context = (
        matmul_rt(d_first_all, w_out_r).astype(jnp.bfloat16).reshape(1, -1, heads_here, HEAD_DIM)
    )
    probs_again = jnp.where(allowed, jnp.exp(scores - log_total), 0.0)
    d_probs = jnp.einsum(
        "sqhe,skhe->shqk", d_context, values_all, preferred_element_type=jnp.float32
    )
    d_scores = (
        probs_again
        * (d_probs - jnp.sum(probs_again * d_probs, axis=-1, keepdims=True))
        * (1.0 / math.sqrt(HEAD_DIM))
    ).astype(jnp.bfloat16)
    d_queries = jnp.einsum(
        "shqk,skhe->sqhe", d_scores, keys_all, preferred_element_type=jnp.float32
    ).reshape(-1, head_cols)
    d_keys = jnp.einsum(
        "shqk,sqhe->skhe", d_scores, queries, preferred_element_type=jnp.float32
    ).reshape(-1, head_cols)
    d_values = jnp.einsum(
        "shqk,sqhe->skhe",
        probs_again.astype(jnp.bfloat16),
        d_context,
        preferred_element_type=jnp.float32,
    ).reshape(-1, head_cols)
    d_qkv = jnp.concatenate([d_queries, d_keys, d_values], axis=-1).astype(jnp.bfloat16)
    d_wqkv = matmul_lt(hb_all, d_qkv)
    input_grad = d_first + scatter_rep(matmul_rt(d_qkv, w_qkv_r))

    zeros_cols = jnp.zeros((D,), jnp.float32)
    d_bq = lax.dynamic_update_slice_in_dim(zeros_cols, jnp.sum(d_queries, axis=0), r * head_cols, 0)
    d_bv = lax.dynamic_update_slice_in_dim(zeros_cols, jnp.sum(d_values, axis=0), r * head_cols, 0)
    d_biases = jnp.stack([d_bq, d_bv, d_bout, d_bias_one, d_bdown, d_bias_two])
    d_gains = jnp.stack([d_gain_one, d_gain_two])
    d_wout_all = lax.dynamic_update_slice_in_dim(
        jnp.zeros((D, D), jnp.bfloat16), d_wout.astype(jnp.bfloat16), r * head_cols, 0
    )
    d_bup_all = lax.dynamic_update_slice_in_dim(
        jnp.zeros((parts, reps, ff_piece), jnp.float32), d_bup.reshape(parts, 1, ff_piece), r, 1
    )
    grad_parts = (
        d_wqkv.astype(jnp.bfloat16).reshape(parts, -1),
        d_wout_all.reshape(parts, -1),
        d_wup.astype(jnp.bfloat16).reshape(parts, -1),
        d_wdown.astype(jnp.bfloat16).reshape(parts, -1),
        d_bup_all.astype(jnp.bfloat16).reshape(parts, -1),
        pack_cols(d_biases.astype(jnp.bfloat16), parts),
        pack_cols(d_gains.astype(jnp.bfloat16), parts),
    )
    g_sizes = [piece.shape[1] for piece in grad_parts]
    g_offsets = [sum(g_sizes[:i]) for i in range(len(g_sizes) + 1)]
    grad_pack = jnp.concatenate(grad_parts, axis=1)
    width = grad_pack.shape[1]
    padded = -(-width // 4096) * 4096
    grad_pack = jnp.pad(grad_pack, ((0, 0), (0, padded - width))).reshape(parts * 32, -1)
    shares = lax.psum_scatter(grad_pack, "shard", scatter_dimension=0, tiled=True)
    joined = lax.all_gather(shares.reshape(-1), "rep", axis=0, tiled=False).astype(jnp.float32)
    got = [joined[:, g_offsets[i] : g_offsets[i + 1]] for i in range(len(g_sizes))]
    grad_w_qkv = got[0].reshape(reps, k_rows, 3, head_cols).transpose(1, 2, 0, 3).reshape(k_rows, -1)
    grad_w_out = jnp.sum(got[1], axis=0).reshape(k_rows, D)
    grad_w_up = got[2].reshape(reps, k_rows, parts, ff_piece).transpose(1, 2, 0, 3).reshape(k_rows, -1)
    grad_w_down = got[3].reshape(reps * ff_piece, D)
    grad_up_bias = jnp.sum(got[4], axis=0)
    grad_biases = jnp.sum(got[5], axis=0).reshape(biases.shape[1], -1)
    grad_gains = jnp.sum(got[6], axis=0).reshape(norm_gains.shape[1], -1)
    return (
        layer_out[None],
        input_grad[None],
        grad_w_qkv[None],
        grad_w_out[None],
        grad_w_up[None],
        grad_w_down[None],
        grad_biases[None],
        grad_gains[None],
        grad_up_bias[None],
    )


def solution(mesh):
    in_specs = (
        P("shard", "rep", None),
        P("shard", "rep"),
        P("shard", "rep", None),
        P(None, "shard", None),
        P(None, "shard", None),
        P(None, "shard", None),
        P(None, "shard", None),
        P(None, None, "shard"),
        P(None, None, "shard"),
        P(None, "shard"),
    )
    out_specs = (
        P("shard", "rep", None),
        P("shard", "rep", None),
        P(None, "shard", None),
        P(None, "shard", None),
        P(None, "shard", None),
        P(None, "shard", None),
        P(None, None, "shard"),
        P(None, None, "shard"),
        P(None, "shard"),
    )
    return jax.shard_map(local, mesh=mesh, in_specs=in_specs, out_specs=out_specs, check_vma=False)
```

```python
import math

import jax
import jax.numpy as jnp
from jax import lax
from jax.sharding import PartitionSpec as P

D = 1024
HEADS = 16
HEAD_DIM = 64
LAYERS = 1


epsilon = 1e-06


def normalize(residual):
    center = residual - jnp.mean(residual, axis=-1, keepdims=True)
    rstd_val = lax.rsqrt(jnp.mean(center * center, axis=-1, keepdims=True) + epsilon)
    return (center * rstd_val, rstd_val)


def norm_back(grad_out, x_hat, rstd_val, gain_row):
    d_hat = grad_out * gain_row
    return rstd_val * (
        d_hat
        - jnp.mean(d_hat, axis=-1, keepdims=True)
        - x_hat * jnp.mean(d_hat * x_hat, axis=-1, keepdims=True)
    )


def gelu_pair(pre_act):
    normal_cdf = 0.5 * (1.0 + lax.erf(pre_act * (1.0 / math.sqrt(2.0))))
    density = jnp.exp(-0.5 * pre_act * pre_act) * (1.0 / math.sqrt(2.0 * math.pi))
    return (pre_act * normal_cdf, normal_cdf + pre_act * density)


def matmul(first_op, second_op):
    return jnp.dot(first_op, second_op, preferred_element_type=jnp.float32)


def matmul_lt(first_op, second_op):
    return lax.dot_general(
        first_op, second_op, (((0,), (0,)), ((), ())), preferred_element_type=jnp.float32
    )


def matmul_rt(first_op, second_op):
    return lax.dot_general(
        first_op, second_op, (((1,), (1,)), ((), ())), preferred_element_type=jnp.float32
    )


def attention_scores(queries, keys_all, seg_rows, seg_cols):
    scores = jnp.einsum(
        "sqhe,skhe->shqk", queries, keys_all, preferred_element_type=jnp.float32
    ) * (1.0 / math.sqrt(HEAD_DIM))
    allowed = seg_rows[:, None, :, None] == seg_cols[:, None, None, :]
    return (scores, allowed)


def pick(tensor, index, axis):
    return lax.dynamic_index_in_dim(tensor, index, axis=axis, keepdims=False)


def pack_cols(tensor, parts):
    rows = tensor.shape[0]
    return tensor.reshape(rows, parts, -1).transpose(1, 0, 2).reshape(parts, -1)


def unpack_cols(flat, parts, rows):
    return flat.reshape(parts, rows, -1).transpose(1, 0, 2).reshape(rows, -1)


def gather_rep(tensor):
    return lax.all_gather(tensor, "rep", axis=0, tiled=True)


def scatter_rep(tensor):
    return lax.psum_scatter(tensor, "rep", scatter_dimension=0, tiled=True)


def local(inputs, segment_ids, cotangent, w_qkv, w_out, w_up, w_down, biases, norm_gains, up_bias):
    parts = lax.axis_size("shard")
    reps = lax.axis_size("rep")
    r = lax.axis_index("rep")
    head_cols = D // reps
    heads_here = HEADS // reps
    ff_all = w_up.shape[2]
    ff_chunk = ff_all // parts
    ff_piece = ff_chunk // reps
    k_rows = D // parts

    qkv_piece = pick(w_qkv[0].reshape(k_rows, 3, reps, head_cols), r, 2).reshape(k_rows, -1)
    out_piece = w_out[0]
    up_piece = pick(w_up[0].reshape(k_rows, parts, reps, ff_piece), r, 2).reshape(k_rows, -1)
    down_piece = pick(w_down[0].reshape(reps, ff_piece, D), r, 0)
    upb_piece = pick(up_bias[0].reshape(reps, ff_piece), r, 0)
    pieces = (qkv_piece, out_piece, up_piece, down_piece, upb_piece, biases[0], norm_gains[0])
    sizes = [piece.size for piece in pieces]
    offsets = [sum(sizes[:i]) for i in range(len(sizes) + 1)]
    packed = jnp.concatenate([piece.reshape(-1) for piece in pieces])
    packed = jnp.pad(packed, (0, -(-packed.size // 1024) * 1024 - packed.size))
    gathered = lax.all_gather(packed, "shard", axis=0, tiled=False)
    got = [gathered[:, offsets[i] : offsets[i + 1]] for i in range(len(sizes))]
    w_qkv_r = got[0].reshape(D, 3 * head_cols)
    w_out_all = got[1].reshape(D, D)
    w_out_r = lax.dynamic_slice_in_dim(w_out_all, r * head_cols, head_cols, axis=0)
    w_up_r = got[2].reshape(D, -1)
    w_down_r = got[3].reshape(-1, D)
    up_bias_r = got[4].reshape(-1)
    bias_all = unpack_cols(got[5], parts, biases.shape[1])
    gain_all = unpack_cols(got[6], parts, norm_gains.shape[1])
    bias_q = lax.dynamic_slice_in_dim(bias_all[0], r * head_cols, head_cols)
    bias_v = lax.dynamic_slice_in_dim(bias_all[1], r * head_cols, head_cols)

    rows_f32 = inputs[0]
    own = rows_f32.shape[0]
    rows_bf = rows_f32.astype(jnp.bfloat16)
    seg_tag = jnp.broadcast_to(segment_ids[0].astype(jnp.bfloat16)[:, None], (own, 128))
    hb_seg = gather_rep(jnp.concatenate([rows_bf, seg_tag], axis=1))
    hb_all = hb_seg[:, :D]
    seg_all = hb_seg[:, D]
    qkv_rows = matmul(hb_all, w_qkv_r)
    queries = (qkv_rows[:, :head_cols] + bias_q).astype(jnp.bfloat16).reshape(1, -1, heads_here, HEAD_DIM)
    keys_all = qkv_rows[:, head_cols : 2 * head_cols].astype(jnp.bfloat16).reshape(1, -1, heads_here, HEAD_DIM)
    values_all = (
        (qkv_rows[:, 2 * head_cols :] + bias_v).astype(jnp.bfloat16).reshape(1, -1, heads_here, HEAD_DIM)
    )
    seg_rows = seg_all[None]
    scores, allowed = attention_scores(queries, keys_all, seg_rows, seg_rows)
    expo_all = jnp.where(allowed, jnp.exp(scores), 0.0)
    row_total = jnp.sum(expo_all, axis=-1, keepdims=True)
    log_total = jnp.log(row_total)
    attn_probs = (expo_all / row_total).astype(jnp.bfloat16)
    context = (
        jnp.einsum("shqk,skhe->sqhe", attn_probs, values_all, preferred_element_type=jnp.float32)
        .astype(jnp.bfloat16)
        .reshape(-1, head_cols)
    )
    first_sum = rows_f32 + scatter_rep(matmul(context, w_out_r)) + bias_all[2]
    norm_one, rstd_one = normalize(first_sum)
    mid_norm = norm_one * gain_all[0] + bias_all[3]
    mid_b = mid_norm.astype(jnp.bfloat16)
    mid_all = gather_rep(mid_b)
    pre_act = matmul(mid_all, w_up_r) + up_bias_r
    act_f32, gelu_slope = gelu_pair(pre_act)
    act_b = act_f32.astype(jnp.bfloat16)
    second_sum = mid_norm + scatter_rep(matmul(act_b, w_down_r)) + bias_all[4]
    norm_two, rstd_two = normalize(second_sum)
    layer_out = norm_two * gain_all[1] + bias_all[5]

    grad_rows = cotangent[0]
    d_gain_two = jnp.sum(grad_rows * norm_two, axis=0)
    d_bias_two = jnp.sum(grad_rows, axis=0)
    d_second = norm_back(grad_rows, norm_two, rstd_two, gain_all[1])
    d_bdown = jnp.sum(d_second, axis=0)
    d_second_all = gather_rep(d_second.astype(jnp.bfloat16))
    d_wdown = matmul_lt(act_b, d_second_all)
    d_pre = matmul_rt(d_second_all, w_down_r) * gelu_slope
    d_bup = jnp.sum(d_pre, axis=0)
    d_pre_b = d_pre.astype(jnp.bfloat16)
    d_wup = matmul_lt(mid_all, d_pre_b)
    d_mid = d_second + scatter_rep(matmul_rt(d_pre_b, w_up_r))
    d_gain_one = jnp.sum(d_mid * norm_one, axis=0)
    d_bias_one = jnp.sum(d_mid, axis=0)
    d_first = norm_back(d_mid, norm_one, rstd_one, gain_all[0])
    d_bout = jnp.sum(d_first, axis=0)
    d_first_all = gather_rep(d_first.astype(jnp.bfloat16))
    d_wout = matmul_lt(context, d_first_all)
    d_context = (
        matmul_rt(d_first_all, w_out_r).astype(jnp.bfloat16).reshape(1, -1, heads_here, HEAD_DIM)
    )
    probs_again = jnp.where(allowed, jnp.exp(scores - log_total), 0.0)
    d_probs = jnp.einsum(
        "sqhe,skhe->shqk", d_context, values_all, preferred_element_type=jnp.float32
    )
    d_scores = (
        probs_again
        * (d_probs - jnp.sum(probs_again * d_probs, axis=-1, keepdims=True))
        * (1.0 / math.sqrt(HEAD_DIM))
    ).astype(jnp.bfloat16)
    d_queries = jnp.einsum(
        "shqk,skhe->sqhe", d_scores, keys_all, preferred_element_type=jnp.float32
    ).reshape(-1, head_cols)
    d_keys = jnp.einsum(
        "shqk,sqhe->skhe", d_scores, queries, preferred_element_type=jnp.float32
    ).reshape(-1, head_cols)
    d_values = jnp.einsum(
        "shqk,sqhe->skhe",
        probs_again.astype(jnp.bfloat16),
        d_context,
        preferred_element_type=jnp.float32,
    ).reshape(-1, head_cols)
    d_qkv = jnp.concatenate([d_queries, d_keys, d_values], axis=-1).astype(jnp.bfloat16)
    d_wqkv = matmul_lt(hb_all, d_qkv)
    input_grad = d_first + scatter_rep(matmul_rt(d_qkv, w_qkv_r))

    zeros_cols = jnp.zeros((D,), jnp.float32)
    d_bq = lax.dynamic_update_slice_in_dim(zeros_cols, jnp.sum(d_queries, axis=0), r * head_cols, 0)
    d_bv = lax.dynamic_update_slice_in_dim(zeros_cols, jnp.sum(d_values, axis=0), r * head_cols, 0)
    d_biases = jnp.stack([d_bq, d_bv, d_bout, d_bias_one, d_bdown, d_bias_two])
    d_gains = jnp.stack([d_gain_one, d_gain_two])
    d_wout_all = lax.dynamic_update_slice_in_dim(
        jnp.zeros((D, D), jnp.bfloat16), d_wout.astype(jnp.bfloat16), r * head_cols, 0
    )
    d_bup_all = lax.dynamic_update_slice_in_dim(
        jnp.zeros((parts, reps, ff_piece), jnp.float32), d_bup.reshape(parts, 1, ff_piece), r, 1
    )
    grad_parts = (
        d_wqkv.astype(jnp.bfloat16).reshape(parts, -1),
        d_wout_all.reshape(parts, -1),
        d_wup.astype(jnp.bfloat16).reshape(parts, -1),
        d_wdown.astype(jnp.bfloat16).reshape(parts, -1),
        d_bup_all.astype(jnp.bfloat16).reshape(parts, -1),
        pack_cols(d_biases.astype(jnp.bfloat16), parts),
        pack_cols(d_gains.astype(jnp.bfloat16), parts),
    )
    g_sizes = [piece.shape[1] for piece in grad_parts]
    g_offsets = [sum(g_sizes[:i]) for i in range(len(g_sizes) + 1)]
    grad_pack = jnp.concatenate(grad_parts, axis=1)
    width = grad_pack.shape[1]
    padded = -(-width // 1024) * 1024
    grad_pack = jnp.pad(grad_pack, ((0, 0), (0, padded - width)))
    received = lax.all_to_all(grad_pack, "shard", 0, 0, tiled=True)
    shares = jnp.sum(received.astype(jnp.float32), axis=0).astype(jnp.bfloat16)
    joined = lax.all_gather(shares.reshape(-1), "rep", axis=0, tiled=False).astype(jnp.float32)
    got = [joined[:, g_offsets[i] : g_offsets[i + 1]] for i in range(len(g_sizes))]
    grad_w_qkv = got[0].reshape(reps, k_rows, 3, head_cols).transpose(1, 2, 0, 3).reshape(k_rows, -1)
    grad_w_out = jnp.sum(got[1], axis=0).reshape(k_rows, D)
    grad_w_up = got[2].reshape(reps, k_rows, parts, ff_piece).transpose(1, 2, 0, 3).reshape(k_rows, -1)
    grad_w_down = got[3].reshape(reps * ff_piece, D)
    grad_up_bias = jnp.sum(got[4], axis=0)
    grad_biases = jnp.sum(got[5], axis=0).reshape(biases.shape[1], -1)
    grad_gains = jnp.sum(got[6], axis=0).reshape(norm_gains.shape[1], -1)
    return (
        layer_out[None],
        input_grad[None],
        grad_w_qkv[None],
        grad_w_out[None],
        grad_w_up[None],
        grad_w_down[None],
        grad_biases[None],
        grad_gains[None],
        grad_up_bias[None],
    )


def solution(mesh):
    in_specs = (
        P("shard", "rep", None),
        P("shard", "rep"),
        P("shard", "rep", None),
        P(None, "shard", None),
        P(None, "shard", None),
        P(None, "shard", None),
        P(None, "shard", None),
        P(None, None, "shard"),
        P(None, None, "shard"),
        P(None, "shard"),
    )
    out_specs = (
        P("shard", "rep", None),
        P("shard", "rep", None),
        P(None, "shard", None),
        P(None, "shard", None),
        P(None, "shard", None),
        P(None, "shard", None),
        P(None, None, "shard"),
        P(None, None, "shard"),
        P(None, "shard"),
    )
    return jax.shard_map(local, mesh=mesh, in_specs=in_specs, out_specs=out_specs, check_vma=False)
```

```python
import math

import jax
import jax.numpy as jnp
from jax import lax
from jax.sharding import PartitionSpec as P

D = 1024
HEADS = 16
HEAD_DIM = 64
LAYERS = 1


epsilon = 1e-06


def normalize(residual):
    center = residual - jnp.mean(residual, axis=-1, keepdims=True)
    rstd_val = lax.rsqrt(jnp.mean(center * center, axis=-1, keepdims=True) + epsilon)
    return (center * rstd_val, rstd_val)


def norm_back(grad_out, x_hat, rstd_val, gain_row):
    d_hat = grad_out * gain_row
    return rstd_val * (
        d_hat
        - jnp.mean(d_hat, axis=-1, keepdims=True)
        - x_hat * jnp.mean(d_hat * x_hat, axis=-1, keepdims=True)
    )


def gelu_pair(pre_act):
    normal_cdf = 0.5 * (1.0 + lax.erf(pre_act * (1.0 / math.sqrt(2.0))))
    density = jnp.exp(-0.5 * pre_act * pre_act) * (1.0 / math.sqrt(2.0 * math.pi))
    return (pre_act * normal_cdf, normal_cdf + pre_act * density)


def matmul(first_op, second_op):
    return jnp.dot(first_op, second_op, preferred_element_type=jnp.float32)


def matmul_lt(first_op, second_op):
    return lax.dot_general(
        first_op, second_op, (((0,), (0,)), ((), ())), preferred_element_type=jnp.float32
    )


def matmul_rt(first_op, second_op):
    return lax.dot_general(
        first_op, second_op, (((1,), (1,)), ((), ())), preferred_element_type=jnp.float32
    )


def attention_scores(queries, keys_all, seg_rows, seg_cols):
    scores = jnp.einsum(
        "sqhe,skhe->shqk", queries, keys_all, preferred_element_type=jnp.float32
    ) * (1.0 / math.sqrt(HEAD_DIM))
    allowed = seg_rows[:, None, :, None] == seg_cols[:, None, None, :]
    return (scores, allowed)


def pick(tensor, index, axis):
    return lax.dynamic_index_in_dim(tensor, index, axis=axis, keepdims=False)


def pack_cols(tensor, parts):
    rows = tensor.shape[0]
    return tensor.reshape(rows, parts, -1).transpose(1, 0, 2).reshape(parts, -1)


def unpack_cols(flat, parts, rows):
    return flat.reshape(parts, rows, -1).transpose(1, 0, 2).reshape(rows, -1)


def gather_rep(tensor):
    return lax.all_gather(tensor, "rep", axis=0, tiled=True)


def scatter_rep(tensor):
    return lax.psum_scatter(tensor, "rep", scatter_dimension=0, tiled=True)


def local(inputs, segment_ids, cotangent, w_qkv, w_out, w_up, w_down, biases, norm_gains, up_bias):
    parts = lax.axis_size("shard")
    reps = lax.axis_size("rep")
    r = lax.axis_index("rep")
    head_cols = D // reps
    heads_here = HEADS // reps
    ff_all = w_up.shape[2]
    ff_chunk = ff_all // parts
    ff_piece = ff_chunk // reps
    k_rows = D // parts

    qkv_piece = pick(w_qkv[0].reshape(k_rows, 3, reps, head_cols), r, 2).reshape(k_rows, -1)
    out_piece = w_out[0]
    up_piece = pick(w_up[0].reshape(k_rows, parts, reps, ff_piece), r, 2).reshape(k_rows, -1)
    down_piece = pick(w_down[0].reshape(reps, ff_piece, D), r, 0)
    upb_piece = pick(up_bias[0].reshape(reps, ff_piece), r, 0)
    pieces = (qkv_piece, upb_piece, biases[0], norm_gains[0])
    sizes = [piece.size for piece in pieces]
    offsets = [sum(sizes[:i]) for i in range(len(sizes) + 1)]
    packed = jnp.concatenate([piece.reshape(-1) for piece in pieces])
    packed = jnp.pad(packed, (0, -(-packed.size // 1024) * 1024 - packed.size))
    gathered = lax.all_gather(packed, "shard", axis=0, tiled=False)
    got = [gathered[:, offsets[i] : offsets[i + 1]] for i in range(len(sizes))]
    w_qkv_r = got[0].reshape(D, 3 * head_cols)
    up_bias_r = got[1].reshape(-1)
    bias_all = unpack_cols(got[2], parts, biases.shape[1])
    gain_all = unpack_cols(got[3], parts, norm_gains.shape[1])
    big = jnp.concatenate([out_piece, up_piece, down_piece], axis=1).reshape(8, -1)
    big_all = lax.all_to_all(
        jnp.broadcast_to(big[None], (parts,) + big.shape), "shard", 0, 0, tiled=True
    ).reshape(parts, k_rows, -1)
    w_out_all = big_all[:, :, :D].reshape(D, D)
    w_out_r = lax.dynamic_slice_in_dim(w_out_all, r * head_cols, head_cols, axis=0)
    w_up_r = big_all[:, :, D : D + up_piece.shape[1]].reshape(D, -1)
    w_down_r = big_all[:, :, D + up_piece.shape[1] :].reshape(-1, D)
    bias_q = lax.dynamic_slice_in_dim(bias_all[0], r * head_cols, head_cols)
    bias_v = lax.dynamic_slice_in_dim(bias_all[1], r * head_cols, head_cols)

    rows_f32 = inputs[0]
    own = rows_f32.shape[0]
    rows_bf = rows_f32.astype(jnp.bfloat16)
    seg_tag = jnp.broadcast_to(segment_ids[0].astype(jnp.bfloat16)[:, None], (own, 128))
    hb_seg = gather_rep(jnp.concatenate([rows_bf, seg_tag], axis=1))
    hb_all = hb_seg[:, :D]
    seg_all = hb_seg[:, D]
    qkv_rows = matmul(hb_all, w_qkv_r)
    queries = (qkv_rows[:, :head_cols] + bias_q).astype(jnp.bfloat16).reshape(1, -1, heads_here, HEAD_DIM)
    keys_all = qkv_rows[:, head_cols : 2 * head_cols].astype(jnp.bfloat16).reshape(1, -1, heads_here, HEAD_DIM)
    values_all = (
        (qkv_rows[:, 2 * head_cols :] + bias_v).astype(jnp.bfloat16).reshape(1, -1, heads_here, HEAD_DIM)
    )
    seg_rows = seg_all[None]
    scores, allowed = attention_scores(queries, keys_all, seg_rows, seg_rows)
    expo_all = jnp.where(allowed, jnp.exp(scores), 0.0)
    row_total = jnp.sum(expo_all, axis=-1, keepdims=True)
    log_total = jnp.log(row_total)
    attn_probs = (expo_all / row_total).astype(jnp.bfloat16)
    context = (
        jnp.einsum("shqk,skhe->sqhe", attn_probs, values_all, preferred_element_type=jnp.float32)
        .astype(jnp.bfloat16)
        .reshape(-1, head_cols)
    )
    first_sum = rows_f32 + scatter_rep(matmul(context, w_out_r)) + bias_all[2]
    norm_one, rstd_one = normalize(first_sum)
    mid_norm = norm_one * gain_all[0] + bias_all[3]
    mid_b = mid_norm.astype(jnp.bfloat16)
    mid_all = gather_rep(mid_b)
    pre_act = matmul(mid_all, w_up_r) + up_bias_r
    act_f32, gelu_slope = gelu_pair(pre_act)
    act_b = act_f32.astype(jnp.bfloat16)
    second_sum = mid_norm + scatter_rep(matmul(act_b, w_down_r)) + bias_all[4]
    norm_two, rstd_two = normalize(second_sum)
    layer_out = norm_two * gain_all[1] + bias_all[5]

    grad_rows = cotangent[0]
    d_gain_two = jnp.sum(grad_rows * norm_two, axis=0)
    d_bias_two = jnp.sum(grad_rows, axis=0)
    d_second = norm_back(grad_rows, norm_two, rstd_two, gain_all[1])
    d_bdown = jnp.sum(d_second, axis=0)
    d_second_all = gather_rep(d_second.astype(jnp.bfloat16))
    d_wdown = matmul_lt(act_b, d_second_all)
    d_pre = matmul_rt(d_second_all, w_down_r) * gelu_slope
    d_bup = jnp.sum(d_pre, axis=0)
    d_pre_b = d_pre.astype(jnp.bfloat16)
    d_wup = matmul_lt(mid_all, d_pre_b)
    ffn_pack = jnp.concatenate(
        [d_wup.astype(jnp.bfloat16).reshape(parts, -1), d_wdown.astype(jnp.bfloat16).reshape(parts, -1)],
        axis=1,
    ).reshape(parts, 8, -1)
    ffn_recv = lax.all_to_all(ffn_pack, "shard", 0, 0, tiled=True)
    ffn_share = jnp.sum(ffn_recv.astype(jnp.float32), axis=0).astype(jnp.bfloat16)
    d_mid = d_second + scatter_rep(matmul_rt(d_pre_b, w_up_r))
    d_gain_one = jnp.sum(d_mid * norm_one, axis=0)
    d_bias_one = jnp.sum(d_mid, axis=0)
    d_first = norm_back(d_mid, norm_one, rstd_one, gain_all[0])
    d_bout = jnp.sum(d_first, axis=0)
    d_first_all = gather_rep(d_first.astype(jnp.bfloat16))
    d_wout = matmul_lt(context, d_first_all)
    d_context = (
        matmul_rt(d_first_all, w_out_r).astype(jnp.bfloat16).reshape(1, -1, heads_here, HEAD_DIM)
    )
    probs_again = jnp.where(allowed, jnp.exp(scores - log_total), 0.0)
    d_probs = jnp.einsum(
        "sqhe,skhe->shqk", d_context, values_all, preferred_element_type=jnp.float32
    )
    d_scores = (
        probs_again
        * (d_probs - jnp.sum(probs_again * d_probs, axis=-1, keepdims=True))
        * (1.0 / math.sqrt(HEAD_DIM))
    ).astype(jnp.bfloat16)
    d_queries = jnp.einsum(
        "shqk,skhe->sqhe", d_scores, keys_all, preferred_element_type=jnp.float32
    ).reshape(-1, head_cols)
    d_keys = jnp.einsum(
        "shqk,sqhe->skhe", d_scores, queries, preferred_element_type=jnp.float32
    ).reshape(-1, head_cols)
    d_values = jnp.einsum(
        "shqk,sqhe->skhe",
        probs_again.astype(jnp.bfloat16),
        d_context,
        preferred_element_type=jnp.float32,
    ).reshape(-1, head_cols)
    d_qkv = jnp.concatenate([d_queries, d_keys, d_values], axis=-1).astype(jnp.bfloat16)
    d_wqkv = matmul_lt(hb_all, d_qkv)
    input_grad = d_first + scatter_rep(matmul_rt(d_qkv, w_qkv_r))

    zeros_cols = jnp.zeros((D,), jnp.float32)
    d_bq = lax.dynamic_update_slice_in_dim(zeros_cols, jnp.sum(d_queries, axis=0), r * head_cols, 0)
    d_bv = lax.dynamic_update_slice_in_dim(zeros_cols, jnp.sum(d_values, axis=0), r * head_cols, 0)
    d_biases = jnp.stack([d_bq, d_bv, d_bout, d_bias_one, d_bdown, d_bias_two])
    d_gains = jnp.stack([d_gain_one, d_gain_two])
    d_wout_all = lax.dynamic_update_slice_in_dim(
        jnp.zeros((D, D), jnp.bfloat16), d_wout.astype(jnp.bfloat16), r * head_cols, 0
    )
    d_bup_all = lax.dynamic_update_slice_in_dim(
        jnp.zeros((parts, reps, ff_piece), jnp.float32), d_bup.reshape(parts, 1, ff_piece), r, 1
    )
    grad_parts = (
        d_wqkv.astype(jnp.bfloat16).reshape(parts, -1),
        d_wout_all.reshape(parts, -1),
        d_bup_all.astype(jnp.bfloat16).reshape(parts, -1),
        pack_cols(d_biases.astype(jnp.bfloat16), parts),
        pack_cols(d_gains.astype(jnp.bfloat16), parts),
    )
    g_sizes = [piece.shape[1] for piece in grad_parts]
    grad_pack = jnp.concatenate(grad_parts, axis=1)
    width = grad_pack.shape[1]
    padded = -(-width // 1024) * 1024
    grad_pack = jnp.pad(grad_pack, ((0, 0), (0, padded - width))).reshape(parts, 8, -1)
    received = lax.all_to_all(grad_pack, "shard", 0, 0, tiled=True)
    shares = jnp.sum(received.astype(jnp.float32), axis=0).astype(jnp.bfloat16)
    all_shares = jnp.concatenate([shares.reshape(-1), ffn_share.reshape(-1)])
    joined = lax.all_gather(all_shares, "rep", axis=0, tiled=False).astype(jnp.float32)
    g_sizes = g_sizes + [padded - width, ffn_share.size // 2, ffn_share.size // 2]
    names = ["qkv", "out", "bup", "bias", "gain", "pad", "up", "down"]
    g_offsets = [sum(g_sizes[:i]) for i in range(len(g_sizes) + 1)]
    got = {names[i]: joined[:, g_offsets[i] : g_offsets[i + 1]] for i in range(len(g_sizes))}
    grad_w_qkv = got["qkv"].reshape(reps, k_rows, 3, head_cols).transpose(1, 2, 0, 3).reshape(k_rows, -1)
    grad_w_out = jnp.sum(got["out"], axis=0).reshape(k_rows, D)
    grad_w_up = got["up"].reshape(reps, k_rows, parts, ff_piece).transpose(1, 2, 0, 3).reshape(k_rows, -1)
    grad_w_down = got["down"].reshape(reps * ff_piece, D)
    grad_up_bias = jnp.sum(got["bup"], axis=0)
    grad_biases = jnp.sum(got["bias"], axis=0).reshape(biases.shape[1], -1)
    grad_gains = jnp.sum(got["gain"], axis=0).reshape(norm_gains.shape[1], -1)
    return (
        layer_out[None],
        input_grad[None],
        grad_w_qkv[None],
        grad_w_out[None],
        grad_w_up[None],
        grad_w_down[None],
        grad_biases[None],
        grad_gains[None],
        grad_up_bias[None],
    )


def solution(mesh):
    in_specs = (
        P("shard", "rep", None),
        P("shard", "rep"),
        P("shard", "rep", None),
        P(None, "shard", None),
        P(None, "shard", None),
        P(None, "shard", None),
        P(None, "shard", None),
        P(None, None, "shard"),
        P(None, None, "shard"),
        P(None, "shard"),
    )
    out_specs = (
        P("shard", "rep", None),
        P("shard", "rep", None),
        P(None, "shard", None),
        P(None, "shard", None),
        P(None, "shard", None),
        P(None, "shard", None),
        P(None, None, "shard"),
        P(None, None, "shard"),
        P(None, "shard"),
    )
    return jax.shard_map(local, mesh=mesh, in_specs=in_specs, out_specs=out_specs, check_vma=False)
```

```python
import math

import jax
import jax.numpy as jnp
from jax import lax
from jax.sharding import PartitionSpec as P

D = 1024
HEADS = 16
HEAD_DIM = 64
LAYERS = 1


epsilon = 1e-06


def normalize(residual):
    center = residual - jnp.mean(residual, axis=-1, keepdims=True)
    rstd_val = lax.rsqrt(jnp.mean(center * center, axis=-1, keepdims=True) + epsilon)
    return (center * rstd_val, rstd_val)


def norm_back(grad_out, x_hat, rstd_val, gain_row):
    d_hat = grad_out * gain_row
    return rstd_val * (
        d_hat
        - jnp.mean(d_hat, axis=-1, keepdims=True)
        - x_hat * jnp.mean(d_hat * x_hat, axis=-1, keepdims=True)
    )


def gelu_pair(pre_act):
    normal_cdf = 0.5 * (1.0 + lax.erf(pre_act * (1.0 / math.sqrt(2.0))))
    density = jnp.exp(-0.5 * pre_act * pre_act) * (1.0 / math.sqrt(2.0 * math.pi))
    return (pre_act * normal_cdf, normal_cdf + pre_act * density)


def matmul(first_op, second_op):
    return jnp.dot(first_op, second_op, preferred_element_type=jnp.float32)


def matmul_lt(first_op, second_op):
    return lax.dot_general(
        first_op, second_op, (((0,), (0,)), ((), ())), preferred_element_type=jnp.float32
    )


def matmul_rt(first_op, second_op):
    return lax.dot_general(
        first_op, second_op, (((1,), (1,)), ((), ())), preferred_element_type=jnp.float32
    )


def attention_scores(queries, keys_all, seg_rows, seg_cols):
    scores = jnp.einsum(
        "sqhe,skhe->shqk", queries, keys_all, preferred_element_type=jnp.float32
    ) * (1.0 / math.sqrt(HEAD_DIM))
    allowed = seg_rows[:, None, :, None] == seg_cols[:, None, None, :]
    return (scores, allowed)


def pick(tensor, index, axis):
    return lax.dynamic_index_in_dim(tensor, index, axis=axis, keepdims=False)


def pack_cols(tensor, parts):
    rows = tensor.shape[0]
    return tensor.reshape(rows, parts, -1).transpose(1, 0, 2).reshape(parts, -1)


def unpack_cols(flat, parts, rows):
    return flat.reshape(parts, rows, -1).transpose(1, 0, 2).reshape(rows, -1)


def gather_rep(tensor):
    return lax.all_gather(tensor, "rep", axis=0, tiled=True)


def scatter_rep(tensor):
    return lax.psum_scatter(tensor, "rep", scatter_dimension=0, tiled=True)


def local(inputs, segment_ids, cotangent, w_qkv, w_out, w_up, w_down, biases, norm_gains, up_bias):
    parts = lax.axis_size("shard")
    reps = lax.axis_size("rep")
    r = lax.axis_index("rep")
    head_cols = D // reps
    heads_here = HEADS // reps
    ff_all = w_up.shape[2]
    ff_chunk = ff_all // parts
    ff_piece = ff_chunk // reps
    k_rows = D // parts

    qkv_piece = pick(w_qkv[0].reshape(k_rows, 3, reps, head_cols), r, 2).reshape(k_rows, -1)
    out_piece = w_out[0]
    up_piece = pick(w_up[0].reshape(k_rows, parts, reps, ff_piece), r, 2).reshape(k_rows, -1)
    down_piece = pick(w_down[0].reshape(reps, ff_piece, D), r, 0)
    upb_piece = pick(up_bias[0].reshape(reps, ff_piece), r, 0)
    pieces = (qkv_piece, out_piece, up_piece, down_piece, upb_piece, biases[0], norm_gains[0])
    sizes = [piece.size for piece in pieces]
    offsets = [sum(sizes[:i]) for i in range(len(sizes) + 1)]
    packed = jnp.concatenate([piece.reshape(-1) for piece in pieces])
    packed = jnp.pad(packed, (0, -(-packed.size // 1024) * 1024 - packed.size))
    gathered = lax.all_gather(packed, "shard", axis=0, tiled=False)
    got = [gathered[:, offsets[i] : offsets[i + 1]] for i in range(len(sizes))]
    w_qkv_r = got[0].reshape(D, 3 * head_cols)
    w_out_all = got[1].reshape(D, D)
    w_out_r = lax.dynamic_slice_in_dim(w_out_all, r * head_cols, head_cols, axis=0)
    w_up_r = got[2].reshape(D, -1)
    w_down_r = got[3].reshape(-1, D)
    up_bias_r = got[4].reshape(-1)
    bias_all = unpack_cols(got[5], parts, biases.shape[1])
    gain_all = unpack_cols(got[6], parts, norm_gains.shape[1])
    bias_q = lax.dynamic_slice_in_dim(bias_all[0], r * head_cols, head_cols)
    bias_v = lax.dynamic_slice_in_dim(bias_all[1], r * head_cols, head_cols)

    rows_f32 = inputs[0]
    own = rows_f32.shape[0]
    rows_bf = rows_f32.astype(jnp.bfloat16)
    seg_tag = jnp.broadcast_to(segment_ids[0].astype(jnp.bfloat16)[:, None], (own, 128))
    hb_seg = gather_rep(jnp.concatenate([rows_bf, seg_tag], axis=1))
    hb_all = hb_seg[:, :D]
    seg_all = hb_seg[:, D]
    qkv_rows = matmul(hb_all, w_qkv_r)
    queries = (qkv_rows[:, :head_cols] + bias_q).astype(jnp.bfloat16).reshape(1, -1, heads_here, HEAD_DIM)
    keys_all = qkv_rows[:, head_cols : 2 * head_cols].astype(jnp.bfloat16).reshape(1, -1, heads_here, HEAD_DIM)
    values_all = (
        (qkv_rows[:, 2 * head_cols :] + bias_v).astype(jnp.bfloat16).reshape(1, -1, heads_here, HEAD_DIM)
    )
    seg_rows = seg_all[None]
    scores, allowed = attention_scores(queries, keys_all, seg_rows, seg_rows)
    expo_all = jnp.where(allowed, jnp.exp(scores), 0.0)
    row_total = jnp.sum(expo_all, axis=-1, keepdims=True)
    log_total = jnp.log(row_total)
    attn_probs = (expo_all / row_total).astype(jnp.bfloat16)
    context = (
        jnp.einsum("shqk,skhe->sqhe", attn_probs, values_all, preferred_element_type=jnp.float32)
        .astype(jnp.bfloat16)
        .reshape(-1, head_cols)
    )
    first_sum = rows_f32 + scatter_rep(matmul(context, w_out_r)) + bias_all[2]
    norm_one, rstd_one = normalize(first_sum)
    mid_norm = norm_one * gain_all[0] + bias_all[3]
    mid_b = mid_norm.astype(jnp.bfloat16)
    mid_all = gather_rep(mid_b)
    pre_act = matmul(mid_all, w_up_r) + up_bias_r
    act_f32, gelu_slope = gelu_pair(pre_act)
    act_b = act_f32.astype(jnp.bfloat16)
    second_sum = mid_norm + scatter_rep(matmul(act_b, w_down_r)) + bias_all[4]
    norm_two, rstd_two = normalize(second_sum)
    layer_out = norm_two * gain_all[1] + bias_all[5]

    grad_rows = cotangent[0]
    d_gain_two = jnp.sum(grad_rows * norm_two, axis=0)
    d_bias_two = jnp.sum(grad_rows, axis=0)
    d_second = norm_back(grad_rows, norm_two, rstd_two, gain_all[1])
    d_bdown = jnp.sum(d_second, axis=0)
    d_second_all = gather_rep(d_second.astype(jnp.bfloat16))
    d_wdown = matmul_lt(act_b, d_second_all)
    d_pre = matmul_rt(d_second_all, w_down_r) * gelu_slope
    d_bup = jnp.sum(d_pre, axis=0)
    d_pre_b = d_pre.astype(jnp.bfloat16)
    d_wup = matmul_lt(mid_all, d_pre_b)
    ffn_pack = jnp.concatenate(
        [d_wup.astype(jnp.bfloat16).reshape(parts, -1), d_wdown.astype(jnp.bfloat16).reshape(parts, -1)],
        axis=1,
    ).reshape(parts, 8, -1)
    ffn_recv = lax.all_to_all(ffn_pack, "shard", 0, 0, tiled=True)
    ffn_share = jnp.sum(ffn_recv.astype(jnp.float32), axis=0).astype(jnp.bfloat16)
    d_mid = d_second + scatter_rep(matmul_rt(d_pre_b, w_up_r))
    d_gain_one = jnp.sum(d_mid * norm_one, axis=0)
    d_bias_one = jnp.sum(d_mid, axis=0)
    d_first = norm_back(d_mid, norm_one, rstd_one, gain_all[0])
    d_bout = jnp.sum(d_first, axis=0)
    d_first_all = gather_rep(d_first.astype(jnp.bfloat16))
    d_wout = matmul_lt(context, d_first_all)
    d_context = (
        matmul_rt(d_first_all, w_out_r).astype(jnp.bfloat16).reshape(1, -1, heads_here, HEAD_DIM)
    )
    probs_again = jnp.where(allowed, jnp.exp(scores - log_total), 0.0)
    d_probs = jnp.einsum(
        "sqhe,skhe->shqk", d_context, values_all, preferred_element_type=jnp.float32
    )
    d_scores = (
        probs_again
        * (d_probs - jnp.sum(probs_again * d_probs, axis=-1, keepdims=True))
        * (1.0 / math.sqrt(HEAD_DIM))
    ).astype(jnp.bfloat16)
    d_queries = jnp.einsum(
        "shqk,skhe->sqhe", d_scores, keys_all, preferred_element_type=jnp.float32
    ).reshape(-1, head_cols)
    d_keys = jnp.einsum(
        "shqk,sqhe->skhe", d_scores, queries, preferred_element_type=jnp.float32
    ).reshape(-1, head_cols)
    d_values = jnp.einsum(
        "shqk,sqhe->skhe",
        probs_again.astype(jnp.bfloat16),
        d_context,
        preferred_element_type=jnp.float32,
    ).reshape(-1, head_cols)
    d_qkv = jnp.concatenate([d_queries, d_keys, d_values], axis=-1).astype(jnp.bfloat16)
    d_wqkv = matmul_lt(hb_all, d_qkv)
    input_grad = d_first + scatter_rep(matmul_rt(d_qkv, w_qkv_r))

    zeros_cols = jnp.zeros((D,), jnp.float32)
    d_bq = lax.dynamic_update_slice_in_dim(zeros_cols, jnp.sum(d_queries, axis=0), r * head_cols, 0)
    d_bv = lax.dynamic_update_slice_in_dim(zeros_cols, jnp.sum(d_values, axis=0), r * head_cols, 0)
    d_biases = jnp.stack([d_bq, d_bv, d_bout, d_bias_one, d_bdown, d_bias_two])
    d_gains = jnp.stack([d_gain_one, d_gain_two])
    d_wout_all = lax.dynamic_update_slice_in_dim(
        jnp.zeros((D, D), jnp.bfloat16), d_wout.astype(jnp.bfloat16), r * head_cols, 0
    )
    d_bup_all = lax.dynamic_update_slice_in_dim(
        jnp.zeros((parts, reps, ff_piece), jnp.float32), d_bup.reshape(parts, 1, ff_piece), r, 1
    )
    grad_parts = (
        d_wqkv.astype(jnp.bfloat16).reshape(parts, -1),
        d_wout_all.reshape(parts, -1),
        d_bup_all.astype(jnp.bfloat16).reshape(parts, -1),
        pack_cols(d_biases.astype(jnp.bfloat16), parts),
        pack_cols(d_gains.astype(jnp.bfloat16), parts),
    )
    g_sizes = [piece.shape[1] for piece in grad_parts]
    grad_pack = jnp.concatenate(grad_parts, axis=1)
    width = grad_pack.shape[1]
    padded = -(-width // 1024) * 1024
    grad_pack = jnp.pad(grad_pack, ((0, 0), (0, padded - width))).reshape(parts, 8, -1)
    received = lax.all_to_all(grad_pack, "shard", 0, 0, tiled=True)
    shares = jnp.sum(received.astype(jnp.float32), axis=0).astype(jnp.bfloat16)
    all_shares = jnp.concatenate([shares.reshape(-1), ffn_share.reshape(-1)])
    joined = lax.all_gather(all_shares, "rep", axis=0, tiled=False).astype(jnp.float32)
    g_sizes = g_sizes + [padded - width, ffn_share.size // 2, ffn_share.size // 2]
    names = ["qkv", "out", "bup", "bias", "gain", "pad", "up", "down"]
    g_offsets = [sum(g_sizes[:i]) for i in range(len(g_sizes) + 1)]
    got = {names[i]: joined[:, g_offsets[i] : g_offsets[i + 1]] for i in range(len(g_sizes))}
    grad_w_qkv = got["qkv"].reshape(reps, k_rows, 3, head_cols).transpose(1, 2, 0, 3).reshape(k_rows, -1)
    grad_w_out = jnp.sum(got["out"], axis=0).reshape(k_rows, D)
    grad_w_up = got["up"].reshape(reps, k_rows, parts, ff_piece).transpose(1, 2, 0, 3).reshape(k_rows, -1)
    grad_w_down = got["down"].reshape(reps * ff_piece, D)
    grad_up_bias = jnp.sum(got["bup"], axis=0)
    grad_biases = jnp.sum(got["bias"], axis=0).reshape(biases.shape[1], -1)
    grad_gains = jnp.sum(got["gain"], axis=0).reshape(norm_gains.shape[1], -1)
    return (
        layer_out[None],
        input_grad[None],
        grad_w_qkv[None],
        grad_w_out[None],
        grad_w_up[None],
        grad_w_down[None],
        grad_biases[None],
        grad_gains[None],
        grad_up_bias[None],
    )


def solution(mesh):
    in_specs = (
        P("shard", "rep", None),
        P("shard", "rep"),
        P("shard", "rep", None),
        P(None, "shard", None),
        P(None, "shard", None),
        P(None, "shard", None),
        P(None, "shard", None),
        P(None, None, "shard"),
        P(None, None, "shard"),
        P(None, "shard"),
    )
    out_specs = (
        P("shard", "rep", None),
        P("shard", "rep", None),
        P(None, "shard", None),
        P(None, "shard", None),
        P(None, "shard", None),
        P(None, "shard", None),
        P(None, None, "shard"),
        P(None, None, "shard"),
        P(None, "shard"),
    )
    return jax.shard_map(local, mesh=mesh, in_specs=in_specs, out_specs=out_specs, check_vma=False)
```

```python
import math

import jax
import jax.numpy as jnp
from jax import lax
from jax.experimental import pallas as pl
from jax.experimental.pallas import tpu as pltpu
from jax.sharding import PartitionSpec as P

D = 1024
HEADS = 16
HEAD_DIM = 64
LAYERS = 1


epsilon = 1e-06


def normalize(residual):
    center = residual - jnp.mean(residual, axis=-1, keepdims=True)
    rstd_val = lax.rsqrt(jnp.mean(center * center, axis=-1, keepdims=True) + epsilon)
    return (center * rstd_val, rstd_val)


def norm_back(grad_out, x_hat, rstd_val, gain_row):
    d_hat = grad_out * gain_row
    return rstd_val * (
        d_hat
        - jnp.mean(d_hat, axis=-1, keepdims=True)
        - x_hat * jnp.mean(d_hat * x_hat, axis=-1, keepdims=True)
    )


def gelu_pair(pre_act):
    normal_cdf = 0.5 * (1.0 + lax.erf(pre_act * (1.0 / math.sqrt(2.0))))
    density = jnp.exp(-0.5 * pre_act * pre_act) * (1.0 / math.sqrt(2.0 * math.pi))
    return (pre_act * normal_cdf, normal_cdf + pre_act * density)


def matmul(first_op, second_op):
    return jnp.dot(first_op, second_op, preferred_element_type=jnp.float32)


def matmul_lt(first_op, second_op):
    return lax.dot_general(
        first_op, second_op, (((0,), (0,)), ((), ())), preferred_element_type=jnp.float32
    )


def matmul_rt(first_op, second_op):
    return lax.dot_general(
        first_op, second_op, (((1,), (1,)), ((), ())), preferred_element_type=jnp.float32
    )


def attention_scores(queries, keys_all, seg_rows, seg_cols):
    scores = jnp.einsum(
        "sqhe,skhe->shqk", queries, keys_all, preferred_element_type=jnp.float32
    ) * (1.0 / math.sqrt(HEAD_DIM))
    allowed = seg_rows[:, None, :, None] == seg_cols[:, None, None, :]
    return (scores, allowed)


def pick(tensor, index, axis):
    return lax.dynamic_index_in_dim(tensor, index, axis=axis, keepdims=False)


def pack_cols(tensor, parts):
    rows = tensor.shape[0]
    return tensor.reshape(rows, parts, -1).transpose(1, 0, 2).reshape(parts, -1)


def unpack_cols(flat, parts, rows):
    return flat.reshape(parts, rows, -1).transpose(1, 0, 2).reshape(rows, -1)


def rep_gather_kernel(x_ref, o_ref, send_sem, recv_sem):
    n = lax.axis_size("rep")
    me = lax.axis_index("rep")
    rows = x_ref.shape[0]
    o_ref[pl.ds(me * rows, rows), :] = x_ref[...]
    barrier = pltpu.get_barrier_semaphore()
    for k in range(1, n):
        pl.semaphore_signal(
            barrier, inc=1, device_id={"rep": lax.rem(me + k, n)}, device_id_type=pl.DeviceIdType.MESH
        )
    pl.semaphore_wait(barrier, n - 1)
    copies = []
    for k in range(1, n):
        copy = pltpu.make_async_remote_copy(
            src_ref=x_ref,
            dst_ref=o_ref.at[pl.ds(me * rows, rows)],
            send_sem=send_sem.at[k - 1],
            recv_sem=recv_sem.at[k - 1],
            device_id={"rep": lax.rem(me + k, n)},
            device_id_type=pl.DeviceIdType.MESH,
        )
        copy.start()
        copies.append(copy)
    for copy in copies:
        copy.wait()


def gather_rep(tensor, cid=1):
    n = lax.axis_size("rep")
    rows, cols = tensor.shape
    return pl.pallas_call(
        rep_gather_kernel,
        out_shape=jax.ShapeDtypeStruct((n * rows, cols), tensor.dtype),
        in_specs=[pl.BlockSpec(memory_space=pltpu.VMEM)],
        out_specs=pl.BlockSpec(memory_space=pltpu.VMEM),
        scratch_shapes=[pltpu.SemaphoreType.DMA((n - 1,)), pltpu.SemaphoreType.DMA((n - 1,))],
        compiler_params=pltpu.CompilerParams(collective_id=cid, has_side_effects=True),
    )(tensor)


def scatter_rep(tensor):
    return lax.psum_scatter(tensor, "rep", scatter_dimension=0, tiled=True)


def local(inputs, segment_ids, cotangent, w_qkv, w_out, w_up, w_down, biases, norm_gains, up_bias):
    parts = lax.axis_size("shard")
    reps = lax.axis_size("rep")
    r = lax.axis_index("rep")
    head_cols = D // reps
    heads_here = HEADS // reps
    ff_all = w_up.shape[2]
    ff_chunk = ff_all // parts
    ff_piece = ff_chunk // reps
    k_rows = D // parts

    qkv_piece = pick(w_qkv[0].reshape(k_rows, 3, reps, head_cols), r, 2).reshape(k_rows, -1)
    out_piece = w_out[0]
    up_piece = pick(w_up[0].reshape(k_rows, parts, reps, ff_piece), r, 2).reshape(k_rows, -1)
    down_piece = pick(w_down[0].reshape(reps, ff_piece, D), r, 0)
    upb_piece = pick(up_bias[0].reshape(reps, ff_piece), r, 0)
    pieces = (qkv_piece, out_piece, up_piece, down_piece, upb_piece, biases[0], norm_gains[0])
    sizes = [piece.size for piece in pieces]
    offsets = [sum(sizes[:i]) for i in range(len(sizes) + 1)]
    packed = jnp.concatenate([piece.reshape(-1) for piece in pieces])
    packed = jnp.pad(packed, (0, -(-packed.size // 1024) * 1024 - packed.size))
    gathered = lax.all_gather(packed, "shard", axis=0, tiled=False)
    got = [gathered[:, offsets[i] : offsets[i + 1]] for i in range(len(sizes))]
    w_qkv_r = got[0].reshape(D, 3 * head_cols)
    w_out_all = got[1].reshape(D, D)
    w_out_r = lax.dynamic_slice_in_dim(w_out_all, r * head_cols, head_cols, axis=0)
    w_up_r = got[2].reshape(D, -1)
    w_down_r = got[3].reshape(-1, D)
    up_bias_r = got[4].reshape(-1)
    bias_all = unpack_cols(got[5], parts, biases.shape[1])
    gain_all = unpack_cols(got[6], parts, norm_gains.shape[1])
    bias_q = lax.dynamic_slice_in_dim(bias_all[0], r * head_cols, head_cols)
    bias_v = lax.dynamic_slice_in_dim(bias_all[1], r * head_cols, head_cols)

    rows_f32 = inputs[0]
    own = rows_f32.shape[0]
    rows_bf = rows_f32.astype(jnp.bfloat16)
    seg_tag = jnp.broadcast_to(segment_ids[0].astype(jnp.bfloat16)[:, None], (own, 128))
    hb_seg = gather_rep(jnp.concatenate([rows_bf, seg_tag], axis=1), cid=0)
    hb_all = hb_seg[:, :D]
    seg_all = hb_seg[:, D]
    qkv_rows = matmul(hb_all, w_qkv_r)
    queries = (qkv_rows[:, :head_cols] + bias_q).astype(jnp.bfloat16).reshape(1, -1, heads_here, HEAD_DIM)
    keys_all = qkv_rows[:, head_cols : 2 * head_cols].astype(jnp.bfloat16).reshape(1, -1, heads_here, HEAD_DIM)
    values_all = (
        (qkv_rows[:, 2 * head_cols :] + bias_v).astype(jnp.bfloat16).reshape(1, -1, heads_here, HEAD_DIM)
    )
    seg_rows = seg_all[None]
    scores, allowed = attention_scores(queries, keys_all, seg_rows, seg_rows)
    expo_all = jnp.where(allowed, jnp.exp(scores), 0.0)
    row_total = jnp.sum(expo_all, axis=-1, keepdims=True)
    log_total = jnp.log(row_total)
    attn_probs = (expo_all / row_total).astype(jnp.bfloat16)
    context = (
        jnp.einsum("shqk,skhe->sqhe", attn_probs, values_all, preferred_element_type=jnp.float32)
        .astype(jnp.bfloat16)
        .reshape(-1, head_cols)
    )
    first_sum = rows_f32 + scatter_rep(matmul(context, w_out_r)) + bias_all[2]
    norm_one, rstd_one = normalize(first_sum)
    mid_norm = norm_one * gain_all[0] + bias_all[3]
    mid_b = mid_norm.astype(jnp.bfloat16)
    mid_all = gather_rep(mid_b)
    pre_act = matmul(mid_all, w_up_r) + up_bias_r
    act_f32, gelu_slope = gelu_pair(pre_act)
    act_b = act_f32.astype(jnp.bfloat16)
    second_sum = mid_norm + scatter_rep(matmul(act_b, w_down_r)) + bias_all[4]
    norm_two, rstd_two = normalize(second_sum)
    layer_out = norm_two * gain_all[1] + bias_all[5]

    grad_rows = cotangent[0]
    d_gain_two = jnp.sum(grad_rows * norm_two, axis=0)
    d_bias_two = jnp.sum(grad_rows, axis=0)
    d_second = norm_back(grad_rows, norm_two, rstd_two, gain_all[1])
    d_bdown = jnp.sum(d_second, axis=0)
    d_second_all = gather_rep(d_second.astype(jnp.bfloat16))
    d_wdown = matmul_lt(act_b, d_second_all)
    d_pre = matmul_rt(d_second_all, w_down_r) * gelu_slope
    d_bup = jnp.sum(d_pre, axis=0)
    d_pre_b = d_pre.astype(jnp.bfloat16)
    d_wup = matmul_lt(mid_all, d_pre_b)
    ffn_pack = jnp.concatenate(
        [d_wup.astype(jnp.bfloat16).reshape(parts, -1), d_wdown.astype(jnp.bfloat16).reshape(parts, -1)],
        axis=1,
    ).reshape(parts, 8, -1)
    ffn_recv = lax.all_to_all(ffn_pack, "shard", 0, 0, tiled=True)
    ffn_share = jnp.sum(ffn_recv.astype(jnp.float32), axis=0).astype(jnp.bfloat16)
    d_mid = d_second + scatter_rep(matmul_rt(d_pre_b, w_up_r))
    d_gain_one = jnp.sum(d_mid * norm_one, axis=0)
    d_bias_one = jnp.sum(d_mid, axis=0)
    d_first = norm_back(d_mid, norm_one, rstd_one, gain_all[0])
    d_bout = jnp.sum(d_first, axis=0)
    d_first_all = gather_rep(d_first.astype(jnp.bfloat16))
    d_wout = matmul_lt(context, d_first_all)
    d_context = (
        matmul_rt(d_first_all, w_out_r).astype(jnp.bfloat16).reshape(1, -1, heads_here, HEAD_DIM)
    )
    probs_again = jnp.where(allowed, jnp.exp(scores - log_total), 0.0)
    d_probs = jnp.einsum(
        "sqhe,skhe->shqk", d_context, values_all, preferred_element_type=jnp.float32
    )
    d_scores = (
        probs_again
        * (d_probs - jnp.sum(probs_again * d_probs, axis=-1, keepdims=True))
        * (1.0 / math.sqrt(HEAD_DIM))
    ).astype(jnp.bfloat16)
    d_queries = jnp.einsum(
        "shqk,skhe->sqhe", d_scores, keys_all, preferred_element_type=jnp.float32
    ).reshape(-1, head_cols)
    d_keys = jnp.einsum(
        "shqk,sqhe->skhe", d_scores, queries, preferred_element_type=jnp.float32
    ).reshape(-1, head_cols)
    d_values = jnp.einsum(
        "shqk,sqhe->skhe",
        probs_again.astype(jnp.bfloat16),
        d_context,
        preferred_element_type=jnp.float32,
    ).reshape(-1, head_cols)
    d_qkv = jnp.concatenate([d_queries, d_keys, d_values], axis=-1).astype(jnp.bfloat16)
    d_wqkv = matmul_lt(hb_all, d_qkv)
    input_grad = d_first + scatter_rep(matmul_rt(d_qkv, w_qkv_r))

    zeros_cols = jnp.zeros((D,), jnp.float32)
    d_bq = lax.dynamic_update_slice_in_dim(zeros_cols, jnp.sum(d_queries, axis=0), r * head_cols, 0)
    d_bv = lax.dynamic_update_slice_in_dim(zeros_cols, jnp.sum(d_values, axis=0), r * head_cols, 0)
    d_biases = jnp.stack([d_bq, d_bv, d_bout, d_bias_one, d_bdown, d_bias_two])
    d_gains = jnp.stack([d_gain_one, d_gain_two])
    d_wout_all = lax.dynamic_update_slice_in_dim(
        jnp.zeros((D, D), jnp.bfloat16), d_wout.astype(jnp.bfloat16), r * head_cols, 0
    )
    d_bup_all = lax.dynamic_update_slice_in_dim(
        jnp.zeros((parts, reps, ff_piece), jnp.float32), d_bup.reshape(parts, 1, ff_piece), r, 1
    )
    grad_parts = (
        d_wqkv.astype(jnp.bfloat16).reshape(parts, -1),
        d_wout_all.reshape(parts, -1),
        d_bup_all.astype(jnp.bfloat16).reshape(parts, -1),
        pack_cols(d_biases.astype(jnp.bfloat16), parts),
        pack_cols(d_gains.astype(jnp.bfloat16), parts),
    )
    g_sizes = [piece.shape[1] for piece in grad_parts]
    grad_pack = jnp.concatenate(grad_parts, axis=1)
    width = grad_pack.shape[1]
    padded = -(-width // 1024) * 1024
    grad_pack = jnp.pad(grad_pack, ((0, 0), (0, padded - width))).reshape(parts, 8, -1)
    received = lax.all_to_all(grad_pack, "shard", 0, 0, tiled=True)
    shares = jnp.sum(received.astype(jnp.float32), axis=0).astype(jnp.bfloat16)
    all_shares = jnp.concatenate([shares.reshape(-1), ffn_share.reshape(-1)])
    joined = lax.all_gather(all_shares, "rep", axis=0, tiled=False).astype(jnp.float32)
    g_sizes = g_sizes + [padded - width, ffn_share.size // 2, ffn_share.size // 2]
    names = ["qkv", "out", "bup", "bias", "gain", "pad", "up", "down"]
    g_offsets = [sum(g_sizes[:i]) for i in range(len(g_sizes) + 1)]
    got = {names[i]: joined[:, g_offsets[i] : g_offsets[i + 1]] for i in range(len(g_sizes))}
    grad_w_qkv = got["qkv"].reshape(reps, k_rows, 3, head_cols).transpose(1, 2, 0, 3).reshape(k_rows, -1)
    grad_w_out = jnp.sum(got["out"], axis=0).reshape(k_rows, D)
    grad_w_up = got["up"].reshape(reps, k_rows, parts, ff_piece).transpose(1, 2, 0, 3).reshape(k_rows, -1)
    grad_w_down = got["down"].reshape(reps * ff_piece, D)
    grad_up_bias = jnp.sum(got["bup"], axis=0)
    grad_biases = jnp.sum(got["bias"], axis=0).reshape(biases.shape[1], -1)
    grad_gains = jnp.sum(got["gain"], axis=0).reshape(norm_gains.shape[1], -1)
    return (
        layer_out[None],
        input_grad[None],
        grad_w_qkv[None],
        grad_w_out[None],
        grad_w_up[None],
        grad_w_down[None],
        grad_biases[None],
        grad_gains[None],
        grad_up_bias[None],
    )


def solution(mesh):
    in_specs = (
        P("shard", "rep", None),
        P("shard", "rep"),
        P("shard", "rep", None),
        P(None, "shard", None),
        P(None, "shard", None),
        P(None, "shard", None),
        P(None, "shard", None),
        P(None, None, "shard"),
        P(None, None, "shard"),
        P(None, "shard"),
    )
    out_specs = (
        P("shard", "rep", None),
        P("shard", "rep", None),
        P(None, "shard", None),
        P(None, "shard", None),
        P(None, "shard", None),
        P(None, "shard", None),
        P(None, None, "shard"),
        P(None, None, "shard"),
        P(None, "shard"),
    )
    return jax.shard_map(local, mesh=mesh, in_specs=in_specs, out_specs=out_specs, check_vma=False)
```

```python
import math

import jax
import jax.numpy as jnp
from jax import lax
from jax.experimental import pallas as pl
from jax.experimental.pallas import tpu as pltpu
from jax.sharding import PartitionSpec as P

D = 1024
HEADS = 16
HEAD_DIM = 64
LAYERS = 1


epsilon = 1e-06


def normalize(residual):
    center = residual - jnp.mean(residual, axis=-1, keepdims=True)
    rstd_val = lax.rsqrt(jnp.mean(center * center, axis=-1, keepdims=True) + epsilon)
    return (center * rstd_val, rstd_val)


def norm_back(grad_out, x_hat, rstd_val, gain_row):
    d_hat = grad_out * gain_row
    return rstd_val * (
        d_hat
        - jnp.mean(d_hat, axis=-1, keepdims=True)
        - x_hat * jnp.mean(d_hat * x_hat, axis=-1, keepdims=True)
    )


def gelu_pair(pre_act):
    normal_cdf = 0.5 * (1.0 + lax.erf(pre_act * (1.0 / math.sqrt(2.0))))
    density = jnp.exp(-0.5 * pre_act * pre_act) * (1.0 / math.sqrt(2.0 * math.pi))
    return (pre_act * normal_cdf, normal_cdf + pre_act * density)


def matmul(first_op, second_op):
    return jnp.dot(first_op, second_op, preferred_element_type=jnp.float32)


def matmul_lt(first_op, second_op):
    return lax.dot_general(
        first_op, second_op, (((0,), (0,)), ((), ())), preferred_element_type=jnp.float32
    )


def matmul_rt(first_op, second_op):
    return lax.dot_general(
        first_op, second_op, (((1,), (1,)), ((), ())), preferred_element_type=jnp.float32
    )


def attention_scores(queries, keys_all, seg_rows, seg_cols):
    scores = jnp.einsum(
        "sqhe,skhe->shqk", queries, keys_all, preferred_element_type=jnp.float32
    ) * (1.0 / math.sqrt(HEAD_DIM))
    allowed = seg_rows[:, None, :, None] == seg_cols[:, None, None, :]
    return (scores, allowed)


def pick(tensor, index, axis):
    return lax.dynamic_index_in_dim(tensor, index, axis=axis, keepdims=False)


def pack_cols(tensor, parts):
    rows = tensor.shape[0]
    return tensor.reshape(rows, parts, -1).transpose(1, 0, 2).reshape(parts, -1)


def unpack_cols(flat, parts, rows):
    return flat.reshape(parts, rows, -1).transpose(1, 0, 2).reshape(rows, -1)


def rep_gather_kernel(x_ref, o_ref, send_sem, recv_sem):
    n = lax.axis_size("rep")
    me = lax.axis_index("rep")
    rows = x_ref.shape[0]
    o_ref[pl.ds(me * rows, rows), :] = x_ref[...]
    barrier = pltpu.get_barrier_semaphore()
    for k in range(1, n):
        pl.semaphore_signal(
            barrier, inc=1, device_id={"rep": lax.rem(me + k, n)}, device_id_type=pl.DeviceIdType.MESH
        )
    pl.semaphore_wait(barrier, n - 1)
    copies = []
    for k in range(1, n):
        copy = pltpu.make_async_remote_copy(
            src_ref=x_ref,
            dst_ref=o_ref.at[pl.ds(me * rows, rows)],
            send_sem=send_sem.at[k - 1],
            recv_sem=recv_sem.at[k - 1],
            device_id={"rep": lax.rem(me + k, n)},
            device_id_type=pl.DeviceIdType.MESH,
        )
        copy.start()
        copies.append(copy)
    for copy in copies:
        copy.wait()


def gather_rep(tensor, cid=1):
    n = lax.axis_size("rep")
    rows, cols = tensor.shape
    return pl.pallas_call(
        rep_gather_kernel,
        out_shape=jax.ShapeDtypeStruct((n * rows, cols), tensor.dtype),
        in_specs=[pl.BlockSpec(memory_space=pltpu.VMEM)],
        out_specs=pl.BlockSpec(memory_space=pltpu.VMEM),
        scratch_shapes=[pltpu.SemaphoreType.DMA((n - 1,)), pltpu.SemaphoreType.DMA((n - 1,))],
        compiler_params=pltpu.CompilerParams(collective_id=cid, has_side_effects=True),
    )(tensor)


def scatter_rep(tensor):
    return lax.psum_scatter(tensor, "rep", scatter_dimension=0, tiled=True)


def local(inputs, segment_ids, cotangent, w_qkv, w_out, w_up, w_down, biases, norm_gains, up_bias):
    parts = lax.axis_size("shard")
    reps = lax.axis_size("rep")
    r = lax.axis_index("rep")
    head_cols = D // reps
    heads_here = HEADS // reps
    ff_all = w_up.shape[2]
    ff_chunk = ff_all // parts
    ff_piece = ff_chunk // reps
    k_rows = D // parts

    qkv_piece = pick(w_qkv[0].reshape(k_rows, 3, reps, head_cols), r, 2).reshape(k_rows, -1)
    out_piece = w_out[0]
    up_piece = pick(w_up[0].reshape(k_rows, parts, reps, ff_piece), r, 2).reshape(k_rows, -1)
    down_piece = pick(w_down[0].reshape(reps, ff_piece, D), r, 0)
    upb_piece = pick(up_bias[0].reshape(reps, ff_piece), r, 0)
    pieces = (qkv_piece, out_piece, up_piece, down_piece, upb_piece, biases[0], norm_gains[0])
    sizes = [piece.size for piece in pieces]
    offsets = [sum(sizes[:i]) for i in range(len(sizes) + 1)]
    packed = jnp.concatenate([piece.reshape(-1) for piece in pieces])
    packed = jnp.pad(packed, (0, -(-packed.size // 1024) * 1024 - packed.size))
    gathered = lax.all_gather(packed, "shard", axis=0, tiled=False)
    got = [gathered[:, offsets[i] : offsets[i + 1]] for i in range(len(sizes))]
    w_qkv_r = got[0].reshape(D, 3 * head_cols)
    w_out_all = got[1].reshape(D, D)
    w_out_r = lax.dynamic_slice_in_dim(w_out_all, r * head_cols, head_cols, axis=0)
    w_up_r = got[2].reshape(D, -1)
    w_down_r = got[3].reshape(-1, D)
    up_bias_r = got[4].reshape(-1)
    bias_all = unpack_cols(got[5], parts, biases.shape[1])
    gain_all = unpack_cols(got[6], parts, norm_gains.shape[1])
    bias_q = lax.dynamic_slice_in_dim(bias_all[0], r * head_cols, head_cols)
    bias_v = lax.dynamic_slice_in_dim(bias_all[1], r * head_cols, head_cols)

    rows_f32 = inputs[0]
    own = rows_f32.shape[0]
    rows_bf = rows_f32.astype(jnp.bfloat16)
    seg_tag = jnp.broadcast_to(segment_ids[0].astype(jnp.bfloat16)[:, None], (own, 128))
    hb_seg = gather_rep(jnp.concatenate([rows_bf, seg_tag], axis=1), cid=0)
    hb_all = hb_seg[:, :D]
    seg_all = hb_seg[:, D]
    qkv_rows = matmul(hb_all, w_qkv_r)
    queries = (qkv_rows[:, :head_cols] + bias_q).astype(jnp.bfloat16).reshape(1, -1, heads_here, HEAD_DIM)
    keys_all = qkv_rows[:, head_cols : 2 * head_cols].astype(jnp.bfloat16).reshape(1, -1, heads_here, HEAD_DIM)
    values_all = (
        (qkv_rows[:, 2 * head_cols :] + bias_v).astype(jnp.bfloat16).reshape(1, -1, heads_here, HEAD_DIM)
    )
    seg_rows = seg_all[None]
    scores, allowed = attention_scores(queries, keys_all, seg_rows, seg_rows)
    expo_all = jnp.where(allowed, jnp.exp(scores), 0.0)
    row_total = jnp.sum(expo_all, axis=-1, keepdims=True)
    log_total = jnp.log(row_total)
    attn_probs = (expo_all / row_total).astype(jnp.bfloat16)
    context = (
        jnp.einsum("shqk,skhe->sqhe", attn_probs, values_all, preferred_element_type=jnp.float32)
        .astype(jnp.bfloat16)
        .reshape(-1, head_cols)
    )
    first_sum = rows_f32 + scatter_rep(matmul(context, w_out_r)) + bias_all[2]
    norm_one, rstd_one = normalize(first_sum)
    mid_norm = norm_one * gain_all[0] + bias_all[3]
    mid_b = mid_norm.astype(jnp.bfloat16)
    mid_all = gather_rep(mid_b)
    pre_act = matmul(mid_all, w_up_r) + up_bias_r
    act_f32, gelu_slope = gelu_pair(pre_act)
    act_b = act_f32.astype(jnp.bfloat16)
    second_sum = mid_norm + scatter_rep(matmul(act_b, w_down_r)) + bias_all[4]
    norm_two, rstd_two = normalize(second_sum)
    layer_out = norm_two * gain_all[1] + bias_all[5]

    grad_rows = cotangent[0]
    d_gain_two = jnp.sum(grad_rows * norm_two, axis=0)
    d_bias_two = jnp.sum(grad_rows, axis=0)
    d_second = norm_back(grad_rows, norm_two, rstd_two, gain_all[1])
    d_bdown = jnp.sum(d_second, axis=0)
    d_second_all = gather_rep(d_second.astype(jnp.bfloat16))
    d_wdown = matmul_lt(act_b, d_second_all)
    d_pre = matmul_rt(d_second_all, w_down_r) * gelu_slope
    d_bup = jnp.sum(d_pre, axis=0)
    d_pre_b = d_pre.astype(jnp.bfloat16)
    d_wup = matmul_lt(mid_all, d_pre_b)
    ffn_pack = jnp.concatenate(
        [d_wup.astype(jnp.bfloat16).reshape(parts, -1), d_wdown.astype(jnp.bfloat16).reshape(parts, -1)],
        axis=1,
    ).reshape(parts, 8, -1)
    ffn_recv = lax.all_to_all(ffn_pack, "shard", 0, 0, tiled=True)
    ffn_share = jnp.sum(ffn_recv.astype(jnp.float32), axis=0).astype(jnp.bfloat16)
    d_mid = d_second + scatter_rep(matmul_rt(d_pre_b, w_up_r))
    d_gain_one = jnp.sum(d_mid * norm_one, axis=0)
    d_bias_one = jnp.sum(d_mid, axis=0)
    d_first = norm_back(d_mid, norm_one, rstd_one, gain_all[0])
    d_bout = jnp.sum(d_first, axis=0)
    d_first_all = gather_rep(d_first.astype(jnp.bfloat16))
    d_wout = matmul_lt(context, d_first_all)
    d_context = (
        matmul_rt(d_first_all, w_out_r).astype(jnp.bfloat16).reshape(1, -1, heads_here, HEAD_DIM)
    )
    probs_again = jnp.where(allowed, jnp.exp(scores - log_total), 0.0)
    d_probs = jnp.einsum(
        "sqhe,skhe->shqk", d_context, values_all, preferred_element_type=jnp.float32
    )
    d_scores = (
        probs_again
        * (d_probs - jnp.sum(probs_again * d_probs, axis=-1, keepdims=True))
        * (1.0 / math.sqrt(HEAD_DIM))
    ).astype(jnp.bfloat16)
    d_queries = jnp.einsum(
        "shqk,skhe->sqhe", d_scores, keys_all, preferred_element_type=jnp.float32
    ).reshape(-1, head_cols)
    d_keys = jnp.einsum(
        "shqk,sqhe->skhe", d_scores, queries, preferred_element_type=jnp.float32
    ).reshape(-1, head_cols)
    d_values = jnp.einsum(
        "shqk,sqhe->skhe",
        probs_again.astype(jnp.bfloat16),
        d_context,
        preferred_element_type=jnp.float32,
    ).reshape(-1, head_cols)
    d_qkv = jnp.concatenate([d_queries, d_keys, d_values], axis=-1).astype(jnp.bfloat16)
    d_wqkv = matmul_lt(hb_all, d_qkv)
    input_grad = d_first + scatter_rep(matmul_rt(d_qkv, w_qkv_r))

    zeros_cols = jnp.zeros((D,), jnp.float32)
    d_bq = lax.dynamic_update_slice_in_dim(zeros_cols, jnp.sum(d_queries, axis=0), r * head_cols, 0)
    d_bv = lax.dynamic_update_slice_in_dim(zeros_cols, jnp.sum(d_values, axis=0), r * head_cols, 0)
    d_biases = jnp.stack([d_bq, d_bv, d_bout, d_bias_one, d_bdown, d_bias_two])
    d_gains = jnp.stack([d_gain_one, d_gain_two])
    d_wout_all = lax.dynamic_update_slice_in_dim(
        jnp.zeros((D, D), jnp.bfloat16), d_wout.astype(jnp.bfloat16), r * head_cols, 0
    )
    d_bup_all = lax.dynamic_update_slice_in_dim(
        jnp.zeros((parts, reps, ff_piece), jnp.float32), d_bup.reshape(parts, 1, ff_piece), r, 1
    )
    grad_parts = (
        d_wqkv.astype(jnp.bfloat16).reshape(parts, -1),
        d_wout_all.reshape(parts, -1),
        d_bup_all.astype(jnp.bfloat16).reshape(parts, -1),
        pack_cols(d_biases.astype(jnp.bfloat16), parts),
        pack_cols(d_gains.astype(jnp.bfloat16), parts),
    )
    g_sizes = [piece.shape[1] for piece in grad_parts]
    grad_pack = jnp.concatenate(grad_parts, axis=1)
    width = grad_pack.shape[1]
    padded = -(-width // 1024) * 1024
    grad_pack = jnp.pad(grad_pack, ((0, 0), (0, padded - width))).reshape(parts, 8, -1)
    received = lax.all_to_all(grad_pack, "shard", 0, 0, tiled=True)
    shares = jnp.sum(received.astype(jnp.float32), axis=0).astype(jnp.bfloat16)
    all_shares = jnp.concatenate([shares.reshape(-1), ffn_share.reshape(-1)])
    joined = gather_rep(all_shares.reshape(-1, 128), cid=2).reshape(reps, -1).astype(jnp.float32)
    g_sizes = g_sizes + [padded - width, ffn_share.size // 2, ffn_share.size // 2]
    names = ["qkv", "out", "bup", "bias", "gain", "pad", "up", "down"]
    g_offsets = [sum(g_sizes[:i]) for i in range(len(g_sizes) + 1)]
    got = {names[i]: joined[:, g_offsets[i] : g_offsets[i + 1]] for i in range(len(g_sizes))}
    grad_w_qkv = got["qkv"].reshape(reps, k_rows, 3, head_cols).transpose(1, 2, 0, 3).reshape(k_rows, -1)
    grad_w_out = jnp.sum(got["out"], axis=0).reshape(k_rows, D)
    grad_w_up = got["up"].reshape(reps, k_rows, parts, ff_piece).transpose(1, 2, 0, 3).reshape(k_rows, -1)
    grad_w_down = got["down"].reshape(reps * ff_piece, D)
    grad_up_bias = jnp.sum(got["bup"], axis=0)
    grad_biases = jnp.sum(got["bias"], axis=0).reshape(biases.shape[1], -1)
    grad_gains = jnp.sum(got["gain"], axis=0).reshape(norm_gains.shape[1], -1)
    return (
        layer_out[None],
        input_grad[None],
        grad_w_qkv[None],
        grad_w_out[None],
        grad_w_up[None],
        grad_w_down[None],
        grad_biases[None],
        grad_gains[None],
        grad_up_bias[None],
    )


def solution(mesh):
    in_specs = (
        P("shard", "rep", None),
        P("shard", "rep"),
        P("shard", "rep", None),
        P(None, "shard", None),
        P(None, "shard", None),
        P(None, "shard", None),
        P(None, "shard", None),
        P(None, None, "shard"),
        P(None, None, "shard"),
        P(None, "shard"),
    )
    out_specs = (
        P("shard", "rep", None),
        P("shard", "rep", None),
        P(None, "shard", None),
        P(None, "shard", None),
        P(None, "shard", None),
        P(None, "shard", None),
        P(None, None, "shard"),
        P(None, None, "shard"),
        P(None, "shard"),
    )
    return jax.shard_map(local, mesh=mesh, in_specs=in_specs, out_specs=out_specs, check_vma=False)
```

```python
import math

import jax
import jax.numpy as jnp
from jax import lax
from jax.experimental import pallas as pl
from jax.experimental.pallas import tpu as pltpu
from jax.sharding import PartitionSpec as P

D = 1024
HEADS = 16
HEAD_DIM = 64
LAYERS = 1


epsilon = 1e-06


def normalize(residual):
    center = residual - jnp.mean(residual, axis=-1, keepdims=True)
    rstd_val = lax.rsqrt(jnp.mean(center * center, axis=-1, keepdims=True) + epsilon)
    return (center * rstd_val, rstd_val)


def norm_back(grad_out, x_hat, rstd_val, gain_row):
    d_hat = grad_out * gain_row
    return rstd_val * (
        d_hat
        - jnp.mean(d_hat, axis=-1, keepdims=True)
        - x_hat * jnp.mean(d_hat * x_hat, axis=-1, keepdims=True)
    )


def gelu_pair(pre_act):
    normal_cdf = 0.5 * (1.0 + lax.erf(pre_act * (1.0 / math.sqrt(2.0))))
    density = jnp.exp(-0.5 * pre_act * pre_act) * (1.0 / math.sqrt(2.0 * math.pi))
    return (pre_act * normal_cdf, normal_cdf + pre_act * density)


def matmul(first_op, second_op):
    return jnp.dot(first_op, second_op, preferred_element_type=jnp.float32)


def matmul_lt(first_op, second_op):
    return lax.dot_general(
        first_op, second_op, (((0,), (0,)), ((), ())), preferred_element_type=jnp.float32
    )


def matmul_rt(first_op, second_op):
    return lax.dot_general(
        first_op, second_op, (((1,), (1,)), ((), ())), preferred_element_type=jnp.float32
    )


def attention_scores(queries, keys_all, seg_rows, seg_cols):
    scores = jnp.einsum(
        "sqhe,skhe->shqk", queries, keys_all, preferred_element_type=jnp.float32
    ) * (1.0 / math.sqrt(HEAD_DIM))
    allowed = seg_rows[:, None, :, None] == seg_cols[:, None, None, :]
    return (scores, allowed)


def pick(tensor, index, axis):
    return lax.dynamic_index_in_dim(tensor, index, axis=axis, keepdims=False)


def pack_cols(tensor, parts):
    rows = tensor.shape[0]
    return tensor.reshape(rows, parts, -1).transpose(1, 0, 2).reshape(parts, -1)


def unpack_cols(flat, parts, rows):
    return flat.reshape(parts, rows, -1).transpose(1, 0, 2).reshape(rows, -1)


def rep_gather_kernel(x_ref, o_ref, send_sem, recv_sem):
    n = lax.axis_size("rep")
    me = lax.axis_index("rep")
    rows = x_ref.shape[0]
    o_ref[pl.ds(me * rows, rows), :] = x_ref[...]
    barrier = pltpu.get_barrier_semaphore()
    for k in range(1, n):
        pl.semaphore_signal(
            barrier, inc=1, device_id={"rep": lax.rem(me + k, n)}, device_id_type=pl.DeviceIdType.MESH
        )
    pl.semaphore_wait(barrier, n - 1)
    copies = []
    for k in range(1, n):
        copy = pltpu.make_async_remote_copy(
            src_ref=x_ref,
            dst_ref=o_ref.at[pl.ds(me * rows, rows)],
            send_sem=send_sem.at[k - 1],
            recv_sem=recv_sem.at[k - 1],
            device_id={"rep": lax.rem(me + k, n)},
            device_id_type=pl.DeviceIdType.MESH,
        )
        copy.start()
        copies.append(copy)
    for copy in copies:
        copy.wait()


def gather_rep(tensor, cid=1):
    n = lax.axis_size("rep")
    rows, cols = tensor.shape
    return pl.pallas_call(
        rep_gather_kernel,
        out_shape=jax.ShapeDtypeStruct((n * rows, cols), tensor.dtype),
        in_specs=[pl.BlockSpec(memory_space=pltpu.VMEM)],
        out_specs=pl.BlockSpec(memory_space=pltpu.VMEM),
        scratch_shapes=[pltpu.SemaphoreType.DMA((n - 1,)), pltpu.SemaphoreType.DMA((n - 1,))],
        compiler_params=pltpu.CompilerParams(collective_id=cid, has_side_effects=True),
    )(tensor)


def scatter_rep(tensor):
    return lax.psum_scatter(tensor, "rep", scatter_dimension=0, tiled=True)


def local(inputs, segment_ids, cotangent, w_qkv, w_out, w_up, w_down, biases, norm_gains, up_bias):
    parts = lax.axis_size("shard")
    reps = lax.axis_size("rep")
    r = lax.axis_index("rep")
    head_cols = D // reps
    heads_here = HEADS // reps
    ff_all = w_up.shape[2]
    ff_chunk = ff_all // parts
    ff_piece = ff_chunk // reps
    k_rows = D // parts

    qkv_piece = pick(w_qkv[0].reshape(k_rows, 3, reps, head_cols), r, 2).reshape(k_rows, -1)
    out_piece = w_out[0]
    up_piece = pick(w_up[0].reshape(k_rows, parts, reps, ff_piece), r, 2).reshape(k_rows, -1)
    down_piece = pick(w_down[0].reshape(reps, ff_piece, D), r, 0)
    upb_piece = pick(up_bias[0].reshape(reps, ff_piece), r, 0)
    pieces = (qkv_piece, out_piece, up_piece, down_piece, upb_piece, biases[0], norm_gains[0])
    sizes = [piece.size for piece in pieces]
    offsets = [sum(sizes[:i]) for i in range(len(sizes) + 1)]
    packed = jnp.concatenate([piece.reshape(-1) for piece in pieces])
    packed = jnp.pad(packed, (0, -(-packed.size // 1024) * 1024 - packed.size))
    gathered = lax.all_gather(packed, "shard", axis=0, tiled=False)
    got = [gathered[:, offsets[i] : offsets[i + 1]] for i in range(len(sizes))]
    w_qkv_r = got[0].reshape(D, 3 * head_cols)
    w_out_all = got[1].reshape(D, D)
    w_out_r = lax.dynamic_slice_in_dim(w_out_all, r * head_cols, head_cols, axis=0)
    w_up_r = got[2].reshape(D, -1)
    w_down_r = got[3].reshape(-1, D)
    up_bias_r = got[4].reshape(-1)
    bias_all = unpack_cols(got[5], parts, biases.shape[1])
    gain_all = unpack_cols(got[6], parts, norm_gains.shape[1])
    bias_q = lax.dynamic_slice_in_dim(bias_all[0], r * head_cols, head_cols)
    bias_v = lax.dynamic_slice_in_dim(bias_all[1], r * head_cols, head_cols)

    rows_f32 = inputs[0]
    own = rows_f32.shape[0]
    rows_bf = rows_f32.astype(jnp.bfloat16)
    seg_tag = jnp.broadcast_to(segment_ids[0].astype(jnp.bfloat16)[:, None], (own, 128))
    hb_seg = gather_rep(jnp.concatenate([rows_bf, seg_tag], axis=1), cid=0)
    hb_all = hb_seg[:, :D]
    seg_all = hb_seg[:, D]
    qkv_rows = matmul(hb_all, w_qkv_r)
    queries = (qkv_rows[:, :head_cols] + bias_q).astype(jnp.bfloat16).reshape(1, -1, heads_here, HEAD_DIM)
    keys_all = qkv_rows[:, head_cols : 2 * head_cols].astype(jnp.bfloat16).reshape(1, -1, heads_here, HEAD_DIM)
    values_all = (
        (qkv_rows[:, 2 * head_cols :] + bias_v).astype(jnp.bfloat16).reshape(1, -1, heads_here, HEAD_DIM)
    )
    seg_rows = seg_all[None]
    scores, allowed = attention_scores(queries, keys_all, seg_rows, seg_rows)
    expo_all = jnp.where(allowed, jnp.exp(scores), 0.0)
    row_total = jnp.sum(expo_all, axis=-1, keepdims=True)
    log_total = jnp.log(row_total)
    attn_probs = (expo_all / row_total).astype(jnp.bfloat16)
    context = (
        jnp.einsum("shqk,skhe->sqhe", attn_probs, values_all, preferred_element_type=jnp.float32)
        .astype(jnp.bfloat16)
        .reshape(-1, head_cols)
    )
    first_sum = rows_f32 + scatter_rep(matmul(context, w_out_r)) + bias_all[2]
    context_stack = gather_rep(context, cid=2).reshape(reps, -1, head_cols)
    norm_one, rstd_one = normalize(first_sum)
    mid_norm = norm_one * gain_all[0] + bias_all[3]
    mid_b = mid_norm.astype(jnp.bfloat16)
    mid_all = gather_rep(mid_b)
    pre_act = matmul(mid_all, w_up_r) + up_bias_r
    act_f32, gelu_slope = gelu_pair(pre_act)
    act_b = act_f32.astype(jnp.bfloat16)
    second_sum = mid_norm + scatter_rep(matmul(act_b, w_down_r)) + bias_all[4]
    norm_two, rstd_two = normalize(second_sum)
    layer_out = norm_two * gain_all[1] + bias_all[5]

    grad_rows = cotangent[0]
    d_gain_two = jnp.sum(grad_rows * norm_two, axis=0)
    d_bias_two = jnp.sum(grad_rows, axis=0)
    d_second = norm_back(grad_rows, norm_two, rstd_two, gain_all[1])
    d_bdown = jnp.sum(d_second, axis=0)
    d_second_all = gather_rep(d_second.astype(jnp.bfloat16))
    d_wdown = matmul_lt(act_b, d_second_all)
    d_pre = matmul_rt(d_second_all, w_down_r) * gelu_slope
    d_bup = jnp.sum(d_pre, axis=0)
    d_pre_b = d_pre.astype(jnp.bfloat16)
    d_wup = matmul_lt(mid_all, d_pre_b)
    ffn_pack = jnp.concatenate(
        [d_wup.astype(jnp.bfloat16).reshape(parts, -1), d_wdown.astype(jnp.bfloat16).reshape(parts, -1)],
        axis=1,
    ).reshape(parts, 8, -1)
    ffn_recv = lax.all_to_all(ffn_pack, "shard", 0, 0, tiled=True)
    ffn_share = jnp.sum(ffn_recv.astype(jnp.float32), axis=0).astype(jnp.bfloat16)
    d_mid = d_second + scatter_rep(matmul_rt(d_pre_b, w_up_r))
    d_gain_one = jnp.sum(d_mid * norm_one, axis=0)
    d_bias_one = jnp.sum(d_mid, axis=0)
    d_first = norm_back(d_mid, norm_one, rstd_one, gain_all[0])
    d_bout = jnp.sum(d_first, axis=0)
    d_first_all = gather_rep(d_first.astype(jnp.bfloat16))
    d_first_cols = lax.dynamic_slice_in_dim(d_first_all, r * head_cols, head_cols, axis=1)
    d_wout_cols = jnp.einsum(
        "utc,tk->uck", context_stack, d_first_cols, preferred_element_type=jnp.float32
    ).reshape(D, head_cols)
    d_context = (
        matmul_rt(d_first_all, w_out_r).astype(jnp.bfloat16).reshape(1, -1, heads_here, HEAD_DIM)
    )
    probs_again = jnp.where(allowed, jnp.exp(scores - log_total), 0.0)
    d_probs = jnp.einsum(
        "sqhe,skhe->shqk", d_context, values_all, preferred_element_type=jnp.float32
    )
    d_scores = (
        probs_again
        * (d_probs - jnp.sum(probs_again * d_probs, axis=-1, keepdims=True))
        * (1.0 / math.sqrt(HEAD_DIM))
    ).astype(jnp.bfloat16)
    d_queries = jnp.einsum(
        "shqk,skhe->sqhe", d_scores, keys_all, preferred_element_type=jnp.float32
    ).reshape(-1, head_cols)
    d_keys = jnp.einsum(
        "shqk,sqhe->skhe", d_scores, queries, preferred_element_type=jnp.float32
    ).reshape(-1, head_cols)
    d_values = jnp.einsum(
        "shqk,sqhe->skhe",
        probs_again.astype(jnp.bfloat16),
        d_context,
        preferred_element_type=jnp.float32,
    ).reshape(-1, head_cols)
    d_qkv = jnp.concatenate([d_queries, d_keys, d_values], axis=-1).astype(jnp.bfloat16)
    d_wqkv = matmul_lt(hb_all, d_qkv)
    input_grad = d_first + scatter_rep(matmul_rt(d_qkv, w_qkv_r))

    zeros_cols = jnp.zeros((D,), jnp.float32)
    d_bq = lax.dynamic_update_slice_in_dim(zeros_cols, jnp.sum(d_queries, axis=0), r * head_cols, 0)
    d_bv = lax.dynamic_update_slice_in_dim(zeros_cols, jnp.sum(d_values, axis=0), r * head_cols, 0)
    d_biases = jnp.stack([d_bq, d_bv, d_bout, d_bias_one, d_bdown, d_bias_two])
    d_gains = jnp.stack([d_gain_one, d_gain_two])
    d_bup_all = lax.dynamic_update_slice_in_dim(
        jnp.zeros((parts, reps, ff_piece), jnp.float32), d_bup.reshape(parts, 1, ff_piece), r, 1
    )
    grad_parts = (
        d_wqkv.astype(jnp.bfloat16).reshape(parts, -1),
        d_wout_cols.astype(jnp.bfloat16).reshape(parts, -1),
        d_bup_all.astype(jnp.bfloat16).reshape(parts, -1),
        pack_cols(d_biases.astype(jnp.bfloat16), parts),
        pack_cols(d_gains.astype(jnp.bfloat16), parts),
    )
    g_sizes = [piece.shape[1] for piece in grad_parts]
    grad_pack = jnp.concatenate(grad_parts, axis=1)
    width = grad_pack.shape[1]
    padded = -(-width // 1024) * 1024
    grad_pack = jnp.pad(grad_pack, ((0, 0), (0, padded - width))).reshape(parts, 8, -1)
    received = lax.all_to_all(grad_pack, "shard", 0, 0, tiled=True)
    shares = jnp.sum(received.astype(jnp.float32), axis=0).astype(jnp.bfloat16)
    all_shares = jnp.concatenate([shares.reshape(-1), ffn_share.reshape(-1)])
    joined = lax.all_gather(all_shares, "rep", axis=0, tiled=False).astype(jnp.float32)
    g_sizes = g_sizes + [padded - width, ffn_share.size // 2, ffn_share.size // 2]
    names = ["qkv", "out", "bup", "bias", "gain", "pad", "up", "down"]
    g_offsets = [sum(g_sizes[:i]) for i in range(len(g_sizes) + 1)]
    got = {names[i]: joined[:, g_offsets[i] : g_offsets[i + 1]] for i in range(len(g_sizes))}
    grad_w_qkv = got["qkv"].reshape(reps, k_rows, 3, head_cols).transpose(1, 2, 0, 3).reshape(k_rows, -1)
    grad_w_out = got["out"].reshape(reps, k_rows, head_cols).transpose(1, 0, 2).reshape(k_rows, D)
    grad_w_up = got["up"].reshape(reps, k_rows, parts, ff_piece).transpose(1, 2, 0, 3).reshape(k_rows, -1)
    grad_w_down = got["down"].reshape(reps * ff_piece, D)
    grad_up_bias = jnp.sum(got["bup"], axis=0)
    grad_biases = jnp.sum(got["bias"], axis=0).reshape(biases.shape[1], -1)
    grad_gains = jnp.sum(got["gain"], axis=0).reshape(norm_gains.shape[1], -1)
    return (
        layer_out[None],
        input_grad[None],
        grad_w_qkv[None],
        grad_w_out[None],
        grad_w_up[None],
        grad_w_down[None],
        grad_biases[None],
        grad_gains[None],
        grad_up_bias[None],
    )


def solution(mesh):
    in_specs = (
        P("shard", "rep", None),
        P("shard", "rep"),
        P("shard", "rep", None),
        P(None, "shard", None),
        P(None, "shard", None),
        P(None, "shard", None),
        P(None, "shard", None),
        P(None, None, "shard"),
        P(None, None, "shard"),
        P(None, "shard"),
    )
    out_specs = (
        P("shard", "rep", None),
        P("shard", "rep", None),
        P(None, "shard", None),
        P(None, "shard", None),
        P(None, "shard", None),
        P(None, "shard", None),
        P(None, None, "shard"),
        P(None, None, "shard"),
        P(None, "shard"),
    )
    return jax.shard_map(local, mesh=mesh, in_specs=in_specs, out_specs=out_specs, check_vma=False)
```

```python
import math

import jax
import jax.numpy as jnp
from jax import lax
from jax.experimental import pallas as pl
from jax.experimental.pallas import tpu as pltpu
from jax.sharding import PartitionSpec as P

D = 1024
HEADS = 16
HEAD_DIM = 64
LAYERS = 1


epsilon = 1e-06


def normalize(residual):
    center = residual - jnp.mean(residual, axis=-1, keepdims=True)
    rstd_val = lax.rsqrt(jnp.mean(center * center, axis=-1, keepdims=True) + epsilon)
    return (center * rstd_val, rstd_val)


def norm_back(grad_out, x_hat, rstd_val, gain_row):
    d_hat = grad_out * gain_row
    return rstd_val * (
        d_hat
        - jnp.mean(d_hat, axis=-1, keepdims=True)
        - x_hat * jnp.mean(d_hat * x_hat, axis=-1, keepdims=True)
    )


def gelu_pair(pre_act):
    normal_cdf = 0.5 * (1.0 + lax.erf(pre_act * (1.0 / math.sqrt(2.0))))
    density = jnp.exp(-0.5 * pre_act * pre_act) * (1.0 / math.sqrt(2.0 * math.pi))
    return (pre_act * normal_cdf, normal_cdf + pre_act * density)


def matmul(first_op, second_op):
    return jnp.dot(first_op, second_op, preferred_element_type=jnp.float32)


def matmul_lt(first_op, second_op):
    return lax.dot_general(
        first_op, second_op, (((0,), (0,)), ((), ())), preferred_element_type=jnp.float32
    )


def matmul_rt(first_op, second_op):
    return lax.dot_general(
        first_op, second_op, (((1,), (1,)), ((), ())), preferred_element_type=jnp.float32
    )


def attention_scores(queries, keys_all, seg_rows, seg_cols):
    scores = jnp.einsum(
        "sqhe,skhe->shqk", queries, keys_all, preferred_element_type=jnp.float32
    ) * (1.0 / math.sqrt(HEAD_DIM))
    allowed = seg_rows[:, None, :, None] == seg_cols[:, None, None, :]
    return (scores, allowed)


def pick(tensor, index, axis):
    return lax.dynamic_index_in_dim(tensor, index, axis=axis, keepdims=False)


def pack_cols(tensor, parts):
    rows = tensor.shape[0]
    return tensor.reshape(rows, parts, -1).transpose(1, 0, 2).reshape(parts, -1)


def unpack_cols(flat, parts, rows):
    return flat.reshape(parts, rows, -1).transpose(1, 0, 2).reshape(rows, -1)


def rep_gather_kernel(x_ref, o_ref, send_sem, recv_sem):
    n = lax.axis_size("rep")
    me = lax.axis_index("rep")
    rows = x_ref.shape[0]
    o_ref[pl.ds(me * rows, rows), :] = x_ref[...]
    barrier = pltpu.get_barrier_semaphore()
    for k in range(1, n):
        pl.semaphore_signal(
            barrier, inc=1, device_id={"rep": lax.rem(me + k, n)}, device_id_type=pl.DeviceIdType.MESH
        )
    pl.semaphore_wait(barrier, n - 1)
    copies = []
    for k in range(1, n):
        copy = pltpu.make_async_remote_copy(
            src_ref=x_ref,
            dst_ref=o_ref.at[pl.ds(me * rows, rows)],
            send_sem=send_sem.at[k - 1],
            recv_sem=recv_sem.at[k - 1],
            device_id={"rep": lax.rem(me + k, n)},
            device_id_type=pl.DeviceIdType.MESH,
        )
        copy.start()
        copies.append(copy)
    for copy in copies:
        copy.wait()


def gather_rep(tensor, cid=1):
    n = lax.axis_size("rep")
    rows, cols = tensor.shape
    return pl.pallas_call(
        rep_gather_kernel,
        out_shape=jax.ShapeDtypeStruct((n * rows, cols), tensor.dtype),
        in_specs=[pl.BlockSpec(memory_space=pltpu.VMEM)],
        out_specs=pl.BlockSpec(memory_space=pltpu.VMEM),
        scratch_shapes=[pltpu.SemaphoreType.DMA((n - 1,)), pltpu.SemaphoreType.DMA((n - 1,))],
        compiler_params=pltpu.CompilerParams(collective_id=cid, has_side_effects=True),
    )(tensor)


def scatter_rep(tensor):
    return lax.psum_scatter(tensor, "rep", scatter_dimension=0, tiled=True)


def local(inputs, segment_ids, cotangent, w_qkv, w_out, w_up, w_down, biases, norm_gains, up_bias):
    parts = lax.axis_size("shard")
    reps = lax.axis_size("rep")
    r = lax.axis_index("rep")
    head_cols = D // reps
    heads_here = HEADS // reps
    ff_all = w_up.shape[2]
    ff_chunk = ff_all // parts
    ff_piece = ff_chunk // reps
    k_rows = D // parts

    qkv_piece = pick(w_qkv[0].reshape(k_rows, 3, reps, head_cols), r, 2).reshape(k_rows, -1)
    out_piece = w_out[0]
    up_piece = pick(w_up[0].reshape(k_rows, parts, reps, ff_piece), r, 2).reshape(k_rows, -1)
    down_piece = pick(w_down[0].reshape(reps, ff_piece, D), r, 0)
    upb_piece = pick(up_bias[0].reshape(reps, ff_piece), r, 0)
    first = (qkv_piece, out_piece, biases[0], norm_gains[0])
    second = (up_piece, down_piece, upb_piece)
    got = []
    for group in (first, second):
        sizes = [piece.size for piece in group]
        offsets = [sum(sizes[:i]) for i in range(len(sizes) + 1)]
        packed = jnp.concatenate([piece.reshape(-1) for piece in group])
        packed = jnp.pad(packed, (0, -(-packed.size // 1024) * 1024 - packed.size))
        gathered = lax.all_gather(packed, "shard", axis=0, tiled=False)
        got += [gathered[:, offsets[i] : offsets[i + 1]] for i in range(len(sizes))]
    w_qkv_r = got[0].reshape(D, 3 * head_cols)
    w_out_all = got[1].reshape(D, D)
    w_out_r = lax.dynamic_slice_in_dim(w_out_all, r * head_cols, head_cols, axis=0)
    bias_all = unpack_cols(got[2], parts, biases.shape[1])
    gain_all = unpack_cols(got[3], parts, norm_gains.shape[1])
    w_up_r = got[4].reshape(D, -1)
    w_down_r = got[5].reshape(-1, D)
    up_bias_r = got[6].reshape(-1)
    bias_q = lax.dynamic_slice_in_dim(bias_all[0], r * head_cols, head_cols)
    bias_v = lax.dynamic_slice_in_dim(bias_all[1], r * head_cols, head_cols)

    rows_f32 = inputs[0]
    own = rows_f32.shape[0]
    rows_bf = rows_f32.astype(jnp.bfloat16)
    seg_tag = jnp.broadcast_to(segment_ids[0].astype(jnp.bfloat16)[:, None], (own, 128))
    hb_seg = gather_rep(jnp.concatenate([rows_bf, seg_tag], axis=1), cid=0)
    hb_all = hb_seg[:, :D]
    seg_all = hb_seg[:, D]
    qkv_rows = matmul(hb_all, w_qkv_r)
    queries = (qkv_rows[:, :head_cols] + bias_q).astype(jnp.bfloat16).reshape(1, -1, heads_here, HEAD_DIM)
    keys_all = qkv_rows[:, head_cols : 2 * head_cols].astype(jnp.bfloat16).reshape(1, -1, heads_here, HEAD_DIM)
    values_all = (
        (qkv_rows[:, 2 * head_cols :] + bias_v).astype(jnp.bfloat16).reshape(1, -1, heads_here, HEAD_DIM)
    )
    seg_rows = seg_all[None]
    scores, allowed = attention_scores(queries, keys_all, seg_rows, seg_rows)
    expo_all = jnp.where(allowed, jnp.exp(scores), 0.0)
    row_total = jnp.sum(expo_all, axis=-1, keepdims=True)
    log_total = jnp.log(row_total)
    attn_probs = (expo_all / row_total).astype(jnp.bfloat16)
    context = (
        jnp.einsum("shqk,skhe->sqhe", attn_probs, values_all, preferred_element_type=jnp.float32)
        .astype(jnp.bfloat16)
        .reshape(-1, head_cols)
    )
    first_sum = rows_f32 + scatter_rep(matmul(context, w_out_r)) + bias_all[2]
    context_stack = gather_rep(context, cid=2).reshape(reps, -1, head_cols)
    norm_one, rstd_one = normalize(first_sum)
    mid_norm = norm_one * gain_all[0] + bias_all[3]
    mid_b = mid_norm.astype(jnp.bfloat16)
    mid_all = gather_rep(mid_b)
    pre_act = matmul(mid_all, w_up_r) + up_bias_r
    act_f32, gelu_slope = gelu_pair(pre_act)
    act_b = act_f32.astype(jnp.bfloat16)
    second_sum = mid_norm + scatter_rep(matmul(act_b, w_down_r)) + bias_all[4]
    norm_two, rstd_two = normalize(second_sum)
    layer_out = norm_two * gain_all[1] + bias_all[5]

    grad_rows = cotangent[0]
    d_gain_two = jnp.sum(grad_rows * norm_two, axis=0)
    d_bias_two = jnp.sum(grad_rows, axis=0)
    d_second = norm_back(grad_rows, norm_two, rstd_two, gain_all[1])
    d_bdown = jnp.sum(d_second, axis=0)
    d_second_all = gather_rep(d_second.astype(jnp.bfloat16))
    d_wdown = matmul_lt(act_b, d_second_all)
    d_pre = matmul_rt(d_second_all, w_down_r) * gelu_slope
    d_bup = jnp.sum(d_pre, axis=0)
    d_pre_b = d_pre.astype(jnp.bfloat16)
    d_wup = matmul_lt(mid_all, d_pre_b)
    ffn_pack = jnp.concatenate(
        [d_wup.astype(jnp.bfloat16).reshape(parts, -1), d_wdown.astype(jnp.bfloat16).reshape(parts, -1)],
        axis=1,
    ).reshape(parts, 8, -1)
    ffn_recv = lax.all_to_all(ffn_pack, "shard", 0, 0, tiled=True)
    ffn_share = jnp.sum(ffn_recv.astype(jnp.float32), axis=0).astype(jnp.bfloat16)
    d_mid = d_second + scatter_rep(matmul_rt(d_pre_b, w_up_r))
    d_gain_one = jnp.sum(d_mid * norm_one, axis=0)
    d_bias_one = jnp.sum(d_mid, axis=0)
    d_first = norm_back(d_mid, norm_one, rstd_one, gain_all[0])
    d_bout = jnp.sum(d_first, axis=0)
    d_first_all = gather_rep(d_first.astype(jnp.bfloat16))
    d_first_cols = lax.dynamic_slice_in_dim(d_first_all, r * head_cols, head_cols, axis=1)
    d_wout_cols = jnp.einsum(
        "utc,tk->uck", context_stack, d_first_cols, preferred_element_type=jnp.float32
    ).reshape(D, head_cols)
    d_context = (
        matmul_rt(d_first_all, w_out_r).astype(jnp.bfloat16).reshape(1, -1, heads_here, HEAD_DIM)
    )
    probs_again = jnp.where(allowed, jnp.exp(scores - log_total), 0.0)
    d_probs = jnp.einsum(
        "sqhe,skhe->shqk", d_context, values_all, preferred_element_type=jnp.float32
    )
    d_scores = (
        probs_again
        * (d_probs - jnp.sum(probs_again * d_probs, axis=-1, keepdims=True))
        * (1.0 / math.sqrt(HEAD_DIM))
    ).astype(jnp.bfloat16)
    d_queries = jnp.einsum(
        "shqk,skhe->sqhe", d_scores, keys_all, preferred_element_type=jnp.float32
    ).reshape(-1, head_cols)
    d_keys = jnp.einsum(
        "shqk,sqhe->skhe", d_scores, queries, preferred_element_type=jnp.float32
    ).reshape(-1, head_cols)
    d_values = jnp.einsum(
        "shqk,sqhe->skhe",
        probs_again.astype(jnp.bfloat16),
        d_context,
        preferred_element_type=jnp.float32,
    ).reshape(-1, head_cols)
    d_qkv = jnp.concatenate([d_queries, d_keys, d_values], axis=-1).astype(jnp.bfloat16)
    d_wqkv = matmul_lt(hb_all, d_qkv)
    input_grad = d_first + scatter_rep(matmul_rt(d_qkv, w_qkv_r))

    zeros_cols = jnp.zeros((D,), jnp.float32)
    d_bq = lax.dynamic_update_slice_in_dim(zeros_cols, jnp.sum(d_queries, axis=0), r * head_cols, 0)
    d_bv = lax.dynamic_update_slice_in_dim(zeros_cols, jnp.sum(d_values, axis=0), r * head_cols, 0)
    d_biases = jnp.stack([d_bq, d_bv, d_bout, d_bias_one, d_bdown, d_bias_two])
    d_gains = jnp.stack([d_gain_one, d_gain_two])
    d_bup_all = lax.dynamic_update_slice_in_dim(
        jnp.zeros((parts, reps, ff_piece), jnp.float32), d_bup.reshape(parts, 1, ff_piece), r, 1
    )
    grad_parts = (
        d_wqkv.astype(jnp.bfloat16).reshape(parts, -1),
        d_wout_cols.astype(jnp.bfloat16).reshape(parts, -1),
        d_bup_all.astype(jnp.bfloat16).reshape(parts, -1),
        pack_cols(d_biases.astype(jnp.bfloat16), parts),
        pack_cols(d_gains.astype(jnp.bfloat16), parts),
    )
    g_sizes = [piece.shape[1] for piece in grad_parts]
    grad_pack = jnp.concatenate(grad_parts, axis=1)
    width = grad_pack.shape[1]
    padded = -(-width // 1024) * 1024
    grad_pack = jnp.pad(grad_pack, ((0, 0), (0, padded - width))).reshape(parts, 8, -1)
    received = lax.all_to_all(grad_pack, "shard", 0, 0, tiled=True)
    shares = jnp.sum(received.astype(jnp.float32), axis=0).astype(jnp.bfloat16)
    all_shares = jnp.concatenate([shares.reshape(-1), ffn_share.reshape(-1)])
    joined = lax.all_gather(all_shares, "rep", axis=0, tiled=False).astype(jnp.float32)
    g_sizes = g_sizes + [padded - width, ffn_share.size // 2, ffn_share.size // 2]
    names = ["qkv", "out", "bup", "bias", "gain", "pad", "up", "down"]
    g_offsets = [sum(g_sizes[:i]) for i in range(len(g_sizes) + 1)]
    got = {names[i]: joined[:, g_offsets[i] : g_offsets[i + 1]] for i in range(len(g_sizes))}
    grad_w_qkv = got["qkv"].reshape(reps, k_rows, 3, head_cols).transpose(1, 2, 0, 3).reshape(k_rows, -1)
    grad_w_out = got["out"].reshape(reps, k_rows, head_cols).transpose(1, 0, 2).reshape(k_rows, D)
    grad_w_up = got["up"].reshape(reps, k_rows, parts, ff_piece).transpose(1, 2, 0, 3).reshape(k_rows, -1)
    grad_w_down = got["down"].reshape(reps * ff_piece, D)
    grad_up_bias = jnp.sum(got["bup"], axis=0)
    grad_biases = jnp.sum(got["bias"], axis=0).reshape(biases.shape[1], -1)
    grad_gains = jnp.sum(got["gain"], axis=0).reshape(norm_gains.shape[1], -1)
    return (
        layer_out[None],
        input_grad[None],
        grad_w_qkv[None],
        grad_w_out[None],
        grad_w_up[None],
        grad_w_down[None],
        grad_biases[None],
        grad_gains[None],
        grad_up_bias[None],
    )


def solution(mesh):
    in_specs = (
        P("shard", "rep", None),
        P("shard", "rep"),
        P("shard", "rep", None),
        P(None, "shard", None),
        P(None, "shard", None),
        P(None, "shard", None),
        P(None, "shard", None),
        P(None, None, "shard"),
        P(None, None, "shard"),
        P(None, "shard"),
    )
    out_specs = (
        P("shard", "rep", None),
        P("shard", "rep", None),
        P(None, "shard", None),
        P(None, "shard", None),
        P(None, "shard", None),
        P(None, "shard", None),
        P(None, None, "shard"),
        P(None, None, "shard"),
        P(None, "shard"),
    )
    return jax.shard_map(local, mesh=mesh, in_specs=in_specs, out_specs=out_specs, check_vma=False)
```

```python
import math

import jax
import jax.numpy as jnp
from jax import lax
from jax.experimental import pallas as pl
from jax.experimental.pallas import tpu as pltpu
from jax.sharding import PartitionSpec as P

D = 1024
HEADS = 16
HEAD_DIM = 64
LAYERS = 1


epsilon = 1e-06


def normalize(residual):
    center = residual - jnp.mean(residual, axis=-1, keepdims=True)
    rstd_val = lax.rsqrt(jnp.mean(center * center, axis=-1, keepdims=True) + epsilon)
    return (center * rstd_val, rstd_val)


def norm_back(grad_out, x_hat, rstd_val, gain_row):
    d_hat = grad_out * gain_row
    return rstd_val * (
        d_hat
        - jnp.mean(d_hat, axis=-1, keepdims=True)
        - x_hat * jnp.mean(d_hat * x_hat, axis=-1, keepdims=True)
    )


def gelu_pair(pre_act):
    normal_cdf = 0.5 * (1.0 + lax.erf(pre_act * (1.0 / math.sqrt(2.0))))
    density = jnp.exp(-0.5 * pre_act * pre_act) * (1.0 / math.sqrt(2.0 * math.pi))
    return (pre_act * normal_cdf, normal_cdf + pre_act * density)


def matmul(first_op, second_op):
    return jnp.dot(first_op, second_op, preferred_element_type=jnp.float32)


def matmul_lt(first_op, second_op):
    return lax.dot_general(
        first_op, second_op, (((0,), (0,)), ((), ())), preferred_element_type=jnp.float32
    )


def matmul_rt(first_op, second_op):
    return lax.dot_general(
        first_op, second_op, (((1,), (1,)), ((), ())), preferred_element_type=jnp.float32
    )


def attention_scores(queries, keys_all, seg_rows, seg_cols):
    scores = jnp.einsum(
        "sqhe,skhe->shqk", queries, keys_all, preferred_element_type=jnp.float32
    ) * (1.0 / math.sqrt(HEAD_DIM))
    allowed = seg_rows[:, None, :, None] == seg_cols[:, None, None, :]
    return (scores, allowed)


def pick(tensor, index, axis):
    return lax.dynamic_index_in_dim(tensor, index, axis=axis, keepdims=False)


def pack_cols(tensor, parts):
    rows = tensor.shape[0]
    return tensor.reshape(rows, parts, -1).transpose(1, 0, 2).reshape(parts, -1)


def unpack_cols(flat, parts, rows):
    return flat.reshape(parts, rows, -1).transpose(1, 0, 2).reshape(rows, -1)


def rep_gather_kernel(x_ref, o_ref, send_sem, recv_sem):
    me = lax.axis_index("rep")
    rows = x_ref.shape[0]
    other_chip = lax.rem(me + 2, 4)
    other_core = me + 1 - 2 * lax.rem(me, 2)
    o_ref[pl.ds(me * rows, rows), :] = x_ref[...]
    barrier = pltpu.get_barrier_semaphore()
    for peer in (other_chip, other_core):
        pl.semaphore_signal(barrier, inc=1, device_id={"rep": peer}, device_id_type=pl.DeviceIdType.MESH)
    pl.semaphore_wait(barrier, 2)
    cross = pltpu.make_async_remote_copy(
        src_ref=x_ref,
        dst_ref=o_ref.at[pl.ds(me * rows, rows)],
        send_sem=send_sem.at[0],
        recv_sem=recv_sem.at[0],
        device_id={"rep": other_chip},
        device_id_type=pl.DeviceIdType.MESH,
    )
    cross.start()
    own = pltpu.make_async_remote_copy(
        src_ref=x_ref,
        dst_ref=o_ref.at[pl.ds(me * rows, rows)],
        send_sem=send_sem.at[1],
        recv_sem=recv_sem.at[1],
        device_id={"rep": other_core},
        device_id_type=pl.DeviceIdType.MESH,
    )
    own.start()
    cross.wait()
    relay = pltpu.make_async_remote_copy(
        src_ref=o_ref.at[pl.ds(other_chip * rows, rows)],
        dst_ref=o_ref.at[pl.ds(other_chip * rows, rows)],
        send_sem=send_sem.at[2],
        recv_sem=recv_sem.at[2],
        device_id={"rep": other_core},
        device_id_type=pl.DeviceIdType.MESH,
    )
    relay.start()
    own.wait()
    relay.wait()


def gather_rep(tensor, cid=1):
    n = lax.axis_size("rep")
    rows, cols = tensor.shape
    return pl.pallas_call(
        rep_gather_kernel,
        out_shape=jax.ShapeDtypeStruct((n * rows, cols), tensor.dtype),
        in_specs=[pl.BlockSpec(memory_space=pltpu.VMEM)],
        out_specs=pl.BlockSpec(memory_space=pltpu.VMEM),
        scratch_shapes=[pltpu.SemaphoreType.DMA((n - 1,)), pltpu.SemaphoreType.DMA((n - 1,))],
        compiler_params=pltpu.CompilerParams(collective_id=cid, has_side_effects=True),
    )(tensor)


def scatter_rep(tensor):
    return lax.psum_scatter(tensor, "rep", scatter_dimension=0, tiled=True)


def local(inputs, segment_ids, cotangent, w_qkv, w_out, w_up, w_down, biases, norm_gains, up_bias):
    parts = lax.axis_size("shard")
    reps = lax.axis_size("rep")
    r = lax.axis_index("rep")
    head_cols = D // reps
    heads_here = HEADS // reps
    ff_all = w_up.shape[2]
    ff_chunk = ff_all // parts
    ff_piece = ff_chunk // reps
    k_rows = D // parts

    qkv_piece = pick(w_qkv[0].reshape(k_rows, 3, reps, head_cols), r, 2).reshape(k_rows, -1)
    out_piece = w_out[0]
    up_piece = pick(w_up[0].reshape(k_rows, parts, reps, ff_piece), r, 2).reshape(k_rows, -1)
    down_piece = pick(w_down[0].reshape(reps, ff_piece, D), r, 0)
    upb_piece = pick(up_bias[0].reshape(reps, ff_piece), r, 0)
    pieces = (qkv_piece, out_piece, up_piece, down_piece, upb_piece, biases[0], norm_gains[0])
    sizes = [piece.size for piece in pieces]
    offsets = [sum(sizes[:i]) for i in range(len(sizes) + 1)]
    packed = jnp.concatenate([piece.reshape(-1) for piece in pieces])
    packed = jnp.pad(packed, (0, -(-packed.size // 1024) * 1024 - packed.size))
    gathered = lax.all_gather(packed, "shard", axis=0, tiled=False)
    got = [gathered[:, offsets[i] : offsets[i + 1]] for i in range(len(sizes))]
    w_qkv_r = got[0].reshape(D, 3 * head_cols)
    w_out_all = got[1].reshape(D, D)
    w_out_r = lax.dynamic_slice_in_dim(w_out_all, r * head_cols, head_cols, axis=0)
    w_up_r = got[2].reshape(D, -1)
    w_down_r = got[3].reshape(-1, D)
    up_bias_r = got[4].reshape(-1)
    bias_all = unpack_cols(got[5], parts, biases.shape[1])
    gain_all = unpack_cols(got[6], parts, norm_gains.shape[1])
    bias_q = lax.dynamic_slice_in_dim(bias_all[0], r * head_cols, head_cols)
    bias_v = lax.dynamic_slice_in_dim(bias_all[1], r * head_cols, head_cols)

    rows_f32 = inputs[0]
    own = rows_f32.shape[0]
    rows_bf = rows_f32.astype(jnp.bfloat16)
    seg_tag = jnp.broadcast_to(segment_ids[0].astype(jnp.bfloat16)[:, None], (own, 128))
    hb_seg = gather_rep(jnp.concatenate([rows_bf, seg_tag], axis=1), cid=0)
    hb_all = hb_seg[:, :D]
    seg_all = hb_seg[:, D]
    qkv_rows = matmul(hb_all, w_qkv_r)
    queries = (qkv_rows[:, :head_cols] + bias_q).astype(jnp.bfloat16).reshape(1, -1, heads_here, HEAD_DIM)
    keys_all = qkv_rows[:, head_cols : 2 * head_cols].astype(jnp.bfloat16).reshape(1, -1, heads_here, HEAD_DIM)
    values_all = (
        (qkv_rows[:, 2 * head_cols :] + bias_v).astype(jnp.bfloat16).reshape(1, -1, heads_here, HEAD_DIM)
    )
    seg_rows = seg_all[None]
    scores, allowed = attention_scores(queries, keys_all, seg_rows, seg_rows)
    expo_all = jnp.where(allowed, jnp.exp(scores), 0.0)
    row_total = jnp.sum(expo_all, axis=-1, keepdims=True)
    log_total = jnp.log(row_total)
    attn_probs = (expo_all / row_total).astype(jnp.bfloat16)
    context = (
        jnp.einsum("shqk,skhe->sqhe", attn_probs, values_all, preferred_element_type=jnp.float32)
        .astype(jnp.bfloat16)
        .reshape(-1, head_cols)
    )
    first_sum = rows_f32 + scatter_rep(matmul(context, w_out_r)) + bias_all[2]
    context_stack = gather_rep(context, cid=2).reshape(reps, -1, head_cols)
    norm_one, rstd_one = normalize(first_sum)
    mid_norm = norm_one * gain_all[0] + bias_all[3]
    mid_b = mid_norm.astype(jnp.bfloat16)
    mid_all = gather_rep(mid_b)
    pre_act = matmul(mid_all, w_up_r) + up_bias_r
    act_f32, gelu_slope = gelu_pair(pre_act)
    act_b = act_f32.astype(jnp.bfloat16)
    second_sum = mid_norm + scatter_rep(matmul(act_b, w_down_r)) + bias_all[4]
    norm_two, rstd_two = normalize(second_sum)
    layer_out = norm_two * gain_all[1] + bias_all[5]

    grad_rows = cotangent[0]
    d_gain_two = jnp.sum(grad_rows * norm_two, axis=0)
    d_bias_two = jnp.sum(grad_rows, axis=0)
    d_second = norm_back(grad_rows, norm_two, rstd_two, gain_all[1])
    d_bdown = jnp.sum(d_second, axis=0)
    d_second_all = gather_rep(d_second.astype(jnp.bfloat16))
    d_wdown = matmul_lt(act_b, d_second_all)
    d_pre = matmul_rt(d_second_all, w_down_r) * gelu_slope
    d_bup = jnp.sum(d_pre, axis=0)
    d_pre_b = d_pre.astype(jnp.bfloat16)
    d_wup = matmul_lt(mid_all, d_pre_b)
    ffn_pack = jnp.concatenate(
        [d_wup.astype(jnp.bfloat16).reshape(parts, -1), d_wdown.astype(jnp.bfloat16).reshape(parts, -1)],
        axis=1,
    ).reshape(parts, 8, -1)
    ffn_recv = lax.all_to_all(ffn_pack, "shard", 0, 0, tiled=True)
    ffn_share = jnp.sum(ffn_recv.astype(jnp.float32), axis=0).astype(jnp.bfloat16)
    d_mid = d_second + scatter_rep(matmul_rt(d_pre_b, w_up_r))
    d_gain_one = jnp.sum(d_mid * norm_one, axis=0)
    d_bias_one = jnp.sum(d_mid, axis=0)
    d_first = norm_back(d_mid, norm_one, rstd_one, gain_all[0])
    d_bout = jnp.sum(d_first, axis=0)
    d_first_all = gather_rep(d_first.astype(jnp.bfloat16))
    d_first_cols = lax.dynamic_slice_in_dim(d_first_all, r * head_cols, head_cols, axis=1)
    d_wout_cols = jnp.einsum(
        "utc,tk->uck", context_stack, d_first_cols, preferred_element_type=jnp.float32
    ).reshape(D, head_cols)
    d_context = (
        matmul_rt(d_first_all, w_out_r).astype(jnp.bfloat16).reshape(1, -1, heads_here, HEAD_DIM)
    )
    probs_again = jnp.where(allowed, jnp.exp(scores - log_total), 0.0)
    d_probs = jnp.einsum(
        "sqhe,skhe->shqk", d_context, values_all, preferred_element_type=jnp.float32
    )
    d_scores = (
        probs_again
        * (d_probs - jnp.sum(probs_again * d_probs, axis=-1, keepdims=True))
        * (1.0 / math.sqrt(HEAD_DIM))
    ).astype(jnp.bfloat16)
    d_queries = jnp.einsum(
        "shqk,skhe->sqhe", d_scores, keys_all, preferred_element_type=jnp.float32
    ).reshape(-1, head_cols)
    d_keys = jnp.einsum(
        "shqk,sqhe->skhe", d_scores, queries, preferred_element_type=jnp.float32
    ).reshape(-1, head_cols)
    d_values = jnp.einsum(
        "shqk,sqhe->skhe",
        probs_again.astype(jnp.bfloat16),
        d_context,
        preferred_element_type=jnp.float32,
    ).reshape(-1, head_cols)
    d_qkv = jnp.concatenate([d_queries, d_keys, d_values], axis=-1).astype(jnp.bfloat16)
    d_wqkv = matmul_lt(hb_all, d_qkv)
    input_grad = d_first + scatter_rep(matmul_rt(d_qkv, w_qkv_r))

    zeros_cols = jnp.zeros((D,), jnp.float32)
    d_bq = lax.dynamic_update_slice_in_dim(zeros_cols, jnp.sum(d_queries, axis=0), r * head_cols, 0)
    d_bv = lax.dynamic_update_slice_in_dim(zeros_cols, jnp.sum(d_values, axis=0), r * head_cols, 0)
    d_biases = jnp.stack([d_bq, d_bv, d_bout, d_bias_one, d_bdown, d_bias_two])
    d_gains = jnp.stack([d_gain_one, d_gain_two])
    d_bup_all = lax.dynamic_update_slice_in_dim(
        jnp.zeros((parts, reps, ff_piece), jnp.float32), d_bup.reshape(parts, 1, ff_piece), r, 1
    )
    grad_parts = (
        d_wqkv.astype(jnp.bfloat16).reshape(parts, -1),
        d_wout_cols.astype(jnp.bfloat16).reshape(parts, -1),
        d_bup_all.astype(jnp.bfloat16).reshape(parts, -1),
        pack_cols(d_biases.astype(jnp.bfloat16), parts),
        pack_cols(d_gains.astype(jnp.bfloat16), parts),
    )
    g_sizes = [piece.shape[1] for piece in grad_parts]
    grad_pack = jnp.concatenate(grad_parts, axis=1)
    width = grad_pack.shape[1]
    padded = -(-width // 1024) * 1024
    grad_pack = jnp.pad(grad_pack, ((0, 0), (0, padded - width))).reshape(parts, 8, -1)
    received = lax.all_to_all(grad_pack, "shard", 0, 0, tiled=True)
    shares = jnp.sum(received.astype(jnp.float32), axis=0).astype(jnp.bfloat16)
    all_shares = jnp.concatenate([shares.reshape(-1), ffn_share.reshape(-1)])
    joined = lax.all_gather(all_shares, "rep", axis=0, tiled=False).astype(jnp.float32)
    g_sizes = g_sizes + [padded - width, ffn_share.size // 2, ffn_share.size // 2]
    names = ["qkv", "out", "bup", "bias", "gain", "pad", "up", "down"]
    g_offsets = [sum(g_sizes[:i]) for i in range(len(g_sizes) + 1)]
    got = {names[i]: joined[:, g_offsets[i] : g_offsets[i + 1]] for i in range(len(g_sizes))}
    grad_w_qkv = got["qkv"].reshape(reps, k_rows, 3, head_cols).transpose(1, 2, 0, 3).reshape(k_rows, -1)
    grad_w_out = got["out"].reshape(reps, k_rows, head_cols).transpose(1, 0, 2).reshape(k_rows, D)
    grad_w_up = got["up"].reshape(reps, k_rows, parts, ff_piece).transpose(1, 2, 0, 3).reshape(k_rows, -1)
    grad_w_down = got["down"].reshape(reps * ff_piece, D)
    grad_up_bias = jnp.sum(got["bup"], axis=0)
    grad_biases = jnp.sum(got["bias"], axis=0).reshape(biases.shape[1], -1)
    grad_gains = jnp.sum(got["gain"], axis=0).reshape(norm_gains.shape[1], -1)
    return (
        layer_out[None],
        input_grad[None],
        grad_w_qkv[None],
        grad_w_out[None],
        grad_w_up[None],
        grad_w_down[None],
        grad_biases[None],
        grad_gains[None],
        grad_up_bias[None],
    )


def solution(mesh):
    in_specs = (
        P("shard", "rep", None),
        P("shard", "rep"),
        P("shard", "rep", None),
        P(None, "shard", None),
        P(None, "shard", None),
        P(None, "shard", None),
        P(None, "shard", None),
        P(None, None, "shard"),
        P(None, None, "shard"),
        P(None, "shard"),
    )
    out_specs = (
        P("shard", "rep", None),
        P("shard", "rep", None),
        P(None, "shard", None),
        P(None, "shard", None),
        P(None, "shard", None),
        P(None, "shard", None),
        P(None, None, "shard"),
        P(None, None, "shard"),
        P(None, "shard"),
    )
    return jax.shard_map(local, mesh=mesh, in_specs=in_specs, out_specs=out_specs, check_vma=False)
```

```python
import math

import jax
import jax.numpy as jnp
from jax import lax
from jax.experimental import pallas as pl
from jax.experimental.pallas import tpu as pltpu
from jax.sharding import PartitionSpec as P

D = 1024
HEADS = 16
HEAD_DIM = 64
LAYERS = 1


epsilon = 1e-06


def normalize(residual):
    center = residual - jnp.mean(residual, axis=-1, keepdims=True)
    rstd_val = lax.rsqrt(jnp.mean(center * center, axis=-1, keepdims=True) + epsilon)
    return (center * rstd_val, rstd_val)


def norm_back(grad_out, x_hat, rstd_val, gain_row):
    d_hat = grad_out * gain_row
    return rstd_val * (
        d_hat
        - jnp.mean(d_hat, axis=-1, keepdims=True)
        - x_hat * jnp.mean(d_hat * x_hat, axis=-1, keepdims=True)
    )


def gelu_pair(pre_act):
    normal_cdf = 0.5 * (1.0 + lax.erf(pre_act * (1.0 / math.sqrt(2.0))))
    density = jnp.exp(-0.5 * pre_act * pre_act) * (1.0 / math.sqrt(2.0 * math.pi))
    return (pre_act * normal_cdf, normal_cdf + pre_act * density)


def matmul(first_op, second_op):
    return jnp.dot(first_op, second_op, preferred_element_type=jnp.float32)


def matmul_lt(first_op, second_op):
    return lax.dot_general(
        first_op, second_op, (((0,), (0,)), ((), ())), preferred_element_type=jnp.float32
    )


def matmul_rt(first_op, second_op):
    return lax.dot_general(
        first_op, second_op, (((1,), (1,)), ((), ())), preferred_element_type=jnp.float32
    )


def attention_scores(queries, keys_all, seg_rows, seg_cols):
    scores = jnp.einsum(
        "sqhe,skhe->shqk", queries, keys_all, preferred_element_type=jnp.float32
    ) * (1.0 / math.sqrt(HEAD_DIM))
    allowed = seg_rows[:, None, :, None] == seg_cols[:, None, None, :]
    return (scores, allowed)


def pick(tensor, index, axis):
    return lax.dynamic_index_in_dim(tensor, index, axis=axis, keepdims=False)


def pack_cols(tensor, parts):
    rows = tensor.shape[0]
    return tensor.reshape(rows, parts, -1).transpose(1, 0, 2).reshape(parts, -1)


def unpack_cols(flat, parts, rows):
    return flat.reshape(parts, rows, -1).transpose(1, 0, 2).reshape(rows, -1)


def rep_gather_kernel(x_ref, o_ref, send_sem, recv_sem):
    me = lax.axis_index("rep")
    rows = x_ref.shape[0]
    other_chip = lax.rem(me + 2, 4)
    other_core = me + 1 - 2 * lax.rem(me, 2)
    o_ref[pl.ds(me * rows, rows), :] = x_ref[...]
    barrier = pltpu.get_barrier_semaphore()
    for peer in (other_chip, other_core):
        pl.semaphore_signal(barrier, inc=1, device_id={"rep": peer}, device_id_type=pl.DeviceIdType.MESH)
    pl.semaphore_wait(barrier, 2)
    cross = pltpu.make_async_remote_copy(
        src_ref=x_ref,
        dst_ref=o_ref.at[pl.ds(me * rows, rows)],
        send_sem=send_sem.at[0],
        recv_sem=recv_sem.at[0],
        device_id={"rep": other_chip},
        device_id_type=pl.DeviceIdType.MESH,
    )
    cross.start()
    own = pltpu.make_async_remote_copy(
        src_ref=x_ref,
        dst_ref=o_ref.at[pl.ds(me * rows, rows)],
        send_sem=send_sem.at[1],
        recv_sem=recv_sem.at[1],
        device_id={"rep": other_core},
        device_id_type=pl.DeviceIdType.MESH,
    )
    own.start()
    cross.wait()
    relay = pltpu.make_async_remote_copy(
        src_ref=o_ref.at[pl.ds(other_chip * rows, rows)],
        dst_ref=o_ref.at[pl.ds(other_chip * rows, rows)],
        send_sem=send_sem.at[2],
        recv_sem=recv_sem.at[2],
        device_id={"rep": other_core},
        device_id_type=pl.DeviceIdType.MESH,
    )
    relay.start()
    own.wait()
    relay.wait()


def gather_rep(tensor, cid=1):
    n = lax.axis_size("rep")
    rows, cols = tensor.shape
    return pl.pallas_call(
        rep_gather_kernel,
        out_shape=jax.ShapeDtypeStruct((n * rows, cols), tensor.dtype),
        in_specs=[pl.BlockSpec(memory_space=pltpu.VMEM)],
        out_specs=pl.BlockSpec(memory_space=pltpu.VMEM),
        scratch_shapes=[pltpu.SemaphoreType.DMA((n - 1,)), pltpu.SemaphoreType.DMA((n - 1,))],
        compiler_params=pltpu.CompilerParams(collective_id=cid, has_side_effects=True),
    )(tensor)


def rep_scatter_kernel(p_ref, o_ref, onchip_buf, cross_buf, partial, send_sem, recv_sem):
    me = lax.axis_index("rep")
    rows = o_ref.shape[0]
    other_chip = lax.rem(me + 2, 4)
    other_core = me + 1 - 2 * lax.rem(me, 2)
    diagonal = lax.rem(other_core + 2, 4)
    barrier = pltpu.get_barrier_semaphore()
    for peer in (other_chip, other_core):
        pl.semaphore_signal(barrier, inc=1, device_id={"rep": peer}, device_id_type=pl.DeviceIdType.MESH)
    pl.semaphore_wait(barrier, 2)
    near = []
    for slot, block in ((0, other_core), (1, diagonal)):
        copy = pltpu.make_async_remote_copy(
            src_ref=p_ref.at[pl.ds(block * rows, rows)],
            dst_ref=onchip_buf.at[slot],
            send_sem=send_sem.at[slot],
            recv_sem=recv_sem.at[slot],
            device_id={"rep": other_core},
            device_id_type=pl.DeviceIdType.MESH,
        )
        copy.start()
        near.append(copy)
    for copy in near:
        copy.wait()
    partial[...] = p_ref[pl.ds(other_chip * rows, rows), :] + onchip_buf[1]
    far = pltpu.make_async_remote_copy(
        src_ref=partial,
        dst_ref=cross_buf,
        send_sem=send_sem.at[2],
        recv_sem=recv_sem.at[2],
        device_id={"rep": other_chip},
        device_id_type=pl.DeviceIdType.MESH,
    )
    far.start()
    far.wait()
    o_ref[...] = p_ref[pl.ds(me * rows, rows), :] + onchip_buf[0] + cross_buf[...]


def scatter_rep(tensor, cid=4):
    n = lax.axis_size("rep")
    rows, cols = tensor.shape[0] // n, tensor.shape[1]
    return pl.pallas_call(
        rep_scatter_kernel,
        out_shape=jax.ShapeDtypeStruct((rows, cols), tensor.dtype),
        in_specs=[pl.BlockSpec(memory_space=pltpu.VMEM)],
        out_specs=pl.BlockSpec(memory_space=pltpu.VMEM),
        scratch_shapes=[
            pltpu.VMEM((2, rows, cols), tensor.dtype),
            pltpu.VMEM((rows, cols), tensor.dtype),
            pltpu.VMEM((rows, cols), tensor.dtype),
            pltpu.SemaphoreType.DMA((3,)),
            pltpu.SemaphoreType.DMA((3,)),
        ],
        compiler_params=pltpu.CompilerParams(collective_id=cid, has_side_effects=True),
    )(tensor)


def local(inputs, segment_ids, cotangent, w_qkv, w_out, w_up, w_down, biases, norm_gains, up_bias):
    parts = lax.axis_size("shard")
    reps = lax.axis_size("rep")
    r = lax.axis_index("rep")
    head_cols = D // reps
    heads_here = HEADS // reps
    ff_all = w_up.shape[2]
    ff_chunk = ff_all // parts
    ff_piece = ff_chunk // reps
    k_rows = D // parts

    qkv_piece = pick(w_qkv[0].reshape(k_rows, 3, reps, head_cols), r, 2).reshape(k_rows, -1)
    out_piece = w_out[0]
    up_piece = pick(w_up[0].reshape(k_rows, parts, reps, ff_piece), r, 2).reshape(k_rows, -1)
    down_piece = pick(w_down[0].reshape(reps, ff_piece, D), r, 0)
    upb_piece = pick(up_bias[0].reshape(reps, ff_piece), r, 0)
    pieces = (qkv_piece, out_piece, up_piece, down_piece, upb_piece, biases[0], norm_gains[0])
    sizes = [piece.size for piece in pieces]
    offsets = [sum(sizes[:i]) for i in range(len(sizes) + 1)]
    packed = jnp.concatenate([piece.reshape(-1) for piece in pieces])
    packed = jnp.pad(packed, (0, -(-packed.size // 1024) * 1024 - packed.size))
    gathered = lax.all_gather(packed, "shard", axis=0, tiled=False)
    got = [gathered[:, offsets[i] : offsets[i + 1]] for i in range(len(sizes))]
    w_qkv_r = got[0].reshape(D, 3 * head_cols)
    w_out_all = got[1].reshape(D, D)
    w_out_r = lax.dynamic_slice_in_dim(w_out_all, r * head_cols, head_cols, axis=0)
    w_up_r = got[2].reshape(D, -1)
    w_down_r = got[3].reshape(-1, D)
    up_bias_r = got[4].reshape(-1)
    bias_all = unpack_cols(got[5], parts, biases.shape[1])
    gain_all = unpack_cols(got[6], parts, norm_gains.shape[1])
    bias_q = lax.dynamic_slice_in_dim(bias_all[0], r * head_cols, head_cols)
    bias_v = lax.dynamic_slice_in_dim(bias_all[1], r * head_cols, head_cols)

    rows_f32 = inputs[0]
    own = rows_f32.shape[0]
    rows_bf = rows_f32.astype(jnp.bfloat16)
    seg_tag = jnp.broadcast_to(segment_ids[0].astype(jnp.bfloat16)[:, None], (own, 128))
    hb_seg = gather_rep(jnp.concatenate([rows_bf, seg_tag], axis=1), cid=0)
    hb_all = hb_seg[:, :D]
    seg_all = hb_seg[:, D]
    qkv_rows = matmul(hb_all, w_qkv_r)
    queries = (qkv_rows[:, :head_cols] + bias_q).astype(jnp.bfloat16).reshape(1, -1, heads_here, HEAD_DIM)
    keys_all = qkv_rows[:, head_cols : 2 * head_cols].astype(jnp.bfloat16).reshape(1, -1, heads_here, HEAD_DIM)
    values_all = (
        (qkv_rows[:, 2 * head_cols :] + bias_v).astype(jnp.bfloat16).reshape(1, -1, heads_here, HEAD_DIM)
    )
    seg_rows = seg_all[None]
    scores, allowed = attention_scores(queries, keys_all, seg_rows, seg_rows)
    expo_all = jnp.where(allowed, jnp.exp(scores), 0.0)
    row_total = jnp.sum(expo_all, axis=-1, keepdims=True)
    log_total = jnp.log(row_total)
    attn_probs = (expo_all / row_total).astype(jnp.bfloat16)
    context = (
        jnp.einsum("shqk,skhe->sqhe", attn_probs, values_all, preferred_element_type=jnp.float32)
        .astype(jnp.bfloat16)
        .reshape(-1, head_cols)
    )
    first_sum = rows_f32 + scatter_rep(matmul(context, w_out_r)) + bias_all[2]
    context_stack = gather_rep(context, cid=2).reshape(reps, -1, head_cols)
    norm_one, rstd_one = normalize(first_sum)
    mid_norm = norm_one * gain_all[0] + bias_all[3]
    mid_b = mid_norm.astype(jnp.bfloat16)
    mid_all = gather_rep(mid_b)
    pre_act = matmul(mid_all, w_up_r) + up_bias_r
    act_f32, gelu_slope = gelu_pair(pre_act)
    act_b = act_f32.astype(jnp.bfloat16)
    second_sum = mid_norm + scatter_rep(matmul(act_b, w_down_r)) + bias_all[4]
    norm_two, rstd_two = normalize(second_sum)
    layer_out = norm_two * gain_all[1] + bias_all[5]

    grad_rows = cotangent[0]
    d_gain_two = jnp.sum(grad_rows * norm_two, axis=0)
    d_bias_two = jnp.sum(grad_rows, axis=0)
    d_second = norm_back(grad_rows, norm_two, rstd_two, gain_all[1])
    d_bdown = jnp.sum(d_second, axis=0)
    d_second_all = gather_rep(d_second.astype(jnp.bfloat16))
    d_wdown = matmul_lt(act_b, d_second_all)
    d_pre = matmul_rt(d_second_all, w_down_r) * gelu_slope
    d_bup = jnp.sum(d_pre, axis=0)
    d_pre_b = d_pre.astype(jnp.bfloat16)
    d_wup = matmul_lt(mid_all, d_pre_b)
    ffn_pack = jnp.concatenate(
        [d_wup.astype(jnp.bfloat16).reshape(parts, -1), d_wdown.astype(jnp.bfloat16).reshape(parts, -1)],
        axis=1,
    ).reshape(parts, 8, -1)
    ffn_recv = lax.all_to_all(ffn_pack, "shard", 0, 0, tiled=True)
    ffn_share = jnp.sum(ffn_recv.astype(jnp.float32), axis=0).astype(jnp.bfloat16)
    d_mid = d_second + scatter_rep(matmul_rt(d_pre_b, w_up_r))
    d_gain_one = jnp.sum(d_mid * norm_one, axis=0)
    d_bias_one = jnp.sum(d_mid, axis=0)
    d_first = norm_back(d_mid, norm_one, rstd_one, gain_all[0])
    d_bout = jnp.sum(d_first, axis=0)
    d_first_all = gather_rep(d_first.astype(jnp.bfloat16))
    d_first_cols = lax.dynamic_slice_in_dim(d_first_all, r * head_cols, head_cols, axis=1)
    d_wout_cols = jnp.einsum(
        "utc,tk->uck", context_stack, d_first_cols, preferred_element_type=jnp.float32
    ).reshape(D, head_cols)
    d_context = (
        matmul_rt(d_first_all, w_out_r).astype(jnp.bfloat16).reshape(1, -1, heads_here, HEAD_DIM)
    )
    probs_again = jnp.where(allowed, jnp.exp(scores - log_total), 0.0)
    d_probs = jnp.einsum(
        "sqhe,skhe->shqk", d_context, values_all, preferred_element_type=jnp.float32
    )
    d_scores = (
        probs_again
        * (d_probs - jnp.sum(probs_again * d_probs, axis=-1, keepdims=True))
        * (1.0 / math.sqrt(HEAD_DIM))
    ).astype(jnp.bfloat16)
    d_queries = jnp.einsum(
        "shqk,skhe->sqhe", d_scores, keys_all, preferred_element_type=jnp.float32
    ).reshape(-1, head_cols)
    d_keys = jnp.einsum(
        "shqk,sqhe->skhe", d_scores, queries, preferred_element_type=jnp.float32
    ).reshape(-1, head_cols)
    d_values = jnp.einsum(
        "shqk,sqhe->skhe",
        probs_again.astype(jnp.bfloat16),
        d_context,
        preferred_element_type=jnp.float32,
    ).reshape(-1, head_cols)
    d_qkv = jnp.concatenate([d_queries, d_keys, d_values], axis=-1).astype(jnp.bfloat16)
    d_wqkv = matmul_lt(hb_all, d_qkv)
    input_grad = d_first + scatter_rep(matmul_rt(d_qkv, w_qkv_r))

    zeros_cols = jnp.zeros((D,), jnp.float32)
    d_bq = lax.dynamic_update_slice_in_dim(zeros_cols, jnp.sum(d_queries, axis=0), r * head_cols, 0)
    d_bv = lax.dynamic_update_slice_in_dim(zeros_cols, jnp.sum(d_values, axis=0), r * head_cols, 0)
    d_biases = jnp.stack([d_bq, d_bv, d_bout, d_bias_one, d_bdown, d_bias_two])
    d_gains = jnp.stack([d_gain_one, d_gain_two])
    d_bup_all = lax.dynamic_update_slice_in_dim(
        jnp.zeros((parts, reps, ff_piece), jnp.float32), d_bup.reshape(parts, 1, ff_piece), r, 1
    )
    grad_parts = (
        d_wqkv.astype(jnp.bfloat16).reshape(parts, -1),
        d_wout_cols.astype(jnp.bfloat16).reshape(parts, -1),
        d_bup_all.astype(jnp.bfloat16).reshape(parts, -1),
        pack_cols(d_biases.astype(jnp.bfloat16), parts),
        pack_cols(d_gains.astype(jnp.bfloat16), parts),
    )
    g_sizes = [piece.shape[1] for piece in grad_parts]
    grad_pack = jnp.concatenate(grad_parts, axis=1)
    width = grad_pack.shape[1]
    padded = -(-width // 1024) * 1024
    grad_pack = jnp.pad(grad_pack, ((0, 0), (0, padded - width))).reshape(parts, 8, -1)
    received = lax.all_to_all(grad_pack, "shard", 0, 0, tiled=True)
    shares = jnp.sum(received.astype(jnp.float32), axis=0).astype(jnp.bfloat16)
    all_shares = jnp.concatenate([shares.reshape(-1), ffn_share.reshape(-1)])
    joined = lax.all_gather(all_shares, "rep", axis=0, tiled=False).astype(jnp.float32)
    g_sizes = g_sizes + [padded - width, ffn_share.size // 2, ffn_share.size // 2]
    names = ["qkv", "out", "bup", "bias", "gain", "pad", "up", "down"]
    g_offsets = [sum(g_sizes[:i]) for i in range(len(g_sizes) + 1)]
    got = {names[i]: joined[:, g_offsets[i] : g_offsets[i + 1]] for i in range(len(g_sizes))}
    grad_w_qkv = got["qkv"].reshape(reps, k_rows, 3, head_cols).transpose(1, 2, 0, 3).reshape(k_rows, -1)
    grad_w_out = got["out"].reshape(reps, k_rows, head_cols).transpose(1, 0, 2).reshape(k_rows, D)
    grad_w_up = got["up"].reshape(reps, k_rows, parts, ff_piece).transpose(1, 2, 0, 3).reshape(k_rows, -1)
    grad_w_down = got["down"].reshape(reps * ff_piece, D)
    grad_up_bias = jnp.sum(got["bup"], axis=0)
    grad_biases = jnp.sum(got["bias"], axis=0).reshape(biases.shape[1], -1)
    grad_gains = jnp.sum(got["gain"], axis=0).reshape(norm_gains.shape[1], -1)
    return (
        layer_out[None],
        input_grad[None],
        grad_w_qkv[None],
        grad_w_out[None],
        grad_w_up[None],
        grad_w_down[None],
        grad_biases[None],
        grad_gains[None],
        grad_up_bias[None],
    )


def solution(mesh):
    in_specs = (
        P("shard", "rep", None),
        P("shard", "rep"),
        P("shard", "rep", None),
        P(None, "shard", None),
        P(None, "shard", None),
        P(None, "shard", None),
        P(None, "shard", None),
        P(None, None, "shard"),
        P(None, None, "shard"),
        P(None, "shard"),
    )
    out_specs = (
        P("shard", "rep", None),
        P("shard", "rep", None),
        P(None, "shard", None),
        P(None, "shard", None),
        P(None, "shard", None),
        P(None, "shard", None),
        P(None, None, "shard"),
        P(None, None, "shard"),
        P(None, "shard"),
    )
    return jax.shard_map(local, mesh=mesh, in_specs=in_specs, out_specs=out_specs, check_vma=False)
```

```python
import math

import jax
import jax.numpy as jnp
from jax import lax
from jax.experimental import pallas as pl
from jax.experimental.pallas import tpu as pltpu
from jax.sharding import PartitionSpec as P

D = 1024
HEADS = 16
HEAD_DIM = 64
LAYERS = 1


epsilon = 1e-06


def normalize(residual):
    center = residual - jnp.mean(residual, axis=-1, keepdims=True)
    rstd_val = lax.rsqrt(jnp.mean(center * center, axis=-1, keepdims=True) + epsilon)
    return (center * rstd_val, rstd_val)


def norm_back(grad_out, x_hat, rstd_val, gain_row):
    d_hat = grad_out * gain_row
    return rstd_val * (
        d_hat
        - jnp.mean(d_hat, axis=-1, keepdims=True)
        - x_hat * jnp.mean(d_hat * x_hat, axis=-1, keepdims=True)
    )


def gelu_pair(pre_act):
    normal_cdf = 0.5 * (1.0 + lax.erf(pre_act * (1.0 / math.sqrt(2.0))))
    density = jnp.exp(-0.5 * pre_act * pre_act) * (1.0 / math.sqrt(2.0 * math.pi))
    return (pre_act * normal_cdf, normal_cdf + pre_act * density)


def matmul(first_op, second_op):
    return jnp.dot(first_op, second_op, preferred_element_type=jnp.float32)


def matmul_lt(first_op, second_op):
    return lax.dot_general(
        first_op, second_op, (((0,), (0,)), ((), ())), preferred_element_type=jnp.float32
    )


def matmul_rt(first_op, second_op):
    return lax.dot_general(
        first_op, second_op, (((1,), (1,)), ((), ())), preferred_element_type=jnp.float32
    )


def attention_scores(queries, keys_all, seg_rows, seg_cols):
    scores = jnp.einsum(
        "sqhe,skhe->shqk", queries, keys_all, preferred_element_type=jnp.float32
    ) * (1.0 / math.sqrt(HEAD_DIM))
    allowed = seg_rows[:, None, :, None] == seg_cols[:, None, None, :]
    return (scores, allowed)


def pick(tensor, index, axis):
    return lax.dynamic_index_in_dim(tensor, index, axis=axis, keepdims=False)


def pack_cols(tensor, parts):
    rows = tensor.shape[0]
    return tensor.reshape(rows, parts, -1).transpose(1, 0, 2).reshape(parts, -1)


def unpack_cols(flat, parts, rows):
    return flat.reshape(parts, rows, -1).transpose(1, 0, 2).reshape(rows, -1)


def rep_gather_kernel(x_ref, o_ref, send_sem, recv_sem):
    me = lax.axis_index("rep")
    rows = x_ref.shape[0]
    other_chip = lax.rem(me + 2, 4)
    other_core = me + 1 - 2 * lax.rem(me, 2)
    o_ref[pl.ds(me * rows, rows), :] = x_ref[...]
    barrier = pltpu.get_barrier_semaphore()
    for peer in (other_chip, other_core):
        pl.semaphore_signal(barrier, inc=1, device_id={"rep": peer}, device_id_type=pl.DeviceIdType.MESH)
    pl.semaphore_wait(barrier, 2)
    cross = pltpu.make_async_remote_copy(
        src_ref=x_ref,
        dst_ref=o_ref.at[pl.ds(me * rows, rows)],
        send_sem=send_sem.at[0],
        recv_sem=recv_sem.at[0],
        device_id={"rep": other_chip},
        device_id_type=pl.DeviceIdType.MESH,
    )
    cross.start()
    own = pltpu.make_async_remote_copy(
        src_ref=x_ref,
        dst_ref=o_ref.at[pl.ds(me * rows, rows)],
        send_sem=send_sem.at[1],
        recv_sem=recv_sem.at[1],
        device_id={"rep": other_core},
        device_id_type=pl.DeviceIdType.MESH,
    )
    own.start()
    cross.wait()
    relay = pltpu.make_async_remote_copy(
        src_ref=o_ref.at[pl.ds(other_chip * rows, rows)],
        dst_ref=o_ref.at[pl.ds(other_chip * rows, rows)],
        send_sem=send_sem.at[2],
        recv_sem=recv_sem.at[2],
        device_id={"rep": other_core},
        device_id_type=pl.DeviceIdType.MESH,
    )
    relay.start()
    own.wait()
    relay.wait()


def gather_rep(tensor, cid=1):
    n = lax.axis_size("rep")
    rows, cols = tensor.shape
    return pl.pallas_call(
        rep_gather_kernel,
        out_shape=jax.ShapeDtypeStruct((n * rows, cols), tensor.dtype),
        in_specs=[pl.BlockSpec(memory_space=pltpu.VMEM)],
        out_specs=pl.BlockSpec(memory_space=pltpu.VMEM),
        scratch_shapes=[pltpu.SemaphoreType.DMA((n - 1,)), pltpu.SemaphoreType.DMA((n - 1,))],
        compiler_params=pltpu.CompilerParams(collective_id=cid, has_side_effects=True),
    )(tensor)


def rep_scatter_kernel(p_ref, o_ref, onchip_buf, cross_buf, partial, send_sem, recv_sem):
    me = lax.axis_index("rep")
    rows = o_ref.shape[0]
    other_chip = lax.rem(me + 2, 4)
    other_core = me + 1 - 2 * lax.rem(me, 2)
    diagonal = lax.rem(other_core + 2, 4)
    barrier = pltpu.get_barrier_semaphore()
    for peer in (other_chip, other_core):
        pl.semaphore_signal(barrier, inc=1, device_id={"rep": peer}, device_id_type=pl.DeviceIdType.MESH)
    pl.semaphore_wait(barrier, 2)
    near = []
    for slot, block in ((0, other_core), (1, diagonal)):
        copy = pltpu.make_async_remote_copy(
            src_ref=p_ref.at[pl.ds(block * rows, rows)],
            dst_ref=onchip_buf.at[slot],
            send_sem=send_sem.at[slot],
            recv_sem=recv_sem.at[slot],
            device_id={"rep": other_core},
            device_id_type=pl.DeviceIdType.MESH,
        )
        copy.start()
        near.append(copy)
    for copy in near:
        copy.wait()
    partial[...] = p_ref[pl.ds(other_chip * rows, rows), :] + onchip_buf[1]
    far = pltpu.make_async_remote_copy(
        src_ref=partial,
        dst_ref=cross_buf,
        send_sem=send_sem.at[2],
        recv_sem=recv_sem.at[2],
        device_id={"rep": other_chip},
        device_id_type=pl.DeviceIdType.MESH,
    )
    far.start()
    far.wait()
    o_ref[...] = p_ref[pl.ds(me * rows, rows), :] + onchip_buf[0] + cross_buf[...]


def scatter_rep(tensor, cid=4):
    n = lax.axis_size("rep")
    rows, cols = tensor.shape[0] // n, tensor.shape[1]
    return pl.pallas_call(
        rep_scatter_kernel,
        out_shape=jax.ShapeDtypeStruct((rows, cols), tensor.dtype),
        in_specs=[pl.BlockSpec(memory_space=pltpu.VMEM)],
        out_specs=pl.BlockSpec(memory_space=pltpu.VMEM),
        scratch_shapes=[
            pltpu.VMEM((2, rows, cols), tensor.dtype),
            pltpu.VMEM((rows, cols), tensor.dtype),
            pltpu.VMEM((rows, cols), tensor.dtype),
            pltpu.SemaphoreType.DMA((3,)),
            pltpu.SemaphoreType.DMA((3,)),
        ],
        compiler_params=pltpu.CompilerParams(collective_id=cid, has_side_effects=True),
    )(tensor)


def local(inputs, segment_ids, cotangent, w_qkv, w_out, w_up, w_down, biases, norm_gains, up_bias):
    parts = lax.axis_size("shard")
    reps = lax.axis_size("rep")
    r = lax.axis_index("rep")
    head_cols = D // reps
    heads_here = HEADS // reps
    ff_all = w_up.shape[2]
    ff_chunk = ff_all // parts
    ff_piece = ff_chunk // reps
    k_rows = D // parts

    qkv_piece = pick(w_qkv[0].reshape(k_rows, 3, reps, head_cols), r, 2).reshape(k_rows, -1)
    out_piece = w_out[0]
    up_piece = pick(w_up[0].reshape(k_rows, parts, reps, ff_piece), r, 2).reshape(k_rows, -1)
    down_piece = pick(w_down[0].reshape(reps, ff_piece, D), r, 0)
    upb_piece = pick(up_bias[0].reshape(reps, ff_piece), r, 0)
    small = jnp.concatenate(
        [biases[0].T, norm_gains[0].T, upb_piece[:, None]], axis=1
    )
    small = jnp.pad(small, ((0, 0), (0, 128 - small.shape[1])))
    pieces = (qkv_piece, out_piece, up_piece, down_piece, small)
    widths = [piece.shape[1] for piece in pieces]
    offsets = [sum(widths[:i]) for i in range(len(widths) + 1)]
    gathered = lax.all_gather(jnp.concatenate(pieces, axis=1), "shard", axis=0, tiled=True)
    got = [gathered[:, offsets[i] : offsets[i + 1]] for i in range(len(widths))]
    w_qkv_r = got[0]
    w_out_all = got[1]
    w_out_r = lax.dynamic_slice_in_dim(w_out_all, r * head_cols, head_cols, axis=0)
    w_up_r = got[2]
    w_down_r = got[3]
    n_bias = biases.shape[1]
    n_gain = norm_gains.shape[1]
    bias_all = got[4][:, :n_bias].T
    gain_all = got[4][:, n_bias : n_bias + n_gain].T
    up_bias_r = got[4][:, n_bias + n_gain]
    bias_q = lax.dynamic_slice_in_dim(bias_all[0], r * head_cols, head_cols)
    bias_v = lax.dynamic_slice_in_dim(bias_all[1], r * head_cols, head_cols)

    rows_f32 = inputs[0]
    own = rows_f32.shape[0]
    rows_bf = rows_f32.astype(jnp.bfloat16)
    seg_tag = jnp.broadcast_to(segment_ids[0].astype(jnp.bfloat16)[:, None], (own, 128))
    hb_seg = gather_rep(jnp.concatenate([rows_bf, seg_tag], axis=1), cid=0)
    hb_all = hb_seg[:, :D]
    seg_all = hb_seg[:, D]
    qkv_rows = matmul(hb_all, w_qkv_r)
    queries = (qkv_rows[:, :head_cols] + bias_q).astype(jnp.bfloat16).reshape(1, -1, heads_here, HEAD_DIM)
    keys_all = qkv_rows[:, head_cols : 2 * head_cols].astype(jnp.bfloat16).reshape(1, -1, heads_here, HEAD_DIM)
    values_all = (
        (qkv_rows[:, 2 * head_cols :] + bias_v).astype(jnp.bfloat16).reshape(1, -1, heads_here, HEAD_DIM)
    )
    seg_rows = seg_all[None]
    scores, allowed = attention_scores(queries, keys_all, seg_rows, seg_rows)
    expo_all = jnp.where(allowed, jnp.exp(scores), 0.0)
    row_total = jnp.sum(expo_all, axis=-1, keepdims=True)
    log_total = jnp.log(row_total)
    attn_probs = (expo_all / row_total).astype(jnp.bfloat16)
    context = (
        jnp.einsum("shqk,skhe->sqhe", attn_probs, values_all, preferred_element_type=jnp.float32)
        .astype(jnp.bfloat16)
        .reshape(-1, head_cols)
    )
    first_sum = rows_f32 + scatter_rep(matmul(context, w_out_r)) + bias_all[2]
    context_stack = gather_rep(context, cid=2).reshape(reps, -1, head_cols)
    norm_one, rstd_one = normalize(first_sum)
    mid_norm = norm_one * gain_all[0] + bias_all[3]
    mid_b = mid_norm.astype(jnp.bfloat16)
    mid_all = gather_rep(mid_b)
    pre_act = matmul(mid_all, w_up_r) + up_bias_r
    act_f32, gelu_slope = gelu_pair(pre_act)
    act_b = act_f32.astype(jnp.bfloat16)
    second_sum = mid_norm + scatter_rep(matmul(act_b, w_down_r)) + bias_all[4]
    norm_two, rstd_two = normalize(second_sum)
    layer_out = norm_two * gain_all[1] + bias_all[5]

    grad_rows = cotangent[0]
    d_gain_two = jnp.sum(grad_rows * norm_two, axis=0)
    d_bias_two = jnp.sum(grad_rows, axis=0)
    d_second = norm_back(grad_rows, norm_two, rstd_two, gain_all[1])
    d_bdown = jnp.sum(d_second, axis=0)
    d_second_all = gather_rep(d_second.astype(jnp.bfloat16))
    d_wdown = matmul_lt(act_b, d_second_all)
    d_pre = matmul_rt(d_second_all, w_down_r) * gelu_slope
    d_bup = jnp.sum(d_pre, axis=0)
    d_pre_b = d_pre.astype(jnp.bfloat16)
    d_wup = matmul_lt(mid_all, d_pre_b)
    ffn_pack = jnp.concatenate(
        [d_wup.astype(jnp.bfloat16).reshape(parts, -1), d_wdown.astype(jnp.bfloat16).reshape(parts, -1)],
        axis=1,
    ).reshape(parts, 8, -1)
    ffn_recv = lax.all_to_all(ffn_pack, "shard", 0, 0, tiled=True)
    ffn_share = jnp.sum(ffn_recv.astype(jnp.float32), axis=0).astype(jnp.bfloat16)
    d_mid = d_second + scatter_rep(matmul_rt(d_pre_b, w_up_r))
    d_gain_one = jnp.sum(d_mid * norm_one, axis=0)
    d_bias_one = jnp.sum(d_mid, axis=0)
    d_first = norm_back(d_mid, norm_one, rstd_one, gain_all[0])
    d_bout = jnp.sum(d_first, axis=0)
    d_first_all = gather_rep(d_first.astype(jnp.bfloat16))
    d_first_cols = lax.dynamic_slice_in_dim(d_first_all, r * head_cols, head_cols, axis=1)
    d_wout_cols = jnp.einsum(
        "utc,tk->uck", context_stack, d_first_cols, preferred_element_type=jnp.float32
    ).reshape(D, head_cols)
    d_context = (
        matmul_rt(d_first_all, w_out_r).astype(jnp.bfloat16).reshape(1, -1, heads_here, HEAD_DIM)
    )
    probs_again = jnp.where(allowed, jnp.exp(scores - log_total), 0.0)
    d_probs = jnp.einsum(
        "sqhe,skhe->shqk", d_context, values_all, preferred_element_type=jnp.float32
    )
    d_scores = (
        probs_again
        * (d_probs - jnp.sum(probs_again * d_probs, axis=-1, keepdims=True))
        * (1.0 / math.sqrt(HEAD_DIM))
    ).astype(jnp.bfloat16)
    d_queries = jnp.einsum(
        "shqk,skhe->sqhe", d_scores, keys_all, preferred_element_type=jnp.float32
    ).reshape(-1, head_cols)
    d_keys = jnp.einsum(
        "shqk,sqhe->skhe", d_scores, queries, preferred_element_type=jnp.float32
    ).reshape(-1, head_cols)
    d_values = jnp.einsum(
        "shqk,sqhe->skhe",
        probs_again.astype(jnp.bfloat16),
        d_context,
        preferred_element_type=jnp.float32,
    ).reshape(-1, head_cols)
    d_qkv = jnp.concatenate([d_queries, d_keys, d_values], axis=-1).astype(jnp.bfloat16)
    d_wqkv = matmul_lt(hb_all, d_qkv)
    input_grad = d_first + scatter_rep(matmul_rt(d_qkv, w_qkv_r))

    zeros_cols = jnp.zeros((D,), jnp.float32)
    d_bq = lax.dynamic_update_slice_in_dim(zeros_cols, jnp.sum(d_queries, axis=0), r * head_cols, 0)
    d_bv = lax.dynamic_update_slice_in_dim(zeros_cols, jnp.sum(d_values, axis=0), r * head_cols, 0)
    d_biases = jnp.stack([d_bq, d_bv, d_bout, d_bias_one, d_bdown, d_bias_two])
    d_gains = jnp.stack([d_gain_one, d_gain_two])
    d_bup_all = lax.dynamic_update_slice_in_dim(
        jnp.zeros((parts, reps, ff_piece), jnp.float32), d_bup.reshape(parts, 1, ff_piece), r, 1
    )
    grad_parts = (
        d_wqkv.astype(jnp.bfloat16).reshape(parts, -1),
        d_wout_cols.astype(jnp.bfloat16).reshape(parts, -1),
        d_bup_all.astype(jnp.bfloat16).reshape(parts, -1),
        pack_cols(d_biases.astype(jnp.bfloat16), parts),
        pack_cols(d_gains.astype(jnp.bfloat16), parts),
    )
    g_sizes = [piece.shape[1] for piece in grad_parts]
    grad_pack = jnp.concatenate(grad_parts, axis=1)
    width = grad_pack.shape[1]
    padded = -(-width // 1024) * 1024
    grad_pack = jnp.pad(grad_pack, ((0, 0), (0, padded - width))).reshape(parts, 8, -1)
    received = lax.all_to_all(grad_pack, "shard", 0, 0, tiled=True)
    shares = jnp.sum(received.astype(jnp.float32), axis=0).astype(jnp.bfloat16)
    all_shares = jnp.concatenate([shares.reshape(-1), ffn_share.reshape(-1)])
    joined = lax.all_gather(all_shares, "rep", axis=0, tiled=False).astype(jnp.float32)
    g_sizes = g_sizes + [padded - width, ffn_share.size // 2, ffn_share.size // 2]
    names = ["qkv", "out", "bup", "bias", "gain", "pad", "up", "down"]
    g_offsets = [sum(g_sizes[:i]) for i in range(len(g_sizes) + 1)]
    got = {names[i]: joined[:, g_offsets[i] : g_offsets[i + 1]] for i in range(len(g_sizes))}
    grad_w_qkv = got["qkv"].reshape(reps, k_rows, 3, head_cols).transpose(1, 2, 0, 3).reshape(k_rows, -1)
    grad_w_out = got["out"].reshape(reps, k_rows, head_cols).transpose(1, 0, 2).reshape(k_rows, D)
    grad_w_up = got["up"].reshape(reps, k_rows, parts, ff_piece).transpose(1, 2, 0, 3).reshape(k_rows, -1)
    grad_w_down = got["down"].reshape(reps * ff_piece, D)
    grad_up_bias = jnp.sum(got["bup"], axis=0)
    grad_biases = jnp.sum(got["bias"], axis=0).reshape(biases.shape[1], -1)
    grad_gains = jnp.sum(got["gain"], axis=0).reshape(norm_gains.shape[1], -1)
    return (
        layer_out[None],
        input_grad[None],
        grad_w_qkv[None],
        grad_w_out[None],
        grad_w_up[None],
        grad_w_down[None],
        grad_biases[None],
        grad_gains[None],
        grad_up_bias[None],
    )


def solution(mesh):
    in_specs = (
        P("shard", "rep", None),
        P("shard", "rep"),
        P("shard", "rep", None),
        P(None, "shard", None),
        P(None, "shard", None),
        P(None, "shard", None),
        P(None, "shard", None),
        P(None, None, "shard"),
        P(None, None, "shard"),
        P(None, "shard"),
    )
    out_specs = (
        P("shard", "rep", None),
        P("shard", "rep", None),
        P(None, "shard", None),
        P(None, "shard", None),
        P(None, "shard", None),
        P(None, "shard", None),
        P(None, None, "shard"),
        P(None, None, "shard"),
        P(None, "shard"),
    )
    return jax.shard_map(local, mesh=mesh, in_specs=in_specs, out_specs=out_specs, check_vma=False)
```

```python
import math

import jax
import jax.numpy as jnp
from jax import lax
from jax.experimental import pallas as pl
from jax.experimental.pallas import tpu as pltpu
from jax.sharding import PartitionSpec as P

D = 1024
HEADS = 16
HEAD_DIM = 64
LAYERS = 1


epsilon = 1e-06


def normalize(residual):
    center = residual - jnp.mean(residual, axis=-1, keepdims=True)
    rstd_val = lax.rsqrt(jnp.mean(center * center, axis=-1, keepdims=True) + epsilon)
    return (center * rstd_val, rstd_val)


def norm_back(grad_out, x_hat, rstd_val, gain_row):
    d_hat = grad_out * gain_row
    return rstd_val * (
        d_hat
        - jnp.mean(d_hat, axis=-1, keepdims=True)
        - x_hat * jnp.mean(d_hat * x_hat, axis=-1, keepdims=True)
    )


def gelu_pair(pre_act):
    normal_cdf = 0.5 * (1.0 + lax.erf(pre_act * (1.0 / math.sqrt(2.0))))
    density = jnp.exp(-0.5 * pre_act * pre_act) * (1.0 / math.sqrt(2.0 * math.pi))
    return (pre_act * normal_cdf, normal_cdf + pre_act * density)


def matmul(first_op, second_op):
    return jnp.dot(first_op, second_op, preferred_element_type=jnp.float32)


def matmul_lt(first_op, second_op):
    return lax.dot_general(
        first_op, second_op, (((0,), (0,)), ((), ())), preferred_element_type=jnp.float32
    )


def matmul_rt(first_op, second_op):
    return lax.dot_general(
        first_op, second_op, (((1,), (1,)), ((), ())), preferred_element_type=jnp.float32
    )


def attention_scores(queries, keys_all, seg_rows, seg_cols):
    scores = jnp.einsum(
        "sqhe,skhe->shqk", queries, keys_all, preferred_element_type=jnp.float32
    ) * (1.0 / math.sqrt(HEAD_DIM))
    allowed = seg_rows[:, None, :, None] == seg_cols[:, None, None, :]
    return (scores, allowed)


def pick(tensor, index, axis):
    return lax.dynamic_index_in_dim(tensor, index, axis=axis, keepdims=False)


def pack_cols(tensor, parts):
    rows = tensor.shape[0]
    return tensor.reshape(rows, parts, -1).transpose(1, 0, 2).reshape(parts, -1)


def unpack_cols(flat, parts, rows):
    return flat.reshape(parts, rows, -1).transpose(1, 0, 2).reshape(rows, -1)


def rep_gather_kernel(x_ref, o_ref, send_sem, recv_sem):
    me = lax.axis_index("rep")
    rows = x_ref.shape[0]
    other_chip = lax.rem(me + 2, 4)
    other_core = me + 1 - 2 * lax.rem(me, 2)
    o_ref[pl.ds(me * rows, rows), :] = x_ref[...]
    barrier = pltpu.get_barrier_semaphore()
    for peer in (other_chip, other_core):
        pl.semaphore_signal(barrier, inc=1, device_id={"rep": peer}, device_id_type=pl.DeviceIdType.MESH)
    pl.semaphore_wait(barrier, 2)
    cross = pltpu.make_async_remote_copy(
        src_ref=x_ref,
        dst_ref=o_ref.at[pl.ds(me * rows, rows)],
        send_sem=send_sem.at[0],
        recv_sem=recv_sem.at[0],
        device_id={"rep": other_chip},
        device_id_type=pl.DeviceIdType.MESH,
    )
    cross.start()
    own = pltpu.make_async_remote_copy(
        src_ref=x_ref,
        dst_ref=o_ref.at[pl.ds(me * rows, rows)],
        send_sem=send_sem.at[1],
        recv_sem=recv_sem.at[1],
        device_id={"rep": other_core},
        device_id_type=pl.DeviceIdType.MESH,
    )
    own.start()
    cross.wait()
    relay = pltpu.make_async_remote_copy(
        src_ref=o_ref.at[pl.ds(other_chip * rows, rows)],
        dst_ref=o_ref.at[pl.ds(other_chip * rows, rows)],
        send_sem=send_sem.at[2],
        recv_sem=recv_sem.at[2],
        device_id={"rep": other_core},
        device_id_type=pl.DeviceIdType.MESH,
    )
    relay.start()
    own.wait()
    relay.wait()


def gather_rep(tensor, cid=1):
    n = lax.axis_size("rep")
    rows, cols = tensor.shape
    return pl.pallas_call(
        rep_gather_kernel,
        out_shape=jax.ShapeDtypeStruct((n * rows, cols), tensor.dtype),
        in_specs=[pl.BlockSpec(memory_space=pltpu.VMEM)],
        out_specs=pl.BlockSpec(memory_space=pltpu.VMEM),
        scratch_shapes=[pltpu.SemaphoreType.DMA((n - 1,)), pltpu.SemaphoreType.DMA((n - 1,))],
        compiler_params=pltpu.CompilerParams(collective_id=cid, has_side_effects=True),
    )(tensor)


def rep_scatter_kernel(p_ref, o_ref, onchip_buf, cross_buf, partial, send_sem, recv_sem):
    me = lax.axis_index("rep")
    rows = o_ref.shape[0]
    other_chip = lax.rem(me + 2, 4)
    other_core = me + 1 - 2 * lax.rem(me, 2)
    diagonal = lax.rem(other_core + 2, 4)
    barrier = pltpu.get_barrier_semaphore()
    for peer in (other_chip, other_core):
        pl.semaphore_signal(barrier, inc=1, device_id={"rep": peer}, device_id_type=pl.DeviceIdType.MESH)
    pl.semaphore_wait(barrier, 2)
    near = []
    for slot, block in ((0, other_core), (1, diagonal)):
        copy = pltpu.make_async_remote_copy(
            src_ref=p_ref.at[pl.ds(block * rows, rows)],
            dst_ref=onchip_buf.at[slot],
            send_sem=send_sem.at[slot],
            recv_sem=recv_sem.at[slot],
            device_id={"rep": other_core},
            device_id_type=pl.DeviceIdType.MESH,
        )
        copy.start()
        near.append(copy)
    for copy in near:
        copy.wait()
    partial[...] = p_ref[pl.ds(other_chip * rows, rows), :] + onchip_buf[1]
    far = pltpu.make_async_remote_copy(
        src_ref=partial,
        dst_ref=cross_buf,
        send_sem=send_sem.at[2],
        recv_sem=recv_sem.at[2],
        device_id={"rep": other_chip},
        device_id_type=pl.DeviceIdType.MESH,
    )
    far.start()
    far.wait()
    o_ref[...] = p_ref[pl.ds(me * rows, rows), :] + onchip_buf[0] + cross_buf[...]


def scatter_rep(tensor, cid=4):
    n = lax.axis_size("rep")
    rows, cols = tensor.shape[0] // n, tensor.shape[1]
    return pl.pallas_call(
        rep_scatter_kernel,
        out_shape=jax.ShapeDtypeStruct((rows, cols), tensor.dtype),
        in_specs=[pl.BlockSpec(memory_space=pltpu.VMEM)],
        out_specs=pl.BlockSpec(memory_space=pltpu.VMEM),
        scratch_shapes=[
            pltpu.VMEM((2, rows, cols), tensor.dtype),
            pltpu.VMEM((rows, cols), tensor.dtype),
            pltpu.VMEM((rows, cols), tensor.dtype),
            pltpu.SemaphoreType.DMA((3,)),
            pltpu.SemaphoreType.DMA((3,)),
        ],
        compiler_params=pltpu.CompilerParams(collective_id=cid, has_side_effects=True),
    )(tensor)


def local(inputs, segment_ids, cotangent, w_qkv, w_out, w_up, w_down, biases, norm_gains, up_bias):
    parts = lax.axis_size("shard")
    reps = lax.axis_size("rep")
    r = lax.axis_index("rep")
    head_cols = D // reps
    heads_here = HEADS // reps
    ff_all = w_up.shape[2]
    ff_chunk = ff_all // parts
    ff_piece = ff_chunk // reps
    k_rows = D // parts

    qkv_piece = pick(w_qkv[0].reshape(k_rows, 3, reps, head_cols), r, 2).reshape(k_rows, -1)
    out_piece = w_out[0]
    up_piece = pick(w_up[0].reshape(k_rows, parts, reps, ff_piece), r, 2).reshape(k_rows, -1)
    down_piece = pick(w_down[0].reshape(reps, ff_piece, D), r, 0)
    upb_piece = pick(up_bias[0].reshape(reps, ff_piece), r, 0)
    small = jnp.concatenate(
        [biases[0].T, norm_gains[0].T, upb_piece[:, None]], axis=1
    )
    small = jnp.pad(small, ((0, 0), (0, 128 - small.shape[1])))
    pieces = (qkv_piece, out_piece, up_piece, down_piece, small)
    widths = [piece.shape[1] for piece in pieces]
    offsets = [sum(widths[:i]) for i in range(len(widths) + 1)]
    gathered = lax.all_gather(jnp.concatenate(pieces, axis=1), "shard", axis=0, tiled=True)
    got = [gathered[:, offsets[i] : offsets[i + 1]] for i in range(len(widths))]
    w_qkv_r = got[0]
    w_out_all = got[1]
    w_out_r = lax.dynamic_slice_in_dim(w_out_all, r * head_cols, head_cols, axis=0)
    w_up_r = got[2]
    w_down_r = got[3]
    n_bias = biases.shape[1]
    n_gain = norm_gains.shape[1]
    bias_all = got[4][:, :n_bias].T
    gain_all = got[4][:, n_bias : n_bias + n_gain].T
    up_bias_r = got[4][:, n_bias + n_gain]
    bias_q = lax.dynamic_slice_in_dim(bias_all[0], r * head_cols, head_cols)
    bias_v = lax.dynamic_slice_in_dim(bias_all[1], r * head_cols, head_cols)

    rows_f32 = inputs[0]
    own = rows_f32.shape[0]
    rows_bf = rows_f32.astype(jnp.bfloat16)
    seg_tag = jnp.broadcast_to(segment_ids[0].astype(jnp.bfloat16)[:, None], (own, 128))
    hb_seg = gather_rep(jnp.concatenate([rows_bf, seg_tag], axis=1), cid=0)
    hb_all = hb_seg[:, :D]
    seg_all = hb_seg[:, D]
    qkv_rows = matmul(hb_all, w_qkv_r)
    queries = (qkv_rows[:, :head_cols] + bias_q).astype(jnp.bfloat16).reshape(1, -1, heads_here, HEAD_DIM)
    keys_all = qkv_rows[:, head_cols : 2 * head_cols].astype(jnp.bfloat16).reshape(1, -1, heads_here, HEAD_DIM)
    values_all = (
        (qkv_rows[:, 2 * head_cols :] + bias_v).astype(jnp.bfloat16).reshape(1, -1, heads_here, HEAD_DIM)
    )
    seg_rows = seg_all[None]
    scores, allowed = attention_scores(queries, keys_all, seg_rows, seg_rows)
    expo_all = jnp.where(allowed, jnp.exp(scores), 0.0)
    row_total = jnp.sum(expo_all, axis=-1, keepdims=True)
    log_total = jnp.log(row_total)
    attn_probs = (expo_all / row_total).astype(jnp.bfloat16)
    context = (
        jnp.einsum("shqk,skhe->sqhe", attn_probs, values_all, preferred_element_type=jnp.float32)
        .astype(jnp.bfloat16)
        .reshape(-1, head_cols)
    )
    first_sum = rows_f32 + scatter_rep(matmul(context, w_out_r)) + bias_all[2]
    context_stack = gather_rep(context, cid=2).reshape(reps, -1, head_cols)
    norm_one, rstd_one = normalize(first_sum)
    mid_norm = norm_one * gain_all[0] + bias_all[3]
    mid_b = mid_norm.astype(jnp.bfloat16)
    mid_all = gather_rep(mid_b)
    pre_act = matmul(mid_all, w_up_r) + up_bias_r
    act_f32, gelu_slope = gelu_pair(pre_act)
    act_b = act_f32.astype(jnp.bfloat16)
    second_sum = mid_norm + scatter_rep(matmul(act_b, w_down_r)) + bias_all[4]
    norm_two, rstd_two = normalize(second_sum)
    layer_out = norm_two * gain_all[1] + bias_all[5]

    grad_rows = cotangent[0]
    d_gain_two = jnp.sum(grad_rows * norm_two, axis=0)
    d_bias_two = jnp.sum(grad_rows, axis=0)
    d_second = norm_back(grad_rows, norm_two, rstd_two, gain_all[1])
    d_bdown = jnp.sum(d_second, axis=0)
    d_second_all = gather_rep(d_second.astype(jnp.bfloat16))
    d_wdown = matmul_lt(act_b, d_second_all)
    d_pre = matmul_rt(d_second_all, w_down_r) * gelu_slope
    d_bup = jnp.sum(d_pre, axis=0)
    d_pre_b = d_pre.astype(jnp.bfloat16)
    d_wup = matmul_lt(mid_all, d_pre_b)
    ffn_block = jnp.concatenate([d_wup.astype(jnp.bfloat16), d_wdown.astype(jnp.bfloat16)], axis=1)
    ffn_recv = lax.all_to_all(ffn_block, "shard", 0, 0, tiled=True)
    ffn_share = jnp.sum(ffn_recv.astype(jnp.float32).reshape(parts, k_rows, -1), axis=0).astype(jnp.bfloat16)
    d_mid = d_second + scatter_rep(matmul_rt(d_pre_b, w_up_r))
    d_gain_one = jnp.sum(d_mid * norm_one, axis=0)
    d_bias_one = jnp.sum(d_mid, axis=0)
    d_first = norm_back(d_mid, norm_one, rstd_one, gain_all[0])
    d_bout = jnp.sum(d_first, axis=0)
    d_first_all = gather_rep(d_first.astype(jnp.bfloat16))
    d_first_cols = lax.dynamic_slice_in_dim(d_first_all, r * head_cols, head_cols, axis=1)
    d_wout_cols = jnp.einsum(
        "utc,tk->uck", context_stack, d_first_cols, preferred_element_type=jnp.float32
    ).reshape(D, head_cols)
    d_context = (
        matmul_rt(d_first_all, w_out_r).astype(jnp.bfloat16).reshape(1, -1, heads_here, HEAD_DIM)
    )
    probs_again = jnp.where(allowed, jnp.exp(scores - log_total), 0.0)
    d_probs = jnp.einsum(
        "sqhe,skhe->shqk", d_context, values_all, preferred_element_type=jnp.float32
    )
    d_scores = (
        probs_again
        * (d_probs - jnp.sum(probs_again * d_probs, axis=-1, keepdims=True))
        * (1.0 / math.sqrt(HEAD_DIM))
    ).astype(jnp.bfloat16)
    d_queries = jnp.einsum(
        "shqk,skhe->sqhe", d_scores, keys_all, preferred_element_type=jnp.float32
    ).reshape(-1, head_cols)
    d_keys = jnp.einsum(
        "shqk,sqhe->skhe", d_scores, queries, preferred_element_type=jnp.float32
    ).reshape(-1, head_cols)
    d_values = jnp.einsum(
        "shqk,sqhe->skhe",
        probs_again.astype(jnp.bfloat16),
        d_context,
        preferred_element_type=jnp.float32,
    ).reshape(-1, head_cols)
    d_qkv = jnp.concatenate([d_queries, d_keys, d_values], axis=-1).astype(jnp.bfloat16)
    d_wqkv = matmul_lt(hb_all, d_qkv)
    input_grad = d_first + scatter_rep(matmul_rt(d_qkv, w_qkv_r))

    zeros_cols = jnp.zeros((D,), jnp.float32)
    d_bq = lax.dynamic_update_slice_in_dim(zeros_cols, jnp.sum(d_queries, axis=0), r * head_cols, 0)
    d_bv = lax.dynamic_update_slice_in_dim(zeros_cols, jnp.sum(d_values, axis=0), r * head_cols, 0)
    d_biases = jnp.stack([d_bq, d_bv, d_bout, d_bias_one, d_bdown, d_bias_two])
    d_gains = jnp.stack([d_gain_one, d_gain_two])
    n_bias = biases.shape[1]
    n_gain = norm_gains.shape[1]
    small = jnp.concatenate([d_biases.T, d_gains.T, d_bup[:, None]], axis=1)
    small = jnp.pad(small, ((0, 0), (0, 128 - small.shape[1])))
    attn_block = jnp.concatenate(
        [d_wqkv.astype(jnp.bfloat16), d_wout_cols.astype(jnp.bfloat16), small.astype(jnp.bfloat16)], axis=1
    )
    attn_recv = lax.all_to_all(attn_block, "shard", 0, 0, tiled=True)
    attn_share = jnp.sum(attn_recv.astype(jnp.float32).reshape(parts, k_rows, -1), axis=0).astype(jnp.bfloat16)
    all_shares = jnp.concatenate([attn_share, ffn_share], axis=1)
    joined = lax.all_gather(all_shares, "rep", axis=0, tiled=False).astype(jnp.float32)
    qkv_w = 3 * head_cols
    grad_w_qkv = (
        joined[:, :, :qkv_w].reshape(reps, k_rows, 3, head_cols).transpose(1, 2, 0, 3).reshape(k_rows, -1)
    )
    grad_w_out = joined[:, :, qkv_w : qkv_w + head_cols].transpose(1, 0, 2).reshape(k_rows, D)
    base = qkv_w + head_cols
    small_all = joined[:, :, base : base + 128]
    grad_biases = jnp.sum(small_all[:, :, :n_bias], axis=0).T
    grad_gains = jnp.sum(small_all[:, :, n_bias : n_bias + n_gain], axis=0).T
    grad_up_bias = small_all[:, :, n_bias + n_gain].reshape(-1)
    base = base + 128
    ff_cols = w_up_r.shape[1]
    grad_w_up = (
        joined[:, :, base : base + ff_cols]
        .reshape(reps, k_rows, parts, ff_piece)
        .transpose(1, 2, 0, 3)
        .reshape(k_rows, -1)
    )
    grad_w_down = joined[:, :, base + ff_cols :].reshape(reps * ff_piece, D)
    return (
        layer_out[None],
        input_grad[None],
        grad_w_qkv[None],
        grad_w_out[None],
        grad_w_up[None],
        grad_w_down[None],
        grad_biases[None],
        grad_gains[None],
        grad_up_bias[None],
    )


def solution(mesh):
    in_specs = (
        P("shard", "rep", None),
        P("shard", "rep"),
        P("shard", "rep", None),
        P(None, "shard", None),
        P(None, "shard", None),
        P(None, "shard", None),
        P(None, "shard", None),
        P(None, None, "shard"),
        P(None, None, "shard"),
        P(None, "shard"),
    )
    out_specs = (
        P("shard", "rep", None),
        P("shard", "rep", None),
        P(None, "shard", None),
        P(None, "shard", None),
        P(None, "shard", None),
        P(None, "shard", None),
        P(None, None, "shard"),
        P(None, None, "shard"),
        P(None, "shard"),
    )
    return jax.shard_map(local, mesh=mesh, in_specs=in_specs, out_specs=out_specs, check_vma=False)
```

```python
import math

import jax
import jax.numpy as jnp
from jax import lax
from jax.experimental import pallas as pl
from jax.experimental.pallas import tpu as pltpu
from jax.sharding import PartitionSpec as P

D = 1024
HEADS = 16
HEAD_DIM = 64
LAYERS = 1


epsilon = 1e-06


def normalize(residual):
    center = residual - jnp.mean(residual, axis=-1, keepdims=True)
    rstd_val = lax.rsqrt(jnp.mean(center * center, axis=-1, keepdims=True) + epsilon)
    return (center * rstd_val, rstd_val)


def norm_back(grad_out, x_hat, rstd_val, gain_row):
    d_hat = grad_out * gain_row
    return rstd_val * (
        d_hat
        - jnp.mean(d_hat, axis=-1, keepdims=True)
        - x_hat * jnp.mean(d_hat * x_hat, axis=-1, keepdims=True)
    )


def gelu_pair(pre_act):
    normal_cdf = 0.5 * (1.0 + lax.erf(pre_act * (1.0 / math.sqrt(2.0))))
    density = jnp.exp(-0.5 * pre_act * pre_act) * (1.0 / math.sqrt(2.0 * math.pi))
    return (pre_act * normal_cdf, normal_cdf + pre_act * density)


def matmul(first_op, second_op):
    return jnp.dot(first_op, second_op, preferred_element_type=jnp.float32)


def matmul_lt(first_op, second_op):
    return lax.dot_general(
        first_op, second_op, (((0,), (0,)), ((), ())), preferred_element_type=jnp.float32
    )


def matmul_rt(first_op, second_op):
    return lax.dot_general(
        first_op, second_op, (((1,), (1,)), ((), ())), preferred_element_type=jnp.float32
    )


def attention_scores(queries, keys_all, seg_rows, seg_cols):
    scores = jnp.einsum(
        "sqhe,skhe->shqk", queries, keys_all, preferred_element_type=jnp.float32
    ) * (1.0 / math.sqrt(HEAD_DIM))
    allowed = seg_rows[:, None, :, None] == seg_cols[:, None, None, :]
    return (scores, allowed)


def pick(tensor, index, axis):
    return lax.dynamic_index_in_dim(tensor, index, axis=axis, keepdims=False)


def pack_cols(tensor, parts):
    rows = tensor.shape[0]
    return tensor.reshape(rows, parts, -1).transpose(1, 0, 2).reshape(parts, -1)


def unpack_cols(flat, parts, rows):
    return flat.reshape(parts, rows, -1).transpose(1, 0, 2).reshape(rows, -1)


def rep_gather_kernel(x_ref, o_ref, send_sem, recv_sem):
    me = lax.axis_index("rep")
    rows = x_ref.shape[0]
    other_chip = lax.rem(me + 2, 4)
    other_core = me + 1 - 2 * lax.rem(me, 2)
    o_ref[pl.ds(me * rows, rows), :] = x_ref[...]
    barrier = pltpu.get_barrier_semaphore()
    for peer in (other_chip, other_core):
        pl.semaphore_signal(barrier, inc=1, device_id={"rep": peer}, device_id_type=pl.DeviceIdType.MESH)
    pl.semaphore_wait(barrier, 2)
    cross = pltpu.make_async_remote_copy(
        src_ref=x_ref,
        dst_ref=o_ref.at[pl.ds(me * rows, rows)],
        send_sem=send_sem.at[0],
        recv_sem=recv_sem.at[0],
        device_id={"rep": other_chip},
        device_id_type=pl.DeviceIdType.MESH,
    )
    cross.start()
    own = pltpu.make_async_remote_copy(
        src_ref=x_ref,
        dst_ref=o_ref.at[pl.ds(me * rows, rows)],
        send_sem=send_sem.at[1],
        recv_sem=recv_sem.at[1],
        device_id={"rep": other_core},
        device_id_type=pl.DeviceIdType.MESH,
    )
    own.start()
    cross.wait()
    relay = pltpu.make_async_remote_copy(
        src_ref=o_ref.at[pl.ds(other_chip * rows, rows)],
        dst_ref=o_ref.at[pl.ds(other_chip * rows, rows)],
        send_sem=send_sem.at[2],
        recv_sem=recv_sem.at[2],
        device_id={"rep": other_core},
        device_id_type=pl.DeviceIdType.MESH,
    )
    relay.start()
    own.wait()
    relay.wait()


def gather_rep(tensor, cid=1):
    n = lax.axis_size("rep")
    rows, cols = tensor.shape
    return pl.pallas_call(
        rep_gather_kernel,
        out_shape=jax.ShapeDtypeStruct((n * rows, cols), tensor.dtype),
        in_specs=[pl.BlockSpec(memory_space=pltpu.VMEM)],
        out_specs=pl.BlockSpec(memory_space=pltpu.VMEM),
        scratch_shapes=[pltpu.SemaphoreType.DMA((n - 1,)), pltpu.SemaphoreType.DMA((n - 1,))],
        compiler_params=pltpu.CompilerParams(collective_id=cid, has_side_effects=True),
    )(tensor)


def rep_scatter_kernel(p_ref, o_ref, onchip_buf, cross_buf, partial, send_sem, recv_sem):
    me = lax.axis_index("rep")
    rows = o_ref.shape[0]
    other_chip = lax.rem(me + 2, 4)
    other_core = me + 1 - 2 * lax.rem(me, 2)
    diagonal = lax.rem(other_core + 2, 4)
    barrier = pltpu.get_barrier_semaphore()
    for peer in (other_chip, other_core):
        pl.semaphore_signal(barrier, inc=1, device_id={"rep": peer}, device_id_type=pl.DeviceIdType.MESH)
    pl.semaphore_wait(barrier, 2)
    near = []
    for slot, block in ((0, other_core), (1, diagonal)):
        copy = pltpu.make_async_remote_copy(
            src_ref=p_ref.at[pl.ds(block * rows, rows)],
            dst_ref=onchip_buf.at[slot],
            send_sem=send_sem.at[slot],
            recv_sem=recv_sem.at[slot],
            device_id={"rep": other_core},
            device_id_type=pl.DeviceIdType.MESH,
        )
        copy.start()
        near.append(copy)
    for copy in near:
        copy.wait()
    partial[...] = p_ref[pl.ds(other_chip * rows, rows), :] + onchip_buf[1]
    far = pltpu.make_async_remote_copy(
        src_ref=partial,
        dst_ref=cross_buf,
        send_sem=send_sem.at[2],
        recv_sem=recv_sem.at[2],
        device_id={"rep": other_chip},
        device_id_type=pl.DeviceIdType.MESH,
    )
    far.start()
    far.wait()
    o_ref[...] = p_ref[pl.ds(me * rows, rows), :] + onchip_buf[0] + cross_buf[...]


def scatter_rep(tensor, cid=4):
    n = lax.axis_size("rep")
    rows, cols = tensor.shape[0] // n, tensor.shape[1]
    return pl.pallas_call(
        rep_scatter_kernel,
        out_shape=jax.ShapeDtypeStruct((rows, cols), tensor.dtype),
        in_specs=[pl.BlockSpec(memory_space=pltpu.VMEM)],
        out_specs=pl.BlockSpec(memory_space=pltpu.VMEM),
        scratch_shapes=[
            pltpu.VMEM((2, rows, cols), tensor.dtype),
            pltpu.VMEM((rows, cols), tensor.dtype),
            pltpu.VMEM((rows, cols), tensor.dtype),
            pltpu.SemaphoreType.DMA((3,)),
            pltpu.SemaphoreType.DMA((3,)),
        ],
        compiler_params=pltpu.CompilerParams(collective_id=cid, has_side_effects=True),
    )(tensor)


def local(inputs, segment_ids, cotangent, w_qkv, w_out, w_up, w_down, biases, norm_gains, up_bias):
    parts = lax.axis_size("shard")
    reps = lax.axis_size("rep")
    r = lax.axis_index("rep")
    head_cols = D // reps
    heads_here = HEADS // reps
    ff_all = w_up.shape[2]
    ff_chunk = ff_all // parts
    ff_piece = ff_chunk // reps
    k_rows = D // parts

    qkv_piece = pick(w_qkv[0].reshape(k_rows, 3, reps, head_cols), r, 2).reshape(k_rows, -1)
    out_piece = w_out[0]
    up_piece = pick(w_up[0].reshape(k_rows, parts, reps, ff_piece), r, 2).reshape(k_rows, -1)
    down_piece = pick(w_down[0].reshape(reps, ff_piece, D), r, 0)
    upb_piece = pick(up_bias[0].reshape(reps, ff_piece), r, 0)
    small = jnp.concatenate(
        [biases[0].T, norm_gains[0].T, upb_piece[:, None]], axis=1
    )
    small = jnp.pad(small, ((0, 0), (0, 128 - small.shape[1])))
    pieces = (qkv_piece, out_piece, up_piece, down_piece, small)
    widths = [piece.shape[1] for piece in pieces]
    offsets = [sum(widths[:i]) for i in range(len(widths) + 1)]
    gathered = lax.all_gather(jnp.concatenate(pieces, axis=1), "shard", axis=0, tiled=True)
    got = [gathered[:, offsets[i] : offsets[i + 1]] for i in range(len(widths))]
    w_qkv_r = got[0]
    w_out_all = got[1]
    w_out_r = lax.dynamic_slice_in_dim(w_out_all, r * head_cols, head_cols, axis=0)
    w_up_r = got[2]
    w_down_r = got[3]
    n_bias = biases.shape[1]
    n_gain = norm_gains.shape[1]
    bias_all = got[4][:, :n_bias].T
    gain_all = got[4][:, n_bias : n_bias + n_gain].T
    up_bias_r = got[4][:, n_bias + n_gain]
    bias_q = lax.dynamic_slice_in_dim(bias_all[0], r * head_cols, head_cols)
    bias_v = lax.dynamic_slice_in_dim(bias_all[1], r * head_cols, head_cols)

    rows_f32 = inputs[0]
    own = rows_f32.shape[0]
    rows_bf = rows_f32.astype(jnp.bfloat16)
    seg_tag = jnp.broadcast_to(segment_ids[0].astype(jnp.bfloat16)[:, None], (own, 128))
    hb_seg = gather_rep(jnp.concatenate([rows_bf, seg_tag], axis=1), cid=0)
    hb_all = hb_seg[:, :D]
    seg_all = hb_seg[:, D]
    qkv_rows = matmul(hb_all, w_qkv_r)
    queries = (qkv_rows[:, :head_cols] + bias_q).astype(jnp.bfloat16).reshape(1, -1, heads_here, HEAD_DIM)
    keys_all = qkv_rows[:, head_cols : 2 * head_cols].astype(jnp.bfloat16).reshape(1, -1, heads_here, HEAD_DIM)
    values_all = (
        (qkv_rows[:, 2 * head_cols :] + bias_v).astype(jnp.bfloat16).reshape(1, -1, heads_here, HEAD_DIM)
    )
    seg_rows = seg_all[None]
    scores, allowed = attention_scores(queries, keys_all, seg_rows, seg_rows)
    expo_all = jnp.where(allowed, jnp.exp(scores), 0.0)
    row_total = jnp.sum(expo_all, axis=-1, keepdims=True)
    log_total = jnp.log(row_total)
    attn_probs = (expo_all / row_total).astype(jnp.bfloat16)
    context = (
        jnp.einsum("shqk,skhe->sqhe", attn_probs, values_all, preferred_element_type=jnp.float32)
        .astype(jnp.bfloat16)
        .reshape(-1, head_cols)
    )
    first_sum = rows_f32 + scatter_rep(matmul(context, w_out_r)) + bias_all[2]
    context_stack = gather_rep(context, cid=2).reshape(reps, -1, head_cols)
    norm_one, rstd_one = normalize(first_sum)
    mid_norm = norm_one * gain_all[0] + bias_all[3]
    mid_b = mid_norm.astype(jnp.bfloat16)
    mid_all = gather_rep(mid_b)
    pre_act = matmul(mid_all, w_up_r) + up_bias_r
    act_f32, gelu_slope = gelu_pair(pre_act)
    act_b = act_f32.astype(jnp.bfloat16)
    second_sum = mid_norm + scatter_rep(matmul(act_b, w_down_r)) + bias_all[4]
    norm_two, rstd_two = normalize(second_sum)
    layer_out = norm_two * gain_all[1] + bias_all[5]

    grad_rows = cotangent[0]
    d_gain_two = jnp.sum(grad_rows * norm_two, axis=0)
    d_bias_two = jnp.sum(grad_rows, axis=0)
    d_second = norm_back(grad_rows, norm_two, rstd_two, gain_all[1])
    d_bdown = jnp.sum(d_second, axis=0)
    d_second_all = gather_rep(d_second.astype(jnp.bfloat16))
    d_wdown = matmul_lt(act_b, d_second_all)
    d_pre = matmul_rt(d_second_all, w_down_r) * gelu_slope
    d_bup = jnp.sum(d_pre, axis=0)
    d_pre_b = d_pre.astype(jnp.bfloat16)
    d_wup = matmul_lt(mid_all, d_pre_b)
    ffn_pack = jnp.concatenate(
        [d_wup.astype(jnp.bfloat16).reshape(parts, -1), d_wdown.astype(jnp.bfloat16).reshape(parts, -1)],
        axis=1,
    ).reshape(parts, 8, -1)
    ffn_recv = lax.all_to_all(ffn_pack, "shard", 0, 0, tiled=True)
    ffn_share = jnp.sum(ffn_recv.astype(jnp.float32), axis=0).astype(jnp.bfloat16)
    d_mid = d_second + scatter_rep(matmul_rt(d_pre_b, w_up_r))
    d_gain_one = jnp.sum(d_mid * norm_one, axis=0)
    d_bias_one = jnp.sum(d_mid, axis=0)
    d_first = norm_back(d_mid, norm_one, rstd_one, gain_all[0])
    d_bout = jnp.sum(d_first, axis=0)
    d_first, ffn_share = lax.optimization_barrier((d_first, ffn_share))
    d_first_all = gather_rep(d_first.astype(jnp.bfloat16))
    d_first_cols = lax.dynamic_slice_in_dim(d_first_all, r * head_cols, head_cols, axis=1)
    d_wout_cols = jnp.einsum(
        "utc,tk->uck", context_stack, d_first_cols, preferred_element_type=jnp.float32
    ).reshape(D, head_cols)
    d_context = (
        matmul_rt(d_first_all, w_out_r).astype(jnp.bfloat16).reshape(1, -1, heads_here, HEAD_DIM)
    )
    probs_again = jnp.where(allowed, jnp.exp(scores - log_total), 0.0)
    d_probs = jnp.einsum(
        "sqhe,skhe->shqk", d_context, values_all, preferred_element_type=jnp.float32
    )
    d_scores = (
        probs_again
        * (d_probs - jnp.sum(probs_again * d_probs, axis=-1, keepdims=True))
        * (1.0 / math.sqrt(HEAD_DIM))
    ).astype(jnp.bfloat16)
    d_queries = jnp.einsum(
        "shqk,skhe->sqhe", d_scores, keys_all, preferred_element_type=jnp.float32
    ).reshape(-1, head_cols)
    d_keys = jnp.einsum(
        "shqk,sqhe->skhe", d_scores, queries, preferred_element_type=jnp.float32
    ).reshape(-1, head_cols)
    d_values = jnp.einsum(
        "shqk,sqhe->skhe",
        probs_again.astype(jnp.bfloat16),
        d_context,
        preferred_element_type=jnp.float32,
    ).reshape(-1, head_cols)
    d_qkv = jnp.concatenate([d_queries, d_keys, d_values], axis=-1).astype(jnp.bfloat16)
    d_wqkv = matmul_lt(hb_all, d_qkv)
    input_grad = d_first + scatter_rep(matmul_rt(d_qkv, w_qkv_r))

    zeros_cols = jnp.zeros((D,), jnp.float32)
    d_bq = lax.dynamic_update_slice_in_dim(zeros_cols, jnp.sum(d_queries, axis=0), r * head_cols, 0)
    d_bv = lax.dynamic_update_slice_in_dim(zeros_cols, jnp.sum(d_values, axis=0), r * head_cols, 0)
    d_biases = jnp.stack([d_bq, d_bv, d_bout, d_bias_one, d_bdown, d_bias_two])
    d_gains = jnp.stack([d_gain_one, d_gain_two])
    d_bup_all = lax.dynamic_update_slice_in_dim(
        jnp.zeros((parts, reps, ff_piece), jnp.float32), d_bup.reshape(parts, 1, ff_piece), r, 1
    )
    grad_parts = (
        d_wqkv.astype(jnp.bfloat16).reshape(parts, -1),
        d_wout_cols.astype(jnp.bfloat16).reshape(parts, -1),
        d_bup_all.astype(jnp.bfloat16).reshape(parts, -1),
        pack_cols(d_biases.astype(jnp.bfloat16), parts),
        pack_cols(d_gains.astype(jnp.bfloat16), parts),
    )
    g_sizes = [piece.shape[1] for piece in grad_parts]
    grad_pack = jnp.concatenate(grad_parts, axis=1)
    width = grad_pack.shape[1]
    padded = -(-width // 1024) * 1024
    grad_pack = jnp.pad(grad_pack, ((0, 0), (0, padded - width))).reshape(parts, 8, -1)
    received = lax.all_to_all(grad_pack, "shard", 0, 0, tiled=True)
    shares = jnp.sum(received.astype(jnp.float32), axis=0).astype(jnp.bfloat16)
    all_shares = jnp.concatenate([shares.reshape(-1), ffn_share.reshape(-1)])
    joined = lax.all_gather(all_shares, "rep", axis=0, tiled=False).astype(jnp.float32)
    g_sizes = g_sizes + [padded - width, ffn_share.size // 2, ffn_share.size // 2]
    names = ["qkv", "out", "bup", "bias", "gain", "pad", "up", "down"]
    g_offsets = [sum(g_sizes[:i]) for i in range(len(g_sizes) + 1)]
    got = {names[i]: joined[:, g_offsets[i] : g_offsets[i + 1]] for i in range(len(g_sizes))}
    grad_w_qkv = got["qkv"].reshape(reps, k_rows, 3, head_cols).transpose(1, 2, 0, 3).reshape(k_rows, -1)
    grad_w_out = got["out"].reshape(reps, k_rows, head_cols).transpose(1, 0, 2).reshape(k_rows, D)
    grad_w_up = got["up"].reshape(reps, k_rows, parts, ff_piece).transpose(1, 2, 0, 3).reshape(k_rows, -1)
    grad_w_down = got["down"].reshape(reps * ff_piece, D)
    grad_up_bias = jnp.sum(got["bup"], axis=0)
    grad_biases = jnp.sum(got["bias"], axis=0).reshape(biases.shape[1], -1)
    grad_gains = jnp.sum(got["gain"], axis=0).reshape(norm_gains.shape[1], -1)
    return (
        layer_out[None],
        input_grad[None],
        grad_w_qkv[None],
        grad_w_out[None],
        grad_w_up[None],
        grad_w_down[None],
        grad_biases[None],
        grad_gains[None],
        grad_up_bias[None],
    )


def solution(mesh):
    in_specs = (
        P("shard", "rep", None),
        P("shard", "rep"),
        P("shard", "rep", None),
        P(None, "shard", None),
        P(None, "shard", None),
        P(None, "shard", None),
        P(None, "shard", None),
        P(None, None, "shard"),
        P(None, None, "shard"),
        P(None, "shard"),
    )
    out_specs = (
        P("shard", "rep", None),
        P("shard", "rep", None),
        P(None, "shard", None),
        P(None, "shard", None),
        P(None, "shard", None),
        P(None, "shard", None),
        P(None, None, "shard"),
        P(None, None, "shard"),
        P(None, "shard"),
    )
    return jax.shard_map(local, mesh=mesh, in_specs=in_specs, out_specs=out_specs, check_vma=False)
```

```python
import math

import jax
import jax.numpy as jnp
from jax import lax
from jax.experimental import pallas as pl
from jax.experimental.pallas import tpu as pltpu
from jax.sharding import PartitionSpec as P

D = 1024
HEADS = 16
HEAD_DIM = 64
LAYERS = 1


epsilon = 1e-06


def normalize(residual):
    center = residual - jnp.mean(residual, axis=-1, keepdims=True)
    rstd_val = lax.rsqrt(jnp.mean(center * center, axis=-1, keepdims=True) + epsilon)
    return (center * rstd_val, rstd_val)


def norm_back(grad_out, x_hat, rstd_val, gain_row):
    d_hat = grad_out * gain_row
    return rstd_val * (
        d_hat
        - jnp.mean(d_hat, axis=-1, keepdims=True)
        - x_hat * jnp.mean(d_hat * x_hat, axis=-1, keepdims=True)
    )


def gelu_pair(pre_act):
    normal_cdf = 0.5 * (1.0 + lax.erf(pre_act * (1.0 / math.sqrt(2.0))))
    density = jnp.exp(-0.5 * pre_act * pre_act) * (1.0 / math.sqrt(2.0 * math.pi))
    return (pre_act * normal_cdf, normal_cdf + pre_act * density)


def matmul(first_op, second_op):
    return jnp.dot(first_op, second_op, preferred_element_type=jnp.float32)


def matmul_lt(first_op, second_op):
    return lax.dot_general(
        first_op, second_op, (((0,), (0,)), ((), ())), preferred_element_type=jnp.float32
    )


def matmul_rt(first_op, second_op):
    return lax.dot_general(
        first_op, second_op, (((1,), (1,)), ((), ())), preferred_element_type=jnp.float32
    )


def attention_scores(queries, keys_all, seg_rows, seg_cols):
    scores = jnp.einsum(
        "sqhe,skhe->shqk", queries, keys_all, preferred_element_type=jnp.float32
    ) * (1.0 / math.sqrt(HEAD_DIM))
    allowed = seg_rows[:, None, :, None] == seg_cols[:, None, None, :]
    return (scores, allowed)


def pick(tensor, index, axis):
    return lax.dynamic_index_in_dim(tensor, index, axis=axis, keepdims=False)


def pack_cols(tensor, parts):
    rows = tensor.shape[0]
    return tensor.reshape(rows, parts, -1).transpose(1, 0, 2).reshape(parts, -1)


def unpack_cols(flat, parts, rows):
    return flat.reshape(parts, rows, -1).transpose(1, 0, 2).reshape(rows, -1)


def rep_gather_kernel(x_ref, o_ref, send_sem, recv_sem):
    me = lax.axis_index("rep")
    rows = x_ref.shape[0]
    other_chip = lax.rem(me + 2, 4)
    other_core = me + 1 - 2 * lax.rem(me, 2)
    o_ref[pl.ds(me * rows, rows), :] = x_ref[...]
    barrier = pltpu.get_barrier_semaphore()
    for peer in (other_chip, other_core):
        pl.semaphore_signal(barrier, inc=1, device_id={"rep": peer}, device_id_type=pl.DeviceIdType.MESH)
    pl.semaphore_wait(barrier, 2)
    cross = pltpu.make_async_remote_copy(
        src_ref=x_ref,
        dst_ref=o_ref.at[pl.ds(me * rows, rows)],
        send_sem=send_sem.at[0],
        recv_sem=recv_sem.at[0],
        device_id={"rep": other_chip},
        device_id_type=pl.DeviceIdType.MESH,
    )
    cross.start()
    own = pltpu.make_async_remote_copy(
        src_ref=x_ref,
        dst_ref=o_ref.at[pl.ds(me * rows, rows)],
        send_sem=send_sem.at[1],
        recv_sem=recv_sem.at[1],
        device_id={"rep": other_core},
        device_id_type=pl.DeviceIdType.MESH,
    )
    own.start()
    cross.wait()
    relay = pltpu.make_async_remote_copy(
        src_ref=o_ref.at[pl.ds(other_chip * rows, rows)],
        dst_ref=o_ref.at[pl.ds(other_chip * rows, rows)],
        send_sem=send_sem.at[2],
        recv_sem=recv_sem.at[2],
        device_id={"rep": other_core},
        device_id_type=pl.DeviceIdType.MESH,
    )
    relay.start()
    own.wait()
    relay.wait()


def gather_rep(tensor, cid=1):
    n = lax.axis_size("rep")
    rows, cols = tensor.shape
    return pl.pallas_call(
        rep_gather_kernel,
        out_shape=jax.ShapeDtypeStruct((n * rows, cols), tensor.dtype),
        in_specs=[pl.BlockSpec(memory_space=pltpu.VMEM)],
        out_specs=pl.BlockSpec(memory_space=pltpu.VMEM),
        scratch_shapes=[pltpu.SemaphoreType.DMA((n - 1,)), pltpu.SemaphoreType.DMA((n - 1,))],
        compiler_params=pltpu.CompilerParams(collective_id=cid, has_side_effects=True),
    )(tensor)


def rep_scatter_kernel(p_ref, o_ref, onchip_buf, cross_buf, partial, send_sem, recv_sem):
    me = lax.axis_index("rep")
    rows = o_ref.shape[0]
    other_chip = lax.rem(me + 2, 4)
    other_core = me + 1 - 2 * lax.rem(me, 2)
    diagonal = lax.rem(other_core + 2, 4)
    barrier = pltpu.get_barrier_semaphore()
    for peer in (other_chip, other_core):
        pl.semaphore_signal(barrier, inc=1, device_id={"rep": peer}, device_id_type=pl.DeviceIdType.MESH)
    pl.semaphore_wait(barrier, 2)
    near = []
    for slot, block in ((0, other_core), (1, diagonal)):
        copy = pltpu.make_async_remote_copy(
            src_ref=p_ref.at[pl.ds(block * rows, rows)],
            dst_ref=onchip_buf.at[slot],
            send_sem=send_sem.at[slot],
            recv_sem=recv_sem.at[slot],
            device_id={"rep": other_core},
            device_id_type=pl.DeviceIdType.MESH,
        )
        copy.start()
        near.append(copy)
    for copy in near:
        copy.wait()
    partial[...] = (p_ref[pl.ds(other_chip * rows, rows), :] + onchip_buf[1]).astype(partial.dtype)
    far = pltpu.make_async_remote_copy(
        src_ref=partial,
        dst_ref=cross_buf,
        send_sem=send_sem.at[2],
        recv_sem=recv_sem.at[2],
        device_id={"rep": other_chip},
        device_id_type=pl.DeviceIdType.MESH,
    )
    far.start()
    far.wait()
    o_ref[...] = p_ref[pl.ds(me * rows, rows), :] + onchip_buf[0] + cross_buf[...].astype(o_ref.dtype)


def scatter_rep(tensor, cid=4):
    n = lax.axis_size("rep")
    rows, cols = tensor.shape[0] // n, tensor.shape[1]
    return pl.pallas_call(
        rep_scatter_kernel,
        out_shape=jax.ShapeDtypeStruct((rows, cols), tensor.dtype),
        in_specs=[pl.BlockSpec(memory_space=pltpu.VMEM)],
        out_specs=pl.BlockSpec(memory_space=pltpu.VMEM),
        scratch_shapes=[
            pltpu.VMEM((2, rows, cols), tensor.dtype),
            pltpu.VMEM((rows, cols), jnp.bfloat16),
            pltpu.VMEM((rows, cols), jnp.bfloat16),
            pltpu.SemaphoreType.DMA((3,)),
            pltpu.SemaphoreType.DMA((3,)),
        ],
        compiler_params=pltpu.CompilerParams(collective_id=cid, has_side_effects=True),
    )(tensor)


def local(inputs, segment_ids, cotangent, w_qkv, w_out, w_up, w_down, biases, norm_gains, up_bias):
    parts = lax.axis_size("shard")
    reps = lax.axis_size("rep")
    r = lax.axis_index("rep")
    head_cols = D // reps
    heads_here = HEADS // reps
    ff_all = w_up.shape[2]
    ff_chunk = ff_all // parts
    ff_piece = ff_chunk // reps
    k_rows = D // parts

    qkv_piece = pick(w_qkv[0].reshape(k_rows, 3, reps, head_cols), r, 2).reshape(k_rows, -1)
    out_piece = w_out[0]
    up_piece = pick(w_up[0].reshape(k_rows, parts, reps, ff_piece), r, 2).reshape(k_rows, -1)
    down_piece = pick(w_down[0].reshape(reps, ff_piece, D), r, 0)
    upb_piece = pick(up_bias[0].reshape(reps, ff_piece), r, 0)
    small = jnp.concatenate(
        [biases[0].T, norm_gains[0].T, upb_piece[:, None]], axis=1
    )
    small = jnp.pad(small, ((0, 0), (0, 128 - small.shape[1])))
    pieces = (qkv_piece, out_piece, up_piece, down_piece, small)
    widths = [piece.shape[1] for piece in pieces]
    offsets = [sum(widths[:i]) for i in range(len(widths) + 1)]
    gathered = lax.all_gather(jnp.concatenate(pieces, axis=1), "shard", axis=0, tiled=True)
    got = [gathered[:, offsets[i] : offsets[i + 1]] for i in range(len(widths))]
    w_qkv_r = got[0]
    w_out_all = got[1]
    w_out_r = lax.dynamic_slice_in_dim(w_out_all, r * head_cols, head_cols, axis=0)
    w_up_r = got[2]
    w_down_r = got[3]
    n_bias = biases.shape[1]
    n_gain = norm_gains.shape[1]
    bias_all = got[4][:, :n_bias].T
    gain_all = got[4][:, n_bias : n_bias + n_gain].T
    up_bias_r = got[4][:, n_bias + n_gain]
    bias_q = lax.dynamic_slice_in_dim(bias_all[0], r * head_cols, head_cols)
    bias_v = lax.dynamic_slice_in_dim(bias_all[1], r * head_cols, head_cols)

    rows_f32 = inputs[0]
    own = rows_f32.shape[0]
    rows_bf = rows_f32.astype(jnp.bfloat16)
    seg_tag = jnp.broadcast_to(segment_ids[0].astype(jnp.bfloat16)[:, None], (own, 128))
    hb_seg = gather_rep(jnp.concatenate([rows_bf, seg_tag], axis=1), cid=0)
    hb_all = hb_seg[:, :D]
    seg_all = hb_seg[:, D]
    qkv_rows = matmul(hb_all, w_qkv_r)
    queries = (qkv_rows[:, :head_cols] + bias_q).astype(jnp.bfloat16).reshape(1, -1, heads_here, HEAD_DIM)
    keys_all = qkv_rows[:, head_cols : 2 * head_cols].astype(jnp.bfloat16).reshape(1, -1, heads_here, HEAD_DIM)
    values_all = (
        (qkv_rows[:, 2 * head_cols :] + bias_v).astype(jnp.bfloat16).reshape(1, -1, heads_here, HEAD_DIM)
    )
    seg_rows = seg_all[None]
    scores, allowed = attention_scores(queries, keys_all, seg_rows, seg_rows)
    expo_all = jnp.where(allowed, jnp.exp(scores), 0.0)
    row_total = jnp.sum(expo_all, axis=-1, keepdims=True)
    log_total = jnp.log(row_total)
    attn_probs = (expo_all / row_total).astype(jnp.bfloat16)
    context = (
        jnp.einsum("shqk,skhe->sqhe", attn_probs, values_all, preferred_element_type=jnp.float32)
        .astype(jnp.bfloat16)
        .reshape(-1, head_cols)
    )
    first_sum = rows_f32 + scatter_rep(matmul(context, w_out_r)) + bias_all[2]
    context_stack = gather_rep(context, cid=2).reshape(reps, -1, head_cols)
    norm_one, rstd_one = normalize(first_sum)
    mid_norm = norm_one * gain_all[0] + bias_all[3]
    mid_b = mid_norm.astype(jnp.bfloat16)
    mid_all = gather_rep(mid_b)
    pre_act = matmul(mid_all, w_up_r) + up_bias_r
    act_f32, gelu_slope = gelu_pair(pre_act)
    act_b = act_f32.astype(jnp.bfloat16)
    second_sum = mid_norm + scatter_rep(matmul(act_b, w_down_r)) + bias_all[4]
    norm_two, rstd_two = normalize(second_sum)
    layer_out = norm_two * gain_all[1] + bias_all[5]

    grad_rows = cotangent[0]
    d_gain_two = jnp.sum(grad_rows * norm_two, axis=0)
    d_bias_two = jnp.sum(grad_rows, axis=0)
    d_second = norm_back(grad_rows, norm_two, rstd_two, gain_all[1])
    d_bdown = jnp.sum(d_second, axis=0)
    d_second_all = gather_rep(d_second.astype(jnp.bfloat16))
    d_wdown = matmul_lt(act_b, d_second_all)
    d_pre = matmul_rt(d_second_all, w_down_r) * gelu_slope
    d_bup = jnp.sum(d_pre, axis=0)
    d_pre_b = d_pre.astype(jnp.bfloat16)
    d_wup = matmul_lt(mid_all, d_pre_b)
    ffn_pack = jnp.concatenate(
        [d_wup.astype(jnp.bfloat16).reshape(parts, -1), d_wdown.astype(jnp.bfloat16).reshape(parts, -1)],
        axis=1,
    ).reshape(parts, 8, -1)
    ffn_recv = lax.all_to_all(ffn_pack, "shard", 0, 0, tiled=True)
    ffn_share = jnp.sum(ffn_recv.astype(jnp.float32), axis=0).astype(jnp.bfloat16)
    d_mid = d_second + scatter_rep(matmul_rt(d_pre_b, w_up_r))
    d_gain_one = jnp.sum(d_mid * norm_one, axis=0)
    d_bias_one = jnp.sum(d_mid, axis=0)
    d_first = norm_back(d_mid, norm_one, rstd_one, gain_all[0])
    d_bout = jnp.sum(d_first, axis=0)
    d_first_all = gather_rep(d_first.astype(jnp.bfloat16))
    d_first_cols = lax.dynamic_slice_in_dim(d_first_all, r * head_cols, head_cols, axis=1)
    d_wout_cols = jnp.einsum(
        "utc,tk->uck", context_stack, d_first_cols, preferred_element_type=jnp.float32
    ).reshape(D, head_cols)
    d_context = (
        matmul_rt(d_first_all, w_out_r).astype(jnp.bfloat16).reshape(1, -1, heads_here, HEAD_DIM)
    )
    probs_again = jnp.where(allowed, jnp.exp(scores - log_total), 0.0)
    d_probs = jnp.einsum(
        "sqhe,skhe->shqk", d_context, values_all, preferred_element_type=jnp.float32
    )
    d_scores = (
        probs_again
        * (d_probs - jnp.sum(probs_again * d_probs, axis=-1, keepdims=True))
        * (1.0 / math.sqrt(HEAD_DIM))
    ).astype(jnp.bfloat16)
    d_queries = jnp.einsum(
        "shqk,skhe->sqhe", d_scores, keys_all, preferred_element_type=jnp.float32
    ).reshape(-1, head_cols)
    d_keys = jnp.einsum(
        "shqk,sqhe->skhe", d_scores, queries, preferred_element_type=jnp.float32
    ).reshape(-1, head_cols)
    d_values = jnp.einsum(
        "shqk,sqhe->skhe",
        probs_again.astype(jnp.bfloat16),
        d_context,
        preferred_element_type=jnp.float32,
    ).reshape(-1, head_cols)
    d_qkv = jnp.concatenate([d_queries, d_keys, d_values], axis=-1).astype(jnp.bfloat16)
    d_wqkv = matmul_lt(hb_all, d_qkv)
    input_grad = d_first + scatter_rep(matmul_rt(d_qkv, w_qkv_r))

    zeros_cols = jnp.zeros((D,), jnp.float32)
    d_bq = lax.dynamic_update_slice_in_dim(zeros_cols, jnp.sum(d_queries, axis=0), r * head_cols, 0)
    d_bv = lax.dynamic_update_slice_in_dim(zeros_cols, jnp.sum(d_values, axis=0), r * head_cols, 0)
    d_biases = jnp.stack([d_bq, d_bv, d_bout, d_bias_one, d_bdown, d_bias_two])
    d_gains = jnp.stack([d_gain_one, d_gain_two])
    d_bup_all = lax.dynamic_update_slice_in_dim(
        jnp.zeros((parts, reps, ff_piece), jnp.float32), d_bup.reshape(parts, 1, ff_piece), r, 1
    )
    grad_parts = (
        d_wqkv.astype(jnp.bfloat16).reshape(parts, -1),
        d_wout_cols.astype(jnp.bfloat16).reshape(parts, -1),
        d_bup_all.astype(jnp.bfloat16).reshape(parts, -1),
        pack_cols(d_biases.astype(jnp.bfloat16), parts),
        pack_cols(d_gains.astype(jnp.bfloat16), parts),
    )
    g_sizes = [piece.shape[1] for piece in grad_parts]
    grad_pack = jnp.concatenate(grad_parts, axis=1)
    width = grad_pack.shape[1]
    padded = -(-width // 1024) * 1024
    grad_pack = jnp.pad(grad_pack, ((0, 0), (0, padded - width))).reshape(parts, 8, -1)
    received = lax.all_to_all(grad_pack, "shard", 0, 0, tiled=True)
    shares = jnp.sum(received.astype(jnp.float32), axis=0).astype(jnp.bfloat16)
    all_shares = jnp.concatenate([shares.reshape(-1), ffn_share.reshape(-1)])
    joined = lax.all_gather(all_shares, "rep", axis=0, tiled=False).astype(jnp.float32)
    g_sizes = g_sizes + [padded - width, ffn_share.size // 2, ffn_share.size // 2]
    names = ["qkv", "out", "bup", "bias", "gain", "pad", "up", "down"]
    g_offsets = [sum(g_sizes[:i]) for i in range(len(g_sizes) + 1)]
    got = {names[i]: joined[:, g_offsets[i] : g_offsets[i + 1]] for i in range(len(g_sizes))}
    grad_w_qkv = got["qkv"].reshape(reps, k_rows, 3, head_cols).transpose(1, 2, 0, 3).reshape(k_rows, -1)
    grad_w_out = got["out"].reshape(reps, k_rows, head_cols).transpose(1, 0, 2).reshape(k_rows, D)
    grad_w_up = got["up"].reshape(reps, k_rows, parts, ff_piece).transpose(1, 2, 0, 3).reshape(k_rows, -1)
    grad_w_down = got["down"].reshape(reps * ff_piece, D)
    grad_up_bias = jnp.sum(got["bup"], axis=0)
    grad_biases = jnp.sum(got["bias"], axis=0).reshape(biases.shape[1], -1)
    grad_gains = jnp.sum(got["gain"], axis=0).reshape(norm_gains.shape[1], -1)
    return (
        layer_out[None],
        input_grad[None],
        grad_w_qkv[None],
        grad_w_out[None],
        grad_w_up[None],
        grad_w_down[None],
        grad_biases[None],
        grad_gains[None],
        grad_up_bias[None],
    )


def solution(mesh):
    in_specs = (
        P("shard", "rep", None),
        P("shard", "rep"),
        P("shard", "rep", None),
        P(None, "shard", None),
        P(None, "shard", None),
        P(None, "shard", None),
        P(None, "shard", None),
        P(None, None, "shard"),
        P(None, None, "shard"),
        P(None, "shard"),
    )
    out_specs = (
        P("shard", "rep", None),
        P("shard", "rep", None),
        P(None, "shard", None),
        P(None, "shard", None),
        P(None, "shard", None),
        P(None, "shard", None),
        P(None, None, "shard"),
        P(None, None, "shard"),
        P(None, "shard"),
    )
    return jax.shard_map(local, mesh=mesh, in_specs=in_specs, out_specs=out_specs, check_vma=False)
```

```python
import math

import jax
import jax.numpy as jnp
from jax import lax
from jax.experimental import pallas as pl
from jax.experimental.pallas import tpu as pltpu
from jax.sharding import PartitionSpec as P

D = 1024
HEADS = 16
HEAD_DIM = 64
LAYERS = 1


epsilon = 1e-06


def normalize(residual):
    center = residual - jnp.mean(residual, axis=-1, keepdims=True)
    rstd_val = lax.rsqrt(jnp.mean(center * center, axis=-1, keepdims=True) + epsilon)
    return (center * rstd_val, rstd_val)


def norm_back(grad_out, x_hat, rstd_val, gain_row):
    d_hat = grad_out * gain_row
    return rstd_val * (
        d_hat
        - jnp.mean(d_hat, axis=-1, keepdims=True)
        - x_hat * jnp.mean(d_hat * x_hat, axis=-1, keepdims=True)
    )


def gelu_pair(pre_act):
    normal_cdf = 0.5 * (1.0 + lax.erf(pre_act * (1.0 / math.sqrt(2.0))))
    density = jnp.exp(-0.5 * pre_act * pre_act) * (1.0 / math.sqrt(2.0 * math.pi))
    return (pre_act * normal_cdf, normal_cdf + pre_act * density)


def matmul(first_op, second_op):
    return jnp.dot(first_op, second_op, preferred_element_type=jnp.float32)


def matmul_lt(first_op, second_op):
    return lax.dot_general(
        first_op, second_op, (((0,), (0,)), ((), ())), preferred_element_type=jnp.float32
    )


def matmul_rt(first_op, second_op):
    return lax.dot_general(
        first_op, second_op, (((1,), (1,)), ((), ())), preferred_element_type=jnp.float32
    )


def attention_scores(queries, keys_all, seg_rows, seg_cols):
    scores = jnp.einsum(
        "sqhe,skhe->shqk", queries, keys_all, preferred_element_type=jnp.float32
    ) * (1.0 / math.sqrt(HEAD_DIM))
    allowed = seg_rows[:, None, :, None] == seg_cols[:, None, None, :]
    return (scores, allowed)


def pick(tensor, index, axis):
    return lax.dynamic_index_in_dim(tensor, index, axis=axis, keepdims=False)


def pack_cols(tensor, parts):
    rows = tensor.shape[0]
    return tensor.reshape(rows, parts, -1).transpose(1, 0, 2).reshape(parts, -1)


def unpack_cols(flat, parts, rows):
    return flat.reshape(parts, rows, -1).transpose(1, 0, 2).reshape(rows, -1)


def rep_gather_kernel(x_ref, o_ref, send_sem, recv_sem):
    me = lax.axis_index("rep")
    rows = x_ref.shape[0]
    half = rows // 2
    other_chip = lax.rem(me + 2, 4)
    other_core = me + 1 - 2 * lax.rem(me, 2)
    o_ref[pl.ds(me * rows, rows), :] = x_ref[...]
    barrier = pltpu.get_barrier_semaphore()
    for peer in (other_chip, other_core):
        pl.semaphore_signal(barrier, inc=1, device_id={"rep": peer}, device_id_type=pl.DeviceIdType.MESH)
    pl.semaphore_wait(barrier, 2)
    cross = []
    for part in range(2):
        copy = pltpu.make_async_remote_copy(
            src_ref=x_ref.at[pl.ds(part * half, half)],
            dst_ref=o_ref.at[pl.ds(me * rows + part * half, half)],
            send_sem=send_sem.at[part],
            recv_sem=recv_sem.at[part],
            device_id={"rep": other_chip},
            device_id_type=pl.DeviceIdType.MESH,
        )
        copy.start()
        cross.append(copy)
    own = pltpu.make_async_remote_copy(
        src_ref=x_ref,
        dst_ref=o_ref.at[pl.ds(me * rows, rows)],
        send_sem=send_sem.at[2],
        recv_sem=recv_sem.at[2],
        device_id={"rep": other_core},
        device_id_type=pl.DeviceIdType.MESH,
    )
    own.start()
    relays = []
    for part in range(2):
        cross[part].wait()
        block = o_ref.at[pl.ds(other_chip * rows + part * half, half)]
        relay = pltpu.make_async_remote_copy(
            src_ref=block,
            dst_ref=block,
            send_sem=send_sem.at[3 + part],
            recv_sem=recv_sem.at[3 + part],
            device_id={"rep": other_core},
            device_id_type=pl.DeviceIdType.MESH,
        )
        relay.start()
        relays.append(relay)
    own.wait()
    for relay in relays:
        relay.wait()


def gather_rep(tensor, cid=1):
    n = lax.axis_size("rep")
    rows, cols = tensor.shape
    return pl.pallas_call(
        rep_gather_kernel,
        out_shape=jax.ShapeDtypeStruct((n * rows, cols), tensor.dtype),
        in_specs=[pl.BlockSpec(memory_space=pltpu.VMEM)],
        out_specs=pl.BlockSpec(memory_space=pltpu.VMEM),
        scratch_shapes=[pltpu.SemaphoreType.DMA((5,)), pltpu.SemaphoreType.DMA((5,))],
        compiler_params=pltpu.CompilerParams(collective_id=cid, has_side_effects=True),
    )(tensor)


def rep_scatter_kernel(p_ref, o_ref, onchip_buf, cross_buf, partial, send_sem, recv_sem):
    me = lax.axis_index("rep")
    rows = o_ref.shape[0]
    other_chip = lax.rem(me + 2, 4)
    other_core = me + 1 - 2 * lax.rem(me, 2)
    diagonal = lax.rem(other_core + 2, 4)
    barrier = pltpu.get_barrier_semaphore()
    for peer in (other_chip, other_core):
        pl.semaphore_signal(barrier, inc=1, device_id={"rep": peer}, device_id_type=pl.DeviceIdType.MESH)
    pl.semaphore_wait(barrier, 2)
    near = []
    for slot, block in ((0, other_core), (1, diagonal)):
        copy = pltpu.make_async_remote_copy(
            src_ref=p_ref.at[pl.ds(block * rows, rows)],
            dst_ref=onchip_buf.at[slot],
            send_sem=send_sem.at[slot],
            recv_sem=recv_sem.at[slot],
            device_id={"rep": other_core},
            device_id_type=pl.DeviceIdType.MESH,
        )
        copy.start()
        near.append(copy)
    for copy in near:
        copy.wait()
    partial[...] = (p_ref[pl.ds(other_chip * rows, rows), :] + onchip_buf[1]).astype(partial.dtype)
    far = pltpu.make_async_remote_copy(
        src_ref=partial,
        dst_ref=cross_buf,
        send_sem=send_sem.at[2],
        recv_sem=recv_sem.at[2],
        device_id={"rep": other_chip},
        device_id_type=pl.DeviceIdType.MESH,
    )
    far.start()
    far.wait()
    o_ref[...] = p_ref[pl.ds(me * rows, rows), :] + onchip_buf[0] + cross_buf[...].astype(o_ref.dtype)


def scatter_rep(tensor, cid=4):
    n = lax.axis_size("rep")
    rows, cols = tensor.shape[0] // n, tensor.shape[1]
    return pl.pallas_call(
        rep_scatter_kernel,
        out_shape=jax.ShapeDtypeStruct((rows, cols), tensor.dtype),
        in_specs=[pl.BlockSpec(memory_space=pltpu.VMEM)],
        out_specs=pl.BlockSpec(memory_space=pltpu.VMEM),
        scratch_shapes=[
            pltpu.VMEM((2, rows, cols), tensor.dtype),
            pltpu.VMEM((rows, cols), jnp.bfloat16),
            pltpu.VMEM((rows, cols), jnp.bfloat16),
            pltpu.SemaphoreType.DMA((3,)),
            pltpu.SemaphoreType.DMA((3,)),
        ],
        compiler_params=pltpu.CompilerParams(collective_id=cid, has_side_effects=True),
    )(tensor)


def local(inputs, segment_ids, cotangent, w_qkv, w_out, w_up, w_down, biases, norm_gains, up_bias):
    parts = lax.axis_size("shard")
    reps = lax.axis_size("rep")
    r = lax.axis_index("rep")
    head_cols = D // reps
    heads_here = HEADS // reps
    ff_all = w_up.shape[2]
    ff_chunk = ff_all // parts
    ff_piece = ff_chunk // reps
    k_rows = D // parts

    qkv_piece = pick(w_qkv[0].reshape(k_rows, 3, reps, head_cols), r, 2).reshape(k_rows, -1)
    out_piece = w_out[0]
    up_piece = pick(w_up[0].reshape(k_rows, parts, reps, ff_piece), r, 2).reshape(k_rows, -1)
    down_piece = pick(w_down[0].reshape(reps, ff_piece, D), r, 0)
    upb_piece = pick(up_bias[0].reshape(reps, ff_piece), r, 0)
    small = jnp.concatenate(
        [biases[0].T, norm_gains[0].T, upb_piece[:, None]], axis=1
    )
    small = jnp.pad(small, ((0, 0), (0, 128 - small.shape[1])))
    pieces = (qkv_piece, out_piece, up_piece, down_piece, small)
    widths = [piece.shape[1] for piece in pieces]
    offsets = [sum(widths[:i]) for i in range(len(widths) + 1)]
    gathered = lax.all_gather(jnp.concatenate(pieces, axis=1), "shard", axis=0, tiled=True)
    got = [gathered[:, offsets[i] : offsets[i + 1]] for i in range(len(widths))]
    w_qkv_r = got[0]
    w_out_all = got[1]
    w_out_r = lax.dynamic_slice_in_dim(w_out_all, r * head_cols, head_cols, axis=0)
    w_up_r = got[2]
    w_down_r = got[3]
    n_bias = biases.shape[1]
    n_gain = norm_gains.shape[1]
    bias_all = got[4][:, :n_bias].T
    gain_all = got[4][:, n_bias : n_bias + n_gain].T
    up_bias_r = got[4][:, n_bias + n_gain]
    bias_q = lax.dynamic_slice_in_dim(bias_all[0], r * head_cols, head_cols)
    bias_v = lax.dynamic_slice_in_dim(bias_all[1], r * head_cols, head_cols)

    rows_f32 = inputs[0]
    own = rows_f32.shape[0]
    rows_bf = rows_f32.astype(jnp.bfloat16)
    seg_tag = jnp.broadcast_to(segment_ids[0].astype(jnp.bfloat16)[:, None], (own, 128))
    hb_seg = gather_rep(jnp.concatenate([rows_bf, seg_tag], axis=1), cid=0)
    hb_all = hb_seg[:, :D]
    seg_all = hb_seg[:, D]
    qkv_rows = matmul(hb_all, w_qkv_r)
    queries = (qkv_rows[:, :head_cols] + bias_q).astype(jnp.bfloat16).reshape(1, -1, heads_here, HEAD_DIM)
    keys_all = qkv_rows[:, head_cols : 2 * head_cols].astype(jnp.bfloat16).reshape(1, -1, heads_here, HEAD_DIM)
    values_all = (
        (qkv_rows[:, 2 * head_cols :] + bias_v).astype(jnp.bfloat16).reshape(1, -1, heads_here, HEAD_DIM)
    )
    seg_rows = seg_all[None]
    scores, allowed = attention_scores(queries, keys_all, seg_rows, seg_rows)
    expo_all = jnp.where(allowed, jnp.exp(scores), 0.0)
    row_total = jnp.sum(expo_all, axis=-1, keepdims=True)
    log_total = jnp.log(row_total)
    attn_probs = (expo_all / row_total).astype(jnp.bfloat16)
    context = (
        jnp.einsum("shqk,skhe->sqhe", attn_probs, values_all, preferred_element_type=jnp.float32)
        .astype(jnp.bfloat16)
        .reshape(-1, head_cols)
    )
    first_sum = rows_f32 + scatter_rep(matmul(context, w_out_r)) + bias_all[2]
    context_stack = gather_rep(context, cid=2).reshape(reps, -1, head_cols)
    norm_one, rstd_one = normalize(first_sum)
    mid_norm = norm_one * gain_all[0] + bias_all[3]
    mid_b = mid_norm.astype(jnp.bfloat16)
    mid_all = gather_rep(mid_b)
    pre_act = matmul(mid_all, w_up_r) + up_bias_r
    act_f32, gelu_slope = gelu_pair(pre_act)
    act_b = act_f32.astype(jnp.bfloat16)
    second_sum = mid_norm + scatter_rep(matmul(act_b, w_down_r)) + bias_all[4]
    norm_two, rstd_two = normalize(second_sum)
    layer_out = norm_two * gain_all[1] + bias_all[5]

    grad_rows = cotangent[0]
    d_gain_two = jnp.sum(grad_rows * norm_two, axis=0)
    d_bias_two = jnp.sum(grad_rows, axis=0)
    d_second = norm_back(grad_rows, norm_two, rstd_two, gain_all[1])
    d_bdown = jnp.sum(d_second, axis=0)
    d_second_all = gather_rep(d_second.astype(jnp.bfloat16))
    d_wdown = matmul_lt(act_b, d_second_all)
    d_pre = matmul_rt(d_second_all, w_down_r) * gelu_slope
    d_bup = jnp.sum(d_pre, axis=0)
    d_pre_b = d_pre.astype(jnp.bfloat16)
    d_wup = matmul_lt(mid_all, d_pre_b)
    ffn_pack = jnp.concatenate(
        [d_wup.astype(jnp.bfloat16).reshape(parts, -1), d_wdown.astype(jnp.bfloat16).reshape(parts, -1)],
        axis=1,
    ).reshape(parts, 8, -1)
    ffn_recv = lax.all_to_all(ffn_pack, "shard", 0, 0, tiled=True)
    ffn_share = jnp.sum(ffn_recv.astype(jnp.float32), axis=0).astype(jnp.bfloat16)
    d_mid = d_second + scatter_rep(matmul_rt(d_pre_b, w_up_r))
    d_gain_one = jnp.sum(d_mid * norm_one, axis=0)
    d_bias_one = jnp.sum(d_mid, axis=0)
    d_first = norm_back(d_mid, norm_one, rstd_one, gain_all[0])
    d_bout = jnp.sum(d_first, axis=0)
    d_first_all = gather_rep(d_first.astype(jnp.bfloat16))
    d_first_cols = lax.dynamic_slice_in_dim(d_first_all, r * head_cols, head_cols, axis=1)
    d_wout_cols = jnp.einsum(
        "utc,tk->uck", context_stack, d_first_cols, preferred_element_type=jnp.float32
    ).reshape(D, head_cols)
    d_context = (
        matmul_rt(d_first_all, w_out_r).astype(jnp.bfloat16).reshape(1, -1, heads_here, HEAD_DIM)
    )
    probs_again = jnp.where(allowed, jnp.exp(scores - log_total), 0.0)
    d_probs = jnp.einsum(
        "sqhe,skhe->shqk", d_context, values_all, preferred_element_type=jnp.float32
    )
    d_scores = (
        probs_again
        * (d_probs - jnp.sum(probs_again * d_probs, axis=-1, keepdims=True))
        * (1.0 / math.sqrt(HEAD_DIM))
    ).astype(jnp.bfloat16)
    d_queries = jnp.einsum(
        "shqk,skhe->sqhe", d_scores, keys_all, preferred_element_type=jnp.float32
    ).reshape(-1, head_cols)
    d_keys = jnp.einsum(
        "shqk,sqhe->skhe", d_scores, queries, preferred_element_type=jnp.float32
    ).reshape(-1, head_cols)
    d_values = jnp.einsum(
        "shqk,sqhe->skhe",
        probs_again.astype(jnp.bfloat16),
        d_context,
        preferred_element_type=jnp.float32,
    ).reshape(-1, head_cols)
    d_qkv = jnp.concatenate([d_queries, d_keys, d_values], axis=-1).astype(jnp.bfloat16)
    d_wqkv = matmul_lt(hb_all, d_qkv)
    input_grad = d_first + scatter_rep(matmul_rt(d_qkv, w_qkv_r))

    zeros_cols = jnp.zeros((D,), jnp.float32)
    d_bq = lax.dynamic_update_slice_in_dim(zeros_cols, jnp.sum(d_queries, axis=0), r * head_cols, 0)
    d_bv = lax.dynamic_update_slice_in_dim(zeros_cols, jnp.sum(d_values, axis=0), r * head_cols, 0)
    d_biases = jnp.stack([d_bq, d_bv, d_bout, d_bias_one, d_bdown, d_bias_two])
    d_gains = jnp.stack([d_gain_one, d_gain_two])
    d_bup_all = lax.dynamic_update_slice_in_dim(
        jnp.zeros((parts, reps, ff_piece), jnp.float32), d_bup.reshape(parts, 1, ff_piece), r, 1
    )
    grad_parts = (
        d_wqkv.astype(jnp.bfloat16).reshape(parts, -1),
        d_wout_cols.astype(jnp.bfloat16).reshape(parts, -1),
        d_bup_all.astype(jnp.bfloat16).reshape(parts, -1),
        pack_cols(d_biases.astype(jnp.bfloat16), parts),
        pack_cols(d_gains.astype(jnp.bfloat16), parts),
    )
    g_sizes = [piece.shape[1] for piece in grad_parts]
    grad_pack = jnp.concatenate(grad_parts, axis=1)
    width = grad_pack.shape[1]
    padded = -(-width // 1024) * 1024
    grad_pack = jnp.pad(grad_pack, ((0, 0), (0, padded - width))).reshape(parts, 8, -1)
    received = lax.all_to_all(grad_pack, "shard", 0, 0, tiled=True)
    shares = jnp.sum(received.astype(jnp.float32), axis=0).astype(jnp.bfloat16)
    all_shares = jnp.concatenate([shares.reshape(-1), ffn_share.reshape(-1)])
    joined = lax.all_gather(all_shares, "rep", axis=0, tiled=False).astype(jnp.float32)
    g_sizes = g_sizes + [padded - width, ffn_share.size // 2, ffn_share.size // 2]
    names = ["qkv", "out", "bup", "bias", "gain", "pad", "up", "down"]
    g_offsets = [sum(g_sizes[:i]) for i in range(len(g_sizes) + 1)]
    got = {names[i]: joined[:, g_offsets[i] : g_offsets[i + 1]] for i in range(len(g_sizes))}
    grad_w_qkv = got["qkv"].reshape(reps, k_rows, 3, head_cols).transpose(1, 2, 0, 3).reshape(k_rows, -1)
    grad_w_out = got["out"].reshape(reps, k_rows, head_cols).transpose(1, 0, 2).reshape(k_rows, D)
    grad_w_up = got["up"].reshape(reps, k_rows, parts, ff_piece).transpose(1, 2, 0, 3).reshape(k_rows, -1)
    grad_w_down = got["down"].reshape(reps * ff_piece, D)
    grad_up_bias = jnp.sum(got["bup"], axis=0)
    grad_biases = jnp.sum(got["bias"], axis=0).reshape(biases.shape[1], -1)
    grad_gains = jnp.sum(got["gain"], axis=0).reshape(norm_gains.shape[1], -1)
    return (
        layer_out[None],
        input_grad[None],
        grad_w_qkv[None],
        grad_w_out[None],
        grad_w_up[None],
        grad_w_down[None],
        grad_biases[None],
        grad_gains[None],
        grad_up_bias[None],
    )


def solution(mesh):
    in_specs = (
        P("shard", "rep", None),
        P("shard", "rep"),
        P("shard", "rep", None),
        P(None, "shard", None),
        P(None, "shard", None),
        P(None, "shard", None),
        P(None, "shard", None),
        P(None, None, "shard"),
        P(None, None, "shard"),
        P(None, "shard"),
    )
    out_specs = (
        P("shard", "rep", None),
        P("shard", "rep", None),
        P(None, "shard", None),
        P(None, "shard", None),
        P(None, "shard", None),
        P(None, "shard", None),
        P(None, None, "shard"),
        P(None, None, "shard"),
        P(None, "shard"),
    )
    return jax.shard_map(local, mesh=mesh, in_specs=in_specs, out_specs=out_specs, check_vma=False)
```
